128 devices in a mesh: row: 16 (over x, y), col: 4 (over z), layer: 2 (over core).
Axes of the slice: x: 4, y: 4, z: 4, core: 2. Of those that a mesh axis runs over, the one named last changes fastest.
Arguments:
- density: float32 [4096, 4096], P('row', ('col', 'layer')), may hold values from -2 to 2
- masks: int32 [6, 64, 64], replicated, may hold values from 0 to 1, as said below
- branch: int32 [5], replicated, may hold values from 0 to 1, as said below
- perm: int32 [64], replicated, may hold values from 0 to 63, each once
Outputs:
- purified: float32 [4096, 4096], P('row', ('col', 'layer'))
The draws below stay inside these ranges and needn't reach their ends.
Inputs may be any that keep to these rules, and one draw needn't show every extreme that they name: masks are symmetric in their last two dimensions, every diagonal block is occupied, and block (i, j) of masks[s] is occupied only where the cyclic distance between i and j is at most 6 + s. `branch`: both values occur among the steps. `perm`: a permutation of 0..63.
All inputs are finite; a program needn't handle non-finite values.
Results may differ from the reference program's by a relative error of at most 0.0003.
Values sent between devices are 32-bit elements; how exact they have to be, the bound alone decides.
No kernel may reach another device: no remote copies, remote signals or barrier semaphores. Data moves between devices by JAX's collectives and lax.ppermute only.
A program may use at most 64 MiB of HBM per device.

```python
import jax
import jax.numpy as jnp
from jax import lax

BS = 64
BAND = 6
STEPS = 5
NB = 64
NORD = 4096


def draw_density(key, part):
    key_one, key_two = jax.random.split(key, 2)
    sigma = 1.0 / jnp.sqrt(jnp.float32(BS * (2 * BAND + 1)))
    base = jnp.clip(jax.random.normal(key_one, (NORD, NORD), jnp.float32), -6.0, 6.0)
    symmetric = (base + base.T) * 0.7071
    diag_vals = jax.random.uniform(key_two, (NORD,), jnp.float32, 0.3, 0.7)
    eye = (jnp.arange(NORD)[:, None] == jnp.arange(NORD)[None, :]).astype(jnp.float32)
    result = symmetric * sigma + eye * diag_vals[None, :]
    return jnp.clip(result, -2.0, 2.0)


def draw_masks(key, part):
    index = jnp.arange(NB)
    gap = jnp.abs(index[:, None] - index[None, :])
    cyclic = jnp.minimum(gap, NB - gap)
    layers = []
    for step in range(STEPS + 1):
        bits = jax.random.randint(jax.random.fold_in(key, 7 + step), (NB, NB), 0, 4)
        paired = (bits + bits.T) % 4
        keep = jnp.logical_or(paired != 0, cyclic == 0)
        inside = cyclic <= BAND + step
        layers.append(jnp.logical_and(keep, inside).astype(jnp.int32))
    return jnp.stack(layers, axis=0)


def draw_branch(key, part):
    bits = jax.random.randint(jax.random.fold_in(key, 31), (STEPS,), 0, 2).astype(jnp.int32)
    all_equal = jnp.all(bits == bits[0])
    flipped = jnp.where(all_equal, 1 - bits[1], bits[1]).astype(jnp.int32)
    return bits.at[1].set(flipped)


def setup_inputs(seed: int = 0) -> dict:
    key_list = jax.random.split(jax.random.key(seed), 5)
    return {
        "density": draw_density(jax.random.fold_in(key_list[4], 71), 0),
        "masks": draw_masks(jax.random.fold_in(key_list[4], 71), 0),
        "branch": draw_branch(jax.random.fold_in(key_list[4], 71), 0),
        "perm": jax.random.permutation(key_list[3], NB).astype(jnp.int32),
    }


def expand(block_mask):
    grown = jnp.repeat(block_mask, BS, axis=0)
    return jnp.repeat(grown, BS, axis=1).astype(jnp.float32)


def reference(density, masks, branch, perm):
    ordered = jnp.take(jnp.take(masks, perm, axis=1), perm, axis=2)
    current = density * expand(ordered[0])
    for step in range(STEPS):
        square = jnp.dot(current, current, preferred_element_type=jnp.float32, precision=lax.Precision.HIGHEST)
        picked = jnp.where(branch[step] == 1, 2.0 * current - square, square)
        current = picked * expand(ordered[step + 1])
    return current
```

```python
import jax
import jax.numpy as jnp
from jax import lax
from jax.experimental import pallas as pl
from jax.experimental.pallas import tpu as pltpu
from jax.sharding import PartitionSpec as P

STEPS = 5
BAND = 6
NB = 64
GROUP = ("col", "layer")
PERM, INV, BRANCH, BITS, PLACE = 0, 64, 128, 136, 136 + 6 * 128
F32, BF16 = jnp.float32, jnp.bfloat16


def ring_xy(pos):
    a, b = pos // 2, pos % 2
    return (a, b) if a < 4 else (7 - a, 3 - b)


RING = [ring_xy(p)[0] * 4 + ring_xy(p)[1] for p in range(16)]


def ring_shift(value, k):
    return lax.ppermute(value, "row", [(RING[p], RING[(p + k) % 16]) for p in range(16)])


def xy_shift(value, dx, dy):
    return lax.ppermute(
        value, "row", [(i, ((i // 4 + dx) % 4) * 4 + (i % 4 + dy) % 4) for i in range(16)]
    )


def z_swap(value, k):
    return lax.ppermute(value, "col", [(i, i ^ k) for i in range(4)])


def core_swap(value):
    return lax.ppermute(value, "layer", [(0, 1), (1, 0)])


def low_half():
    return lax.broadcasted_iota(jnp.int32, (8, 128), 1) < 64


def swap_halves(tile):
    return pltpu.roll(tile, 64, 1)


def bit(tab, s, i, j):
    word = tab[BITS + s * 128 + i * 2 + lax.shift_right_logical(j, 5)]
    return lax.shift_right_logical(word, j & 31) & 1


def shifted(tiles, d, count):
    n = len(tiles)
    get = lambda seq, t: seq[t] if 0 <= t < n else None
    if d % 2 == 0:
        return [get(tiles, m - d // 2) for m in range(count)]
    q = (d - 1) // 2
    low = low_half()
    turned = [swap_halves(t) for t in tiles]
    out = []
    for m in range(count):
        a, b = get(turned, m - q - 1), get(turned, m - q)
        if a is None and b is None:
            out.append(None)
        else:
            zero = jnp.zeros((8, 128), F32)
            out.append(jnp.where(low, zero if a is None else a, zero if b is None else b))
    return out


def store_split(hi_ref, lo_ref, row, first, second):
    zero = jnp.zeros((8, 128), F32)
    for m, (a, b) in enumerate(zip(first, second)):
        both = jnp.concatenate([zero if a is None else a, zero if b is None else b], axis=0)
        hi = both.astype(BF16)
        hi_ref[row : row + 16, m * 128 : (m + 1) * 128] = hi
        lo_ref[row : row + 16, m * 128 : (m + 1) * 128] = (both - hi.astype(F32)).astype(BF16)


def tdot(a, b):
    return lax.dot_general(a, b, (((0,), (0,)), ((), ())), preferred_element_type=F32)


def product(hi_ref, lo_ref, start, width):
    xh = hi_ref[:, start : start + width]
    xl = lo_ref[:, start : start + width]
    zh = hi_ref[...]
    return tdot(xh, zh) + tdot(xh, lo_ref[...]) + tdot(xl, zh)


def call(kernel, outs, tab, args, scratch=(), anyspace=False):
    space = pl.ANY if anyspace else pltpu.VMEM
    return pl.pallas_call(
        kernel,
        out_shape=[jax.ShapeDtypeStruct(o, F32) for o in outs],
        in_specs=[pl.BlockSpec(memory_space=pltpu.SMEM)]
        + [pl.BlockSpec(memory_space=space)] * len(args),
        out_specs=[pl.BlockSpec(memory_space=pltpu.VMEM)] * len(outs),
        scratch_shapes=list(scratch),
        compiler_params=pltpu.CompilerParams(vmem_limit_bytes=48 * 1024 * 1024),
    )(tab, *args)


def split_kernel(tab, d_ref, out_ref):
    for c in range(8):
        for e in range(4):
            rows = d_ref[e * 64 + c * 8 : e * 64 + c * 8 + 8, :]
            for t in range(4):
                out_ref[c, e, t] = rows[:, t * 128 : (t + 1) * 128]


def compact_kernel(tab, x_ref, a_ref, b_ref):
    low = low_half()
    row0 = tab[PLACE] * 4
    for e in range(4):
        i = tab[PERM + row0 + e]
        out_ref = a_ref if e < 2 else b_ref
        halves = []
        for t in range(2 * BAND + 2):
            if t > 2 * BAND:
                halves.append(jnp.zeros((8, 128), F32))
                continue
            j = (i + t - BAND) & 63
            sj = tab[INV + j]
            tile = x_ref[sj >> 3, e, (sj & 7) >> 1]
            tile = jnp.where((sj & 1) == (t & 1), tile, swap_halves(tile))
            halves.append(jnp.where(bit(tab, 0, i, j) == 1, tile, 0.0))
        for t in range(BAND + 1):
            out_ref[e % 2, t] = jnp.where(low, halves[2 * t], halves[2 * t + 1])


def gather_rows(half_a, half_b):
    stack_a = jnp.stack([half_a] + [xy_shift(half_a, k, 0) for k in (1, 2, 3)])
    stack_b = jnp.stack([half_b] + [xy_shift(half_b, 0, k) for k in (1, 2, 3)])
    all_a = [stack_a] + [xy_shift(stack_a, 0, k) for k in (1, 2, 3)]
    all_b = [stack_b] + [xy_shift(stack_b, k, 0) for k in (1, 2, 3)]
    return all_a + all_b


def fetch(refs, g_ref, sem):
    copies = [pltpu.make_async_copy(refs[n], g_ref.at[n], sem.at[n]) for n in range(8)]
    for copy in copies:
        copy.start()
    for copy in copies:
        copy.wait()


def seat(tab, r, e):
    dx = (tab[PLACE + 2] - (r >> 2)) & 3
    dy = (tab[PLACE + 3] - (r & 3)) & 3
    first = e < 2
    return jnp.where(first, dy, 4 + dx), jnp.where(first, dx, dy), e & 1


def write_slabs(tab, p_ref, own_ref, oth_ref, e, base, d, tiles):
    h = tab[PLACE + 4]
    low = low_half()
    for zz in range(4):
        for ref, core in ((own_ref, h), (oth_ref, 1 - h)):
            rows = p_ref[base + 2 * zz + core]
            if d % 2 == 0:
                for m in range(tiles):
                    at = (d // 2 + m) * 128
                    ref[zz, e, m] = rows[:, at : at + 128]
            else:
                q = d // 2
                turned = []
                for m in range(tiles + 1):
                    at = (q + m) * 128
                    if at < rows.shape[1]:
                        turned.append(swap_halves(rows[:, at : at + 128]))
                    else:
                        turned.append(jnp.zeros((8, 128), F32))
                for m in range(tiles):
                    ref[zz, e, m] = jnp.where(low, turned[m], turned[m + 1])


def geometry(w):
    left = w + 1 + (w + 1) % 2
    return left, (left + 4 + w + 1 + 1) // 2


def step_body(tab, strips, w, own_ref, oth_ref, hi_ref, lo_ref, p_ref):
    left, count = geometry(w)
    nk = 4 + 2 * w
    for a in range(0, nk, 2):
        pair = []
        for b in (a, a + 1):
            pair.append(shifted(strips(b), left - 2 * w + b, count))
        store_split(hi_ref, lo_ref, a * 8, pair[0], pair[1])
    p_ref[...] = product(hi_ref, lo_ref, left * 64, 256).reshape(32, 8, count * 128)
    for e in range(4):
        write_slabs(tab, p_ref, own_ref, oth_ref, e, e * 8, left - (w + 1) + e, w + 2)


def first_step_kernel(tab, *refs):
    ins, (own_ref, oth_ref, cur_ref, hi_ref, lo_ref, p_ref, g_ref, sem) = refs[:8], refs[8:]
    fetch(ins, g_ref, sem)
    w = BAND
    base = tab[PLACE + 5] * 4 + 64 - w

    def strips(b):
        sk = tab[INV + ((base + b) & 63)]
        u, v, e = seat(tab, sk >> 2, sk & 3)
        strip = g_ref[u, v, e]
        if w <= b < w + 4:
            cur_ref[b - w] = strip
        return [strip[t] for t in range(w + 1)]

    step_body(tab, strips, w, own_ref, oth_ref, hi_ref, lo_ref, p_ref)


def step_kernel(w, reach, tab, *refs):
    n = 1 + 2 * len(reach)
    ins, (own_ref, oth_ref, hi_ref, lo_ref, p_ref) = refs[:n], refs[n:]

    def strips(b):
        off = b - w
        if 0 <= off < 4:
            ref, row = ins[0], off
        elif off < 0:
            d = (-off + 3) // 4
            ref, row = ins[2 * d - 1], off + 4 * (d - 1) + reach[d - 1]
        else:
            d = off // 4
            ref, row = ins[2 * d], off - 4 * d
        return [ref[row, t] for t in range(w + 1)]

    step_body(tab, strips, w, own_ref, oth_ref, hi_ref, lo_ref, p_ref)


def reach_of(w):
    return [min(4, w - 4 * d) for d in range((w + 3) // 4)]


def last_step_kernel(tab, *refs):
    ins, (own_ref, oth_ref, cur_ref, hi_ref, lo_ref, p_ref, g_ref, sem) = refs[:8], refs[8:]
    fetch(ins, g_ref, sem)
    w = BAND + STEPS - 1
    row0 = tab[PLACE] * 4
    left, count = w + 2, w + 2
    for e in range(4):
        i = tab[PERM + row0 + e]

        def strips(b):
            k = (i + b - w) & 63
            pos = k >> 2
            a, odd = pos >> 1, pos & 1
            r = jnp.where(a < 4, a * 4 + odd, (7 - a) * 4 + 3 - odd)
            u, v, ee = seat(tab, r, k & 3)
            strip = g_ref[u, v, ee]
            if b == w:
                cur_ref[e] = strip
            return [strip[t] for t in range(w + 1)]

        for a in range(0, 2 * w + 2, 2):
            one = shifted(strips(a), left - 2 * w + a, count)
            two = [None] * count
            if a + 1 <= 2 * w:
                two = shifted(strips(a + 1), left - 2 * w + a + 1, count)
            store_split(hi_ref, lo_ref, a * 8, one, two)
        p_ref[...] = product(hi_ref, lo_ref, left * 64, 64).reshape(8, 8, count * 128)
        write_slabs(tab, p_ref, own_ref, oth_ref, e, 0, 0, count)


def pair_kernel(tab, own_ref, got_ref, *outs):
    z = tab[PLACE + 6]
    for k in range(4):
        outs[k][...] = own_ref[z ^ k] + got_ref[z ^ k]


def polynomial(tab, step, cur, square):
    return jnp.where(tab[BRANCH + step] == 1, 2.0 * cur - square, square)


def close_kernel(step, cuts, tab, p0, p1, p2, p3, *refs):
    w = BAND + step
    if step == 0:
        cur_ref, refs = refs[0], refs[1:]
    else:
        cur_ref, refs = refs[0], refs[1:]
    low = low_half()
    i0 = tab[PLACE + 5] * 4
    for e in range(4):
        i = i0 + e
        turned = [swap_halves(cur_ref[e, t]) for t in range(w + 1)]
        zero = jnp.zeros((8, 128), F32)
        for m in range(w + 2):
            before = turned[m - 1] if m >= 1 else zero
            after = turned[m] if m <= w else zero
            cur = jnp.where(low, before, after)
            square = (p0[e, m] + p1[e, m]) + (p2[e, m] + p3[e, m])
            one = bit(tab, step + 1, i, (i + 2 * m + 63 - w) & 63)
            two = 0
            if 2 * m + 1 <= 2 * w + 2:
                two = bit(tab, step + 1, i, (i + 2 * m + 64 - w) & 63)
            keep = jnp.where(low, one, two) == 1
            value = jnp.where(keep, polynomial(tab, step, cur, square), 0.0)
            for ref, (lo, hi) in zip(refs, cuts):
                if lo <= e < hi:
                    ref[e - lo, m] = value


def finish_kernel(tab, p0, p1, p2, p3, cur_ref, y_ref):
    w = BAND + STEPS - 1
    low = low_half()
    row0 = tab[PLACE] * 4
    y_ref[...] = jnp.zeros_like(y_ref)
    for e in range(4):
        i = tab[PERM + row0 + e]
        for m in range(w + 2):
            cur = cur_ref[e, m - 1] if 1 <= m <= w + 1 else jnp.zeros((8, 128), F32)
            square = (p0[e, m] + p1[e, m]) + (p2[e, m] + p3[e, m])
            value = polynomial(tab, STEPS - 1, cur, square)
            turned = swap_halves(value)
            for half in (0, 1):
                v = 2 * m + half
                if v == 0:
                    continue
                j = (i + v + 64 - (w + 2)) & 63
                sj = tab[INV + j]
                odd = sj & 1
                piece = jnp.where(odd == half, value, turned)
                piece = jnp.where(bit(tab, STEPS, i, j) == 1, piece, 0.0)
                side = jnp.where(low, 0, 1) == odd
                c, t = sj >> 3, (sj & 7) >> 1
                y_ref[c, e, t] = jnp.where(side, piece, y_ref[c, e, t])


def join_kernel(tab, y_ref, out_ref):
    for c in range(8):
        for e in range(4):
            for t in range(4):
                out_ref[e * 64 + c * 8 : e * 64 + c * 8 + 8, t * 128 : (t + 1) * 128] = y_ref[c, e, t]


def tables(masks, branch, perm):
    r = lax.axis_index("row")
    z = lax.axis_index("col")
    h = lax.axis_index("layer")
    ids = jnp.arange(64, dtype=jnp.int32)
    inverse = jnp.sum(jnp.where(perm[:, None] == ids[None, :], ids[:, None], 0), axis=0)
    shifts = jnp.arange(32, dtype=jnp.int32)
    bits = jnp.sum(masks.reshape(6, 64, 2, 32) << shifts, axis=-1, dtype=jnp.int32)
    pos = jnp.sum(jnp.where(jnp.asarray(RING) == r, jnp.arange(16), 0))
    place = jnp.stack([r, z * 2 + h, r // 4, r % 4, h, pos, z, z]).astype(jnp.int32)
    return jnp.concatenate(
        [perm, inverse.astype(jnp.int32), branch, jnp.zeros((3,), jnp.int32), bits.reshape(-1), place]
    )


def reduce_group(tab, own, oth, tiles):
    got = core_swap(oth)
    parts = call(pair_kernel, [(4, tiles, 8, 128)] * 4, tab, [own, got])
    return [parts[0]] + [z_swap(parts[k], k) for k in (1, 2, 3)]


def exchange(value):
    return lax.all_to_all(value, GROUP, 0, 0, tiled=True)


def shards(density, masks, branch, perm):
    tab = tables(masks, branch, perm)
    (split,) = call(split_kernel, [(8, 4, 4, 8, 128)], tab, [density])
    split = exchange(split)
    halves = call(compact_kernel, [(2, BAND + 1, 8, 128)] * 2, tab, [split])
    gathered = gather_rows(*halves)
    for step in range(STEPS - 1):
        w = BAND + step
        left, count = geometry(w)
        rows = (4 + 2 * w) * 8
        part = (4, 4, w + 2, 8, 128)
        scratch = [
            pltpu.VMEM((rows, count * 128), BF16),
            pltpu.VMEM((rows, count * 128), BF16),
            pltpu.VMEM((32, 8, count * 128), F32),
        ]
        if step == 0:
            scratch += [pltpu.VMEM((8, 4, 2, w + 1, 8, 128), F32), pltpu.SemaphoreType.DMA((8,))]
            own, oth, cur = call(
                first_step_kernel, [part, part, (4, w + 1, 8, 128)], tab, gathered, scratch, True
            )
        else:
            reach = reach_of(w)
            kernel = lambda *refs, w=w, reach=reach: step_kernel(w, reach, *refs)
            own, oth = call(kernel, [part, part], tab, around, scratch)
        parts = reduce_group(tab, own, oth, w + 2)
        if step < STEPS - 2:
            reach = reach_of(w + 1)
            cuts = [(0, 4)]
            for n in reach:
                for cut in ((4 - n, 4), (0, n)):
                    if cut not in cuts:
                        cuts.append(cut)
        else:
            cuts = [(0, 2), (2, 4)]
        kernel = lambda *refs, step=step, cuts=cuts: close_kernel(step, cuts, *refs)
        shapes = [(hi - lo, w + 2, 8, 128) for lo, hi in cuts]
        pieces = call(kernel, shapes, tab, parts + [cur])
        if step < STEPS - 2:
            cur = pieces[0]
            around = [cur]
            for d, n in enumerate(reach):
                around.append(ring_shift(pieces[cuts.index((4 - n, 4))], d + 1))
                around.append(ring_shift(pieces[cuts.index((0, n))], -(d + 1)))
        else:
            gathered = gather_rows(*pieces)
    w = BAND + STEPS - 1
    part = (4, 4, w + 2, 8, 128)
    scratch = [
        pltpu.VMEM(((2 * w + 2) * 8, (w + 2) * 128), BF16),
        pltpu.VMEM(((2 * w + 2) * 8, (w + 2) * 128), BF16),
        pltpu.VMEM((8, 8, (w + 2) * 128), F32),
        pltpu.VMEM((8, 4, 2, w + 1, 8, 128), F32),
        pltpu.SemaphoreType.DMA((8,)),
    ]
    own, oth, cur = call(
        last_step_kernel, [part, part, (4, w + 1, 8, 128)], tab, gathered, scratch, True
    )
    parts = reduce_group(tab, own, oth, w + 2)
    (full,) = call(finish_kernel, [(8, 4, 4, 8, 128)], tab, parts + [cur])
    full = exchange(full)
    (out,) = call(join_kernel, [(256, 512)], tab, [full])
    return out


def solution(mesh):
    return jax.shard_map(
        shards,
        mesh=mesh,
        in_specs=(P("row", GROUP), P(), P(), P()),
        out_specs=P("row", GROUP),
        check_vma=False,
    )
```

```python
import jax
import jax.numpy as jnp
from jax import lax
from jax.experimental import pallas as pl
from jax.experimental.pallas import tpu as pltpu
from jax.sharding import PartitionSpec as P

STEPS = 5
BAND = 6
NB = 64
GROUP = ("col", "layer")
PERM, INV, BRANCH, BITS, PLACE = 0, 64, 128, 136, 136 + 6 * 128
F32, BF16 = jnp.float32, jnp.bfloat16


def ring_xy(pos):
    a, b = pos // 2, pos % 2
    return (a, b) if a < 4 else (7 - a, 3 - b)


RING = [ring_xy(p)[0] * 4 + ring_xy(p)[1] for p in range(16)]


def ring_shift(value, k):
    return lax.ppermute(value, "row", [(RING[p], RING[(p + k) % 16]) for p in range(16)])


def z_swap(value, k):
    return lax.ppermute(value, "col", [(i, i ^ k) for i in range(4)])


def core_swap(value):
    return lax.ppermute(value, "layer", [(0, 1), (1, 0)])


def low_half():
    return lax.broadcasted_iota(jnp.int32, (8, 128), 1) < 64


def swap_halves(tile):
    return pltpu.roll(tile, 64, 1)


def bit(tab, s, i, j):
    word = tab[BITS + s * 128 + i * 2 + lax.shift_right_logical(j, 5)]
    return lax.shift_right_logical(word, j & 31) & 1


def shifted(tiles, d, count):
    n = len(tiles)
    get = lambda seq, t: seq[t] if 0 <= t < n else None
    if d % 2 == 0:
        return [get(tiles, m - d // 2) for m in range(count)]
    q = (d - 1) // 2
    low = low_half()
    turned = [swap_halves(t) for t in tiles]
    out = []
    for m in range(count):
        a, b = get(turned, m - q - 1), get(turned, m - q)
        if a is None and b is None:
            out.append(None)
        else:
            zero = jnp.zeros((8, 128), F32)
            out.append(jnp.where(low, zero if a is None else a, zero if b is None else b))
    return out


def store_split(hi_ref, lo_ref, row, first, second):
    zero = jnp.zeros((8, 128), F32)
    for m, (a, b) in enumerate(zip(first, second)):
        both = jnp.concatenate([zero if a is None else a, zero if b is None else b], axis=0)
        hi = both.astype(BF16)
        hi_ref[row : row + 16, m * 128 : (m + 1) * 128] = hi
        lo_ref[row : row + 16, m * 128 : (m + 1) * 128] = (both - hi.astype(F32)).astype(BF16)


def tdot(a, b):
    return lax.dot_general(a, b, (((0,), (0,)), ((), ())), preferred_element_type=F32)


def product(hi_ref, lo_ref, start, width):
    xh = hi_ref[:, start : start + width]
    xl = lo_ref[:, start : start + width]
    zh = hi_ref[...]
    return tdot(xh, zh) + tdot(xh, lo_ref[...]) + tdot(xl, zh)


def call(kernel, outs, args, scratch=(), tab=None, here=(), there=()):
    space = lambda n, rest: pl.BlockSpec(memory_space=pl.ANY if n in rest else pltpu.VMEM)
    table = [] if tab is None else [pl.BlockSpec(memory_space=pltpu.SMEM)]
    return pl.pallas_call(
        kernel,
        out_shape=[jax.ShapeDtypeStruct(o, F32) for o in outs],
        in_specs=table + [space(n, here) for n in range(len(args))],
        out_specs=[space(n, there) for n in range(len(outs))],
        scratch_shapes=list(scratch),
        compiler_params=pltpu.CompilerParams(vmem_limit_bytes=48 * 1024 * 1024),
    )(*([] if tab is None else [tab]), *args)


def split_kernel(d_ref, *outs):
    me = lax.axis_index("col") * 2 + lax.axis_index("layer")
    for k in range(8):
        for e in range(4):
            start = pl.multiple_of(e * 64 + (me ^ k) * 8, 8)
            rows = d_ref[pl.ds(start, 8), :]
            for t in range(4):
                outs[k][e, t] = rows[:, t * 128 : (t + 1) * 128]


def copies_out(src_ref, out_ref, sem):
    copies = [pltpu.make_async_copy(src_ref, out_ref.at[n], sem.at[n]) for n in range(16)]
    for copy in copies:
        copy.start()
    for copy in copies:
        copy.wait()


def compact_kernel(tab, *refs):
    ins, (out_ref, x_ref, a_ref, sem) = refs[:8], refs[8:]
    for k in range(8):
        x_ref[k] = ins[k][...]
    low = low_half()
    row0 = tab[PLACE] * 4
    me = tab[PLACE + 1]
    for e in range(4):
        i = tab[PERM + row0 + e]
        halves = []
        for t in range(2 * BAND + 2):
            if t > 2 * BAND:
                halves.append(jnp.zeros((8, 128), F32))
                continue
            j = (i + t - BAND) & 63
            sj = tab[INV + j]
            tile = x_ref[(sj >> 3) ^ me, e, (sj & 7) >> 1]
            tile = jnp.where((sj & 1) == (t & 1), tile, swap_halves(tile))
            halves.append(jnp.where(bit(tab, 0, i, j) == 1, tile, 0.0))
        for t in range(BAND + 1):
            a_ref[e, t] = jnp.where(low, halves[2 * t], halves[2 * t + 1])
    copies_out(a_ref, out_ref, sem)


def gather_rows(copies):
    return lax.all_to_all(copies, "row", 0, 0, tiled=True)


def write_slabs(tab, p_ref, own_ref, oth_ref, e, base, d, tiles):
    h = tab[PLACE + 4]
    low = low_half()
    for zz in range(4):
        for ref, core in ((own_ref, h), (oth_ref, 1 - h)):
            rows = p_ref[base + 2 * zz + core]
            if d % 2 == 0:
                for m in range(tiles):
                    at = (d // 2 + m) * 128
                    ref[zz, e, m] = rows[:, at : at + 128]
            else:
                q = d // 2
                turned = []
                for m in range(tiles + 1):
                    at = (q + m) * 128
                    if at < rows.shape[1]:
                        turned.append(swap_halves(rows[:, at : at + 128]))
                    else:
                        turned.append(jnp.zeros((8, 128), F32))
                for m in range(tiles):
                    ref[zz, e, m] = jnp.where(low, turned[m], turned[m + 1])


def geometry(w):
    left = w + 1 + (w + 1) % 2
    return left, (left + 4 + w + 1 + 1) // 2


def step_body(tab, strips, w, own_ref, oth_ref, hi_ref, lo_ref, p_ref):
    left, count = geometry(w)
    nk = 4 + 2 * w
    for a in range(0, nk, 2):
        pair = []
        for b in (a, a + 1):
            tiles, first = strips(b)
            pair.append(shifted(tiles, left - 2 * w + b + 2 * first, count))
        store_split(hi_ref, lo_ref, a * 8, pair[0], pair[1])
    p_ref[...] = product(hi_ref, lo_ref, left * 64, 256).reshape(32, 8, count * 128)
    for e in range(4):
        write_slabs(tab, p_ref, own_ref, oth_ref, e, e * 8, left - (w + 1) + e, w + 2)


def first_step_kernel(tab, all_ref, own_ref, oth_ref, cur_ref, hi_ref, lo_ref, p_ref, g_ref, sem):
    w = BAND
    base = tab[PLACE + 5] * 4 + 64 - w
    copies = []
    for b in range(4 + 2 * w):
        sk = tab[INV + ((base + b) & 63)]
        copies.append(pltpu.make_async_copy(all_ref.at[sk >> 2, sk & 3], g_ref.at[b], sem.at[b]))
    for copy in copies:
        copy.start()
    for copy in copies:
        copy.wait()
    cur_ref[...] = g_ref[w : w + 4]

    def strips(b):
        return [g_ref[b, t] for t in range(w + 1)], 0

    step_body(tab, strips, w, own_ref, oth_ref, hi_ref, lo_ref, p_ref)


def step_kernel(w, pieces, tab, *refs):
    n = 1 + len(pieces)
    ins, (own_ref, oth_ref, hi_ref, lo_ref, p_ref) = refs[:n], refs[n:]

    def strips(b):
        off = b - w
        if 0 <= off < 4:
            return [ins[0][off, t] for t in range(w + 1)], 0
        d = (-off + 3) // 4 if off < 0 else -(off // 4)
        at = [piece[0] for piece in pieces].index(d)
        _, (lo, hi, first, last) = pieces[at]
        row = off + 4 * d - lo
        return [ins[1 + at][row, t] for t in range(last - first)], first

    step_body(tab, strips, w, own_ref, oth_ref, hi_ref, lo_ref, p_ref)


def halo_pieces(w):
    out = []
    for d in range(1, (w + 3) // 4 + 1):
        n = min(4, w - 4 * (d - 1))
        out.append((d, (4 - n, 4, 2 * (d - 1), w + 1)))
        out.append((-d, (0, n, 0, w + 1 - 2 * (d - 1))))
    return out


def last_step_kernel(tab, g_ref, own_ref, oth_ref, cur_ref, hi_ref, lo_ref, p_ref):
    w = BAND + STEPS - 1
    row0 = tab[PLACE] * 4
    left, count = w + 2, w + 2
    for e in range(4):
        i = tab[PERM + row0 + e]

        def strips(b):
            k = (i + b - w) & 63
            pos = k >> 2
            a, odd = pos >> 1, pos & 1
            r = jnp.where(a < 4, a * 4 + odd, (7 - a) * 4 + 3 - odd)
            strip = g_ref[r, k & 3]
            if b == w:
                cur_ref[e] = strip
            return [strip[t] for t in range(w + 1)]

        for a in range(0, 2 * w + 2, 2):
            one = shifted(strips(a), left - 2 * w + a, count)
            two = [None] * count
            if a + 1 <= 2 * w:
                two = shifted(strips(a + 1), left - 2 * w + a + 1, count)
            store_split(hi_ref, lo_ref, a * 8, one, two)
        p_ref[...] = product(hi_ref, lo_ref, left * 64, 64).reshape(8, 8, count * 128)
        write_slabs(tab, p_ref, own_ref, oth_ref, e, 0, 0, count)


def pair_kernel(tab, own_ref, got_ref, *outs):
    z = tab[PLACE + 6]
    for k in range(4):
        outs[k][...] = own_ref[z ^ k] + got_ref[z ^ k]


def polynomial(tab, step, cur, square):
    return jnp.where(tab[BRANCH + step] == 1, 2.0 * cur - square, square)


def close_kernel(step, cuts, tab, p0, p1, p2, p3, cur_ref, *refs):
    w = BAND + step
    if cuts is None:
        copies_ref, refs, sem = refs[0], refs[1:2], refs[2]
        cuts, spread = [(0, 4, 0, w + 2)], True
    else:
        spread = False
    low = low_half()
    i0 = tab[PLACE + 5] * 4
    for e in range(4):
        i = i0 + e
        turned = [swap_halves(cur_ref[e, t]) for t in range(w + 1)]
        zero = jnp.zeros((8, 128), F32)
        for m in range(w + 2):
            before = turned[m - 1] if m >= 1 else zero
            after = turned[m] if m <= w else zero
            cur = jnp.where(low, before, after)
            square = (p0[e, m] + p1[e, m]) + (p2[e, m] + p3[e, m])
            one = bit(tab, step + 1, i, (i + 2 * m + 63 - w) & 63)
            two = 0
            if 2 * m + 1 <= 2 * w + 2:
                two = bit(tab, step + 1, i, (i + 2 * m + 64 - w) & 63)
            keep = jnp.where(low, one, two) == 1
            value = jnp.where(keep, polynomial(tab, step, cur, square), 0.0)
            for ref, (lo, hi, first, last) in zip(refs, cuts):
                if lo <= e < hi and first <= m < last:
                    ref[e - lo, m - first] = value
    if spread:
        copies_out(refs[0], copies_ref, sem)


def finish_kernel(tab, p0, p1, p2, p3, cur_ref, y_ref):
    w = BAND + STEPS - 1
    low = low_half()
    row0 = tab[PLACE] * 4
    y_ref[...] = jnp.zeros_like(y_ref)
    for e in range(4):
        i = tab[PERM + row0 + e]
        for m in range(w + 2):
            cur = cur_ref[e, m - 1] if 1 <= m <= w + 1 else jnp.zeros((8, 128), F32)
            square = (p0[e, m] + p1[e, m]) + (p2[e, m] + p3[e, m])
            value = polynomial(tab, STEPS - 1, cur, square)
            turned = swap_halves(value)
            for half in (0, 1):
                v = 2 * m + half
                if v == 0:
                    continue
                j = (i + v + 64 - (w + 2)) & 63
                sj = tab[INV + j]
                odd = sj & 1
                piece = jnp.where(odd == half, value, turned)
                piece = jnp.where(bit(tab, STEPS, i, j) == 1, piece, 0.0)
                side = jnp.where(low, 0, 1) == odd
                c, t = sj >> 3, (sj & 7) >> 1
                y_ref[c, e, t] = jnp.where(side, piece, y_ref[c, e, t])


def join_kernel(y_ref, out_ref):
    for c in range(8):
        for e in range(4):
            for t in range(4):
                out_ref[e * 64 + c * 8 : e * 64 + c * 8 + 8, t * 128 : (t + 1) * 128] = y_ref[c, e, t]


def tables(masks, branch, perm):
    r = lax.axis_index("row")
    z = lax.axis_index("col")
    h = lax.axis_index("layer")
    ids = jnp.arange(64, dtype=jnp.int32)
    inverse = jnp.sum(jnp.where(perm[:, None] == ids[None, :], ids[:, None], 0), axis=0)
    shifts = jnp.arange(32, dtype=jnp.int32)
    bits = jnp.sum(masks.reshape(6, 64, 2, 32) << shifts, axis=-1, dtype=jnp.int32)
    pos = jnp.sum(jnp.where(jnp.asarray(RING) == r, jnp.arange(16), 0))
    place = jnp.stack([r, z * 2 + h, r // 4, r % 4, h, pos, z, z]).astype(jnp.int32)
    return jnp.concatenate(
        [perm, inverse.astype(jnp.int32), branch, jnp.zeros((3,), jnp.int32), bits.reshape(-1), place]
    )


def reduce_group(tab, own, oth, tiles):
    got = core_swap(oth)
    parts = call(pair_kernel, [(4, tiles, 8, 128)] * 4, [own, got], tab=tab)
    return [parts[0]] + [z_swap(parts[k], k) for k in (1, 2, 3)]


def exchange(value):
    return lax.all_to_all(value, GROUP, 0, 0, tiled=True)


def group_swap(value, k):
    return lax.ppermute(value, GROUP, [(i, i ^ k) for i in range(8)])


def shards(density, masks, branch, perm):
    split = call(split_kernel, [(4, 4, 8, 128)] * 8, [density])
    split = [split[0]] + [group_swap(split[k], k) for k in range(1, 8)]
    tab = tables(masks, branch, perm)
    spread = [pltpu.SemaphoreType.DMA((16,))]
    (copies,) = call(
        compact_kernel,
        [(16, 4, BAND + 1, 8, 128)],
        split,
        [pltpu.VMEM((8, 4, 4, 8, 128), F32), pltpu.VMEM((4, BAND + 1, 8, 128), F32)] + spread,
        tab=tab,
        there=(0,),
    )
    gathered = gather_rows(copies)
    for step in range(STEPS - 1):
        w = BAND + step
        left, count = geometry(w)
        rows = (4 + 2 * w) * 8
        part = (4, 4, w + 2, 8, 128)
        scratch = [
            pltpu.VMEM((rows, count * 128), BF16),
            pltpu.VMEM((rows, count * 128), BF16),
            pltpu.VMEM((32, 8, count * 128), F32),
        ]
        if step == 0:
            strips = 4 + 2 * w
            scratch += [pltpu.VMEM((strips, w + 1, 8, 128), F32), pltpu.SemaphoreType.DMA((strips,))]
            own, oth, cur = call(
                first_step_kernel,
                [part, part, (4, w + 1, 8, 128)],
                [gathered],
                scratch,
                tab=tab,
                here=(0,),
            )
        else:
            kernel = lambda *refs, w=w, pieces=pieces: step_kernel(w, pieces, *refs)
            own, oth = call(kernel, [part, part], [cur] + around, scratch, tab=tab)
        parts = reduce_group(tab, own, oth, w + 2)
        if step < STEPS - 2:
            pieces = halo_pieces(w + 1)
            cuts = [(0, 4, 0, w + 2)]
            for _, cut in pieces:
                if cut not in cuts:
                    cuts.append(cut)
            kernel = lambda *refs, step=step, cuts=cuts: close_kernel(step, cuts, *refs)
            shapes = [(hi - lo, last - first, 8, 128) for lo, hi, first, last in cuts]
            sent = call(kernel, shapes, parts + [cur], tab=tab)
            cur = sent[0]
            around = [ring_shift(sent[cuts.index(cut)], d) for d, cut in pieces]
        else:
            kernel = lambda *refs, step=step: close_kernel(step, None, *refs)
            scratch = [pltpu.VMEM((4, w + 2, 8, 128), F32)] + spread
            (copies,) = call(
                kernel, [(16, 4, w + 2, 8, 128)], parts + [cur], scratch, tab=tab, there=(0,)
            )
            gathered = gather_rows(copies)
    w = BAND + STEPS - 1
    part = (4, 4, w + 2, 8, 128)
    scratch = [
        pltpu.VMEM(((2 * w + 2) * 8, (w + 2) * 128), BF16),
        pltpu.VMEM(((2 * w + 2) * 8, (w + 2) * 128), BF16),
        pltpu.VMEM((8, 8, (w + 2) * 128), F32),
    ]
    own, oth, cur = call(
        last_step_kernel, [part, part, (4, w + 1, 8, 128)], [gathered], scratch, tab=tab
    )
    parts = reduce_group(tab, own, oth, w + 2)
    (full,) = call(finish_kernel, [(8, 4, 4, 8, 128)], parts + [cur], tab=tab)
    full = exchange(full)
    (out,) = call(join_kernel, [(256, 512)], [full])
    return out


def solution(mesh):
    return jax.shard_map(
        shards,
        mesh=mesh,
        in_specs=(P("row", GROUP), P(), P(), P()),
        out_specs=P("row", GROUP),
        check_vma=False,
    )
```

```python
import jax
import jax.numpy as jnp
from jax import lax
from jax.experimental import pallas as pl
from jax.experimental.pallas import tpu as pltpu
from jax.sharding import PartitionSpec as P

STEPS = 5
BAND = 6
NB = 64
GROUP = ("col", "layer")
PERM, INV, BRANCH, BITS, PLACE = 0, 64, 128, 136, 136 + 6 * 128
F32, BF16 = jnp.float32, jnp.bfloat16


def ring_xy(pos):
    a, b = pos // 2, pos % 2
    return (a, b) if a < 4 else (7 - a, 3 - b)


RING = [ring_xy(p)[0] * 4 + ring_xy(p)[1] for p in range(16)]


def ring_shift(value, k):
    return lax.ppermute(value, "row", [(RING[p], RING[(p + k) % 16]) for p in range(16)])


def core_swap(value):
    return lax.ppermute(value, "layer", [(0, 1), (1, 0)])


def low_half():
    return lax.broadcasted_iota(jnp.int32, (8, 128), 1) < 64


def swap_halves(tile):
    return pltpu.roll(tile, 64, 1)


def bit(tab, s, i, j):
    word = tab[BITS + s * 128 + i * 2 + lax.shift_right_logical(j, 5)]
    return lax.shift_right_logical(word, j & 31) & 1


def shifted(tiles, d, count):
    n = len(tiles)
    get = lambda seq, t: seq[t] if 0 <= t < n else None
    if d % 2 == 0:
        return [get(tiles, m - d // 2) for m in range(count)]
    q = (d - 1) // 2
    low = low_half()
    turned = [swap_halves(t) for t in tiles]
    out = []
    for m in range(count):
        a, b = get(turned, m - q - 1), get(turned, m - q)
        if a is None and b is None:
            out.append(None)
        else:
            zero = jnp.zeros((8, 128), F32)
            out.append(jnp.where(low, zero if a is None else a, zero if b is None else b))
    return out


def store_split(hi_ref, lo_ref, row, first, second):
    zero = jnp.zeros((8, 128), F32)
    for m, (a, b) in enumerate(zip(first, second)):
        both = jnp.concatenate([zero if a is None else a, zero if b is None else b], axis=0)
        hi = both.astype(BF16)
        hi_ref[row : row + 16, m * 128 : (m + 1) * 128] = hi
        lo_ref[row : row + 16, m * 128 : (m + 1) * 128] = (both - hi.astype(F32)).astype(BF16)


def tdot(a, b):
    return lax.dot_general(a, b, (((0,), (0,)), ((), ())), preferred_element_type=F32)


def product(hi_ref, lo_ref, start, width):
    xh = hi_ref[:, start : start + width]
    xl = lo_ref[:, start : start + width]
    zh = hi_ref[...]
    return tdot(xh, zh) + tdot(xh, lo_ref[...]) + tdot(xl, zh)


def call(kernel, outs, args, scratch=(), tab=None, here=(), there=()):
    space = lambda n, rest: pl.BlockSpec(memory_space=pl.ANY if n in rest else pltpu.VMEM)
    table = [] if tab is None else [pl.BlockSpec(memory_space=pltpu.SMEM)]
    return pl.pallas_call(
        kernel,
        out_shape=[jax.ShapeDtypeStruct(o, F32) for o in outs],
        in_specs=table + [space(n, here) for n in range(len(args))],
        out_specs=[space(n, there) for n in range(len(outs))],
        scratch_shapes=list(scratch),
        compiler_params=pltpu.CompilerParams(vmem_limit_bytes=48 * 1024 * 1024),
    )(*([] if tab is None else [tab]), *args)


def split_kernel(d_ref, *outs):
    me = lax.axis_index("col") * 2 + lax.axis_index("layer")
    for k in range(8):
        for e in range(4):
            start = pl.multiple_of(e * 64 + (me ^ k) * 8, 8)
            rows = d_ref[pl.ds(start, 8), :]
            for t in range(4):
                outs[k][e, t] = rows[:, t * 128 : (t + 1) * 128]


def compact_kernel(tab, *refs):
    ins, (a_ref, x_ref) = refs[:8], refs[8:]
    for k in range(8):
        x_ref[k] = ins[k][...]
    low = low_half()
    row0 = tab[PLACE] * 4
    me = tab[PLACE + 1]
    for e in range(4):
        i = tab[PERM + row0 + e]
        halves = []
        for t in range(2 * BAND + 2):
            if t > 2 * BAND:
                halves.append(jnp.zeros((8, 128), F32))
                continue
            j = (i + t - BAND) & 63
            sj = tab[INV + j]
            tile = x_ref[(sj >> 3) ^ me, e, (sj & 7) >> 1]
            tile = jnp.where((sj & 1) == (t & 1), tile, swap_halves(tile))
            halves.append(jnp.where(bit(tab, 0, i, j) == 1, tile, 0.0))
        for t in range(BAND + 1):
            a_ref[e, t] = jnp.where(low, halves[2 * t], halves[2 * t + 1])


def gather_rows(rows):
    copies = jnp.broadcast_to(rows[None], (16,) + rows.shape)
    return lax.all_to_all(copies, "row", 0, 0, tiled=True)


def write_slabs(tab, p_ref, own_ref, oth_ref, e, base, d, tiles):
    h = tab[PLACE + 4]
    low = low_half()
    for zz in range(4):
        for ref, core in ((own_ref, h), (oth_ref, 1 - h)):
            rows = p_ref[base + 2 * zz + core]
            if d % 2 == 0:
                for m in range(tiles):
                    at = (d // 2 + m) * 128
                    ref[zz, e, m] = rows[:, at : at + 128]
            else:
                q = d // 2
                turned = []
                for m in range(tiles + 1):
                    at = (q + m) * 128
                    if at < rows.shape[1]:
                        turned.append(swap_halves(rows[:, at : at + 128]))
                    else:
                        turned.append(jnp.zeros((8, 128), F32))
                for m in range(tiles):
                    ref[zz, e, m] = jnp.where(low, turned[m], turned[m + 1])


def geometry(w):
    left = w + 1 + (w + 1) % 2
    return left, (left + 4 + w + 1 + 1) // 2


def step_body(tab, strips, w, own_ref, oth_ref, hi_ref, lo_ref, p_ref):
    left, count = geometry(w)
    nk = 4 + 2 * w
    for a in range(0, nk, 2):
        pair = []
        for b in (a, a + 1):
            tiles, first = strips(b)
            pair.append(shifted(tiles, left - 2 * w + b + 2 * first, count))
        store_split(hi_ref, lo_ref, a * 8, pair[0], pair[1])
    p_ref[...] = product(hi_ref, lo_ref, left * 64, 256).reshape(32, 8, count * 128)
    for e in range(4):
        write_slabs(tab, p_ref, own_ref, oth_ref, e, e * 8, left - (w + 1) + e, w + 2)


def first_step_kernel(tab, all_ref, own_ref, oth_ref, cur_ref, hi_ref, lo_ref, p_ref, g_ref, sem):
    w = BAND
    base = tab[PLACE + 5] * 4 + 64 - w
    copies = []
    for b in range(4 + 2 * w):
        sk = tab[INV + ((base + b) & 63)]
        copies.append(pltpu.make_async_copy(all_ref.at[sk >> 2, sk & 3], g_ref.at[b], sem.at[b]))
    for copy in copies:
        copy.start()
    for copy in copies:
        copy.wait()
    cur_ref[...] = g_ref[w : w + 4]

    def strips(b):
        return [g_ref[b, t] for t in range(w + 1)], 0

    step_body(tab, strips, w, own_ref, oth_ref, hi_ref, lo_ref, p_ref)


def step_kernel(w, pieces, tab, *refs):
    n = 1 + len(pieces)
    ins, (own_ref, oth_ref, hi_ref, lo_ref, p_ref) = refs[:n], refs[n:]

    def strips(b):
        off = b - w
        if 0 <= off < 4:
            return [ins[0][off, t] for t in range(w + 1)], 0
        d = (-off + 3) // 4 if off < 0 else -(off // 4)
        at = [piece[0] for piece in pieces].index(d)
        _, (lo, hi, first, last) = pieces[at]
        row = off + 4 * d - lo
        return [ins[1 + at][row, t] for t in range(last - first)], first

    step_body(tab, strips, w, own_ref, oth_ref, hi_ref, lo_ref, p_ref)


def halo_pieces(w):
    out = []
    for d in range(1, (w + 3) // 4 + 1):
        n = min(4, w - 4 * (d - 1))
        out.append((d, (4 - n, 4, 2 * (d - 1), w + 1)))
        out.append((-d, (0, n, 0, w + 1 - 2 * (d - 1))))
    return out


def last_step_kernel(tab, g_ref, own_ref, oth_ref, cur_ref, hi_ref, lo_ref, p_ref):
    w = BAND + STEPS - 1
    row0 = tab[PLACE] * 4
    left, count = w + 2, w + 2
    for e in range(4):
        i = tab[PERM + row0 + e]

        def strips(b):
            k = (i + b - w) & 63
            pos = k >> 2
            a, odd = pos >> 1, pos & 1
            r = jnp.where(a < 4, a * 4 + odd, (7 - a) * 4 + 3 - odd)
            strip = g_ref[r, k & 3]
            if b == w:
                cur_ref[e] = strip
            return [strip[t] for t in range(w + 1)]

        for a in range(0, 2 * w + 2, 2):
            one = shifted(strips(a), left - 2 * w + a, count)
            two = [None] * count
            if a + 1 <= 2 * w:
                two = shifted(strips(a + 1), left - 2 * w + a + 1, count)
            store_split(hi_ref, lo_ref, a * 8, one, two)
        p_ref[...] = product(hi_ref, lo_ref, left * 64, 64).reshape(8, 8, count * 128)
        write_slabs(tab, p_ref, own_ref, oth_ref, e, 0, 0, count)


def pair_kernel(own_ref, got_ref, out_ref):
    out_ref[...] = own_ref[...] + got_ref[...]


def total(ref, e, m):
    return (ref[0, e, m] + ref[1, e, m]) + (ref[2, e, m] + ref[3, e, m])


def polynomial(tab, step, cur, square):
    return jnp.where(tab[BRANCH + step] == 1, 2.0 * cur - square, square)


def close_kernel(step, cuts, tab, part_ref, cur_ref, *refs):
    w = BAND + step
    low = low_half()
    i0 = tab[PLACE + 5] * 4
    for e in range(4):
        i = i0 + e
        turned = [swap_halves(cur_ref[e, t]) for t in range(w + 1)]
        zero = jnp.zeros((8, 128), F32)
        for m in range(w + 2):
            before = turned[m - 1] if m >= 1 else zero
            after = turned[m] if m <= w else zero
            cur = jnp.where(low, before, after)
            square = total(part_ref, e, m)
            one = bit(tab, step + 1, i, (i + 2 * m + 63 - w) & 63)
            two = 0
            if 2 * m + 1 <= 2 * w + 2:
                two = bit(tab, step + 1, i, (i + 2 * m + 64 - w) & 63)
            keep = jnp.where(low, one, two) == 1
            value = jnp.where(keep, polynomial(tab, step, cur, square), 0.0)
            for ref, (lo, hi, first, last) in zip(refs, cuts):
                if lo <= e < hi and first <= m < last:
                    ref[e - lo, m - first] = value


def finish_kernel(tab, part_ref, cur_ref, y_ref):
    w = BAND + STEPS - 1
    low = low_half()
    row0 = tab[PLACE] * 4
    y_ref[...] = jnp.zeros_like(y_ref)
    for e in range(4):
        i = tab[PERM + row0 + e]
        for m in range(w + 2):
            cur = cur_ref[e, m - 1] if 1 <= m <= w + 1 else jnp.zeros((8, 128), F32)
            square = total(part_ref, e, m)
            value = polynomial(tab, STEPS - 1, cur, square)
            turned = swap_halves(value)
            for half in (0, 1):
                v = 2 * m + half
                if v == 0:
                    continue
                j = (i + v + 64 - (w + 2)) & 63
                sj = tab[INV + j]
                odd = sj & 1
                piece = jnp.where(odd == half, value, turned)
                piece = jnp.where(bit(tab, STEPS, i, j) == 1, piece, 0.0)
                side = jnp.where(low, 0, 1) == odd
                c, t = sj >> 3, (sj & 7) >> 1
                y_ref[c, e, t] = jnp.where(side, piece, y_ref[c, e, t])


def join_kernel(y_ref, out_ref):
    for c in range(8):
        for e in range(4):
            for t in range(4):
                out_ref[e * 64 + c * 8 : e * 64 + c * 8 + 8, t * 128 : (t + 1) * 128] = y_ref[c, e, t]


def tables(masks, branch, perm):
    r = lax.axis_index("row")
    z = lax.axis_index("col")
    h = lax.axis_index("layer")
    ids = jnp.arange(64, dtype=jnp.int32)
    inverse = jnp.sum(jnp.where(perm[:, None] == ids[None, :], ids[:, None], 0), axis=0)
    shifts = jnp.arange(32, dtype=jnp.int32)
    bits = jnp.sum(masks.reshape(6, 64, 2, 32) << shifts, axis=-1, dtype=jnp.int32)
    pos = jnp.sum(jnp.where(jnp.asarray(RING) == r, jnp.arange(16), 0))
    place = jnp.stack([r, z * 2 + h, r // 4, r % 4, h, pos, z, z]).astype(jnp.int32)
    return jnp.concatenate(
        [perm, inverse.astype(jnp.int32), branch, jnp.zeros((3,), jnp.int32), bits.reshape(-1), place]
    )


def reduce_group(own, oth):
    (pair,) = call(pair_kernel, [own.shape], [own, core_swap(oth)])
    return lax.all_to_all(pair, "col", 0, 0, tiled=True)


def exchange(value):
    return lax.all_to_all(value, GROUP, 0, 0, tiled=True)


def group_swap(value, k):
    return lax.ppermute(value, GROUP, [(i, i ^ k) for i in range(8)])


def shards(density, masks, branch, perm):
    split = call(split_kernel, [(4, 4, 8, 128)] * 8, [density])
    split = [split[0]] + [group_swap(split[k], k) for k in range(1, 8)]
    tab = tables(masks, branch, perm)
    (rows,) = call(
        compact_kernel,
        [(4, BAND + 1, 8, 128)],
        split,
        [pltpu.VMEM((8, 4, 4, 8, 128), F32)],
        tab=tab,
    )
    gathered = gather_rows(rows)
    for step in range(STEPS - 1):
        w = BAND + step
        left, count = geometry(w)
        rows = (4 + 2 * w) * 8
        part = (4, 4, w + 2, 8, 128)
        scratch = [
            pltpu.VMEM((rows, count * 128), BF16),
            pltpu.VMEM((rows, count * 128), BF16),
            pltpu.VMEM((32, 8, count * 128), F32),
        ]
        if step == 0:
            strips = 4 + 2 * w
            scratch += [pltpu.VMEM((strips, w + 1, 8, 128), F32), pltpu.SemaphoreType.DMA((strips,))]
            own, oth, cur = call(
                first_step_kernel,
                [part, part, (4, w + 1, 8, 128)],
                [gathered],
                scratch,
                tab=tab,
                here=(0,),
            )
        else:
            kernel = lambda *refs, w=w, pieces=pieces: step_kernel(w, pieces, *refs)
            own, oth = call(kernel, [part, part], [cur] + around, scratch, tab=tab)
        parts = reduce_group(own, oth)
        pieces = halo_pieces(w + 1) if step < STEPS - 2 else []
        cuts = [(0, 4, 0, w + 2)]
        for _, cut in pieces:
            if cut not in cuts:
                cuts.append(cut)
        kernel = lambda *refs, step=step, cuts=cuts: close_kernel(step, cuts, *refs)
        shapes = [(hi - lo, last - first, 8, 128) for lo, hi, first, last in cuts]
        sent = call(kernel, shapes, [parts, cur], tab=tab)
        cur = sent[0]
        around = [ring_shift(sent[cuts.index(cut)], d) for d, cut in pieces]
    gathered = gather_rows(cur)
    w = BAND + STEPS - 1
    part = (4, 4, w + 2, 8, 128)
    scratch = [
        pltpu.VMEM(((2 * w + 2) * 8, (w + 2) * 128), BF16),
        pltpu.VMEM(((2 * w + 2) * 8, (w + 2) * 128), BF16),
        pltpu.VMEM((8, 8, (w + 2) * 128), F32),
    ]
    own, oth, cur = call(
        last_step_kernel, [part, part, (4, w + 1, 8, 128)], [gathered], scratch, tab=tab
    )
    parts = reduce_group(own, oth)
    (full,) = call(finish_kernel, [(8, 4, 4, 8, 128)], [parts, cur], tab=tab)
    full = exchange(full)
    (out,) = call(join_kernel, [(256, 512)], [full])
    return out


def solution(mesh):
    return jax.shard_map(
        shards,
        mesh=mesh,
        in_specs=(P("row", GROUP), P(), P(), P()),
        out_specs=P("row", GROUP),
        check_vma=False,
    )
```

```python
import jax
import jax.numpy as jnp
from jax import lax
from jax.experimental import pallas as pl
from jax.experimental.pallas import tpu as pltpu
from jax.sharding import PartitionSpec as P

STEPS = 5
BAND = 6
NB = 64
GROUP = ("col", "layer")
PERM, INV, BRANCH, BITS, PLACE = 0, 64, 128, 136, 136 + 6 * 128
F32, BF16 = jnp.float32, jnp.bfloat16


def ring_xy(pos):
    a, b = pos // 2, pos % 2
    return (a, b) if a < 4 else (7 - a, 3 - b)


RING = [ring_xy(p)[0] * 4 + ring_xy(p)[1] for p in range(16)]


def permute(value, axes, pairs):
    flat = value.reshape(-1, 128)
    return lax.ppermute(flat, axes, pairs).reshape(value.shape)


def exchange(value, axes):
    flat = value.reshape(value.shape[0], -1, 128)
    return lax.all_to_all(flat, axes, 0, 0, tiled=True).reshape(value.shape)


def ring_shift(value, k):
    return permute(value, "row", [(RING[p], RING[(p + k) % 16]) for p in range(16)])


def core_swap(value):
    return permute(value, "layer", [(0, 1), (1, 0)])


def low_half():
    return lax.broadcasted_iota(jnp.int32, (8, 128), 1) < 64


def swap_halves(tile):
    return pltpu.roll(tile, 64, 1)


def bit(tab, s, i, j):
    word = tab[BITS + s * 128 + i * 2 + lax.shift_right_logical(j, 5)]
    return lax.shift_right_logical(word, j & 31) & 1


def shifted(tiles, d, count):
    n = len(tiles)
    get = lambda seq, t: seq[t] if 0 <= t < n else None
    if d % 2 == 0:
        return [get(tiles, m - d // 2) for m in range(count)]
    q = (d - 1) // 2
    low = low_half()
    turned = [swap_halves(t) for t in tiles]
    out = []
    for m in range(count):
        a, b = get(turned, m - q - 1), get(turned, m - q)
        if a is None and b is None:
            out.append(None)
        else:
            zero = jnp.zeros((8, 128), F32)
            out.append(jnp.where(low, zero if a is None else a, zero if b is None else b))
    return out


def store_split(hi_ref, lo_ref, row, first, second):
    zero = jnp.zeros((8, 128), F32)
    for m, (a, b) in enumerate(zip(first, second)):
        both = jnp.concatenate([zero if a is None else a, zero if b is None else b], axis=0)
        hi = both.astype(BF16)
        hi_ref[row : row + 16, m * 128 : (m + 1) * 128] = hi
        lo_ref[row : row + 16, m * 128 : (m + 1) * 128] = (both - hi.astype(F32)).astype(BF16)


def tdot(a, b):
    return lax.dot_general(a, b, (((0,), (0,)), ((), ())), preferred_element_type=F32)


def product(hi_ref, lo_ref, start, width):
    xh = hi_ref[:, start : start + width]
    xl = lo_ref[:, start : start + width]
    zh = hi_ref[...]
    return tdot(xh, zh) + tdot(xh, lo_ref[...]) + tdot(xl, zh)


def call(kernel, outs, args, scratch=(), tab=None, here=(), there=()):
    space = lambda n, rest: pl.BlockSpec(memory_space=pl.ANY if n in rest else pltpu.VMEM)
    table = [] if tab is None else [pl.BlockSpec(memory_space=pltpu.SMEM)]
    return pl.pallas_call(
        kernel,
        out_shape=[jax.ShapeDtypeStruct(o, F32) for o in outs],
        in_specs=table + [space(n, here) for n in range(len(args))],
        out_specs=[space(n, there) for n in range(len(outs))],
        scratch_shapes=list(scratch),
        compiler_params=pltpu.CompilerParams(vmem_limit_bytes=48 * 1024 * 1024),
    )(*([] if tab is None else [tab]), *args)


def split_kernel(d_ref, *outs):
    me = lax.axis_index("col") * 2 + lax.axis_index("layer")
    for k in range(8):
        for e in range(4):
            start = pl.multiple_of(e * 64 + (me ^ k) * 8, 8)
            rows = d_ref[pl.ds(start, 8), :]
            for t in range(4):
                outs[k][e, t] = rows[:, t * 128 : (t + 1) * 128]


def compact_kernel(tab, *refs):
    ins, (a_ref, x_ref) = refs[:8], refs[8:]
    for k in range(8):
        x_ref[k] = ins[k][...]
    low = low_half()
    row0 = tab[PLACE] * 4
    me = tab[PLACE + 1]
    for e in range(4):
        i = tab[PERM + row0 + e]
        halves = []
        for t in range(2 * BAND + 2):
            if t > 2 * BAND:
                halves.append(jnp.zeros((8, 128), F32))
                continue
            j = (i + t - BAND) & 63
            sj = tab[INV + j]
            tile = x_ref[(sj >> 3) ^ me, e, (sj & 7) >> 1]
            tile = jnp.where((sj & 1) == (t & 1), tile, swap_halves(tile))
            halves.append(jnp.where(bit(tab, 0, i, j) == 1, tile, 0.0))
        for t in range(BAND + 1):
            a_ref[e, t] = jnp.where(low, halves[2 * t], halves[2 * t + 1])


def gather_rows(rows):
    copies = jnp.broadcast_to(rows[None], (16,) + rows.shape)
    return exchange(copies, "row")


def write_slabs(tab, p_ref, own_ref, oth_ref, e, base, d, tiles):
    h = tab[PLACE + 4]
    low = low_half()
    for zz in range(4):
        for ref, core in ((own_ref, h), (oth_ref, 1 - h)):
            rows = p_ref[base + 2 * zz + core]
            if d % 2 == 0:
                for m in range(tiles):
                    at = (d // 2 + m) * 128
                    ref[zz, e, m] = rows[:, at : at + 128]
            else:
                q = d // 2
                turned = []
                for m in range(tiles + 1):
                    at = (q + m) * 128
                    if at < rows.shape[1]:
                        turned.append(swap_halves(rows[:, at : at + 128]))
                    else:
                        turned.append(jnp.zeros((8, 128), F32))
                for m in range(tiles):
                    ref[zz, e, m] = jnp.where(low, turned[m], turned[m + 1])


def geometry(w):
    left = w + 1 + (w + 1) % 2
    return left, (left + 4 + w + 1 + 1) // 2


def step_body(tab, strips, w, own_ref, oth_ref, hi_ref, lo_ref, p_ref):
    left, count = geometry(w)
    nk = 4 + 2 * w
    for a in range(0, nk, 2):
        pair = []
        for b in (a, a + 1):
            tiles, first = strips(b)
            pair.append(shifted(tiles, left - 2 * w + b + 2 * first, count))
        store_split(hi_ref, lo_ref, a * 8, pair[0], pair[1])
    p_ref[...] = product(hi_ref, lo_ref, left * 64, 256).reshape(32, 8, count * 128)
    for e in range(4):
        write_slabs(tab, p_ref, own_ref, oth_ref, e, e * 8, left - (w + 1) + e, w + 2)


def first_step_kernel(tab, all_ref, own_ref, oth_ref, cur_ref, hi_ref, lo_ref, p_ref, g_ref, sem):
    w = BAND
    base = tab[PLACE + 5] * 4 + 64 - w
    copies = []
    for b in range(4 + 2 * w):
        sk = tab[INV + ((base + b) & 63)]
        copies.append(pltpu.make_async_copy(all_ref.at[sk >> 2, sk & 3], g_ref.at[b], sem.at[b]))
    for copy in copies:
        copy.start()
    for copy in copies:
        copy.wait()
    cur_ref[...] = g_ref[w : w + 4]

    def strips(b):
        return [g_ref[b, t] for t in range(w + 1)], 0

    step_body(tab, strips, w, own_ref, oth_ref, hi_ref, lo_ref, p_ref)


def step_kernel(w, pieces, tab, *refs):
    n = 1 + len(pieces)
    ins, (own_ref, oth_ref, hi_ref, lo_ref, p_ref) = refs[:n], refs[n:]

    def strips(b):
        off = b - w
        if 0 <= off < 4:
            return [ins[0][off, t] for t in range(w + 1)], 0
        d = (-off + 3) // 4 if off < 0 else -(off // 4)
        at = [piece[0] for piece in pieces].index(d)
        _, (lo, hi, first, last) = pieces[at]
        row = off + 4 * d - lo
        return [ins[1 + at][row, t] for t in range(last - first)], first

    step_body(tab, strips, w, own_ref, oth_ref, hi_ref, lo_ref, p_ref)


def halo_pieces(w):
    out = []
    for d in range(1, (w + 3) // 4 + 1):
        n = min(4, w - 4 * (d - 1))
        out.append((d, (4 - n, 4, 2 * (d - 1), w + 1)))
        out.append((-d, (0, n, 0, w + 1 - 2 * (d - 1))))
    return out


def last_step_kernel(tab, g_ref, own_ref, oth_ref, cur_ref, hi_ref, lo_ref, p_ref):
    w = BAND + STEPS - 1
    row0 = tab[PLACE] * 4
    left, count = w + 2, w + 2
    for e in range(4):
        i = tab[PERM + row0 + e]

        def strips(b):
            k = (i + b - w) & 63
            pos = k >> 2
            a, odd = pos >> 1, pos & 1
            r = jnp.where(a < 4, a * 4 + odd, (7 - a) * 4 + 3 - odd)
            strip = g_ref[r, k & 3]
            if b == w:
                cur_ref[e] = strip
            return [strip[t] for t in range(w + 1)]

        for a in range(0, 2 * w + 2, 2):
            one = shifted(strips(a), left - 2 * w + a, count)
            two = [None] * count
            if a + 1 <= 2 * w:
                two = shifted(strips(a + 1), left - 2 * w + a + 1, count)
            store_split(hi_ref, lo_ref, a * 8, one, two)
        p_ref[...] = product(hi_ref, lo_ref, left * 64, 64).reshape(8, 8, count * 128)
        write_slabs(tab, p_ref, own_ref, oth_ref, e, 0, 0, count)


def pair_kernel(own_ref, got_ref, out_ref):
    out_ref[...] = own_ref[...] + got_ref[...]


def total(ref, e, m):
    return (ref[0, e, m] + ref[1, e, m]) + (ref[2, e, m] + ref[3, e, m])


def polynomial(tab, step, cur, square):
    return jnp.where(tab[BRANCH + step] == 1, 2.0 * cur - square, square)


def close_kernel(step, cuts, tab, part_ref, cur_ref, *refs):
    w = BAND + step
    low = low_half()
    i0 = tab[PLACE + 5] * 4
    for e in range(4):
        i = i0 + e
        turned = [swap_halves(cur_ref[e, t]) for t in range(w + 1)]
        zero = jnp.zeros((8, 128), F32)
        for m in range(w + 2):
            before = turned[m - 1] if m >= 1 else zero
            after = turned[m] if m <= w else zero
            cur = jnp.where(low, before, after)
            square = total(part_ref, e, m)
            one = bit(tab, step + 1, i, (i + 2 * m + 63 - w) & 63)
            two = 0
            if 2 * m + 1 <= 2 * w + 2:
                two = bit(tab, step + 1, i, (i + 2 * m + 64 - w) & 63)
            keep = jnp.where(low, one, two) == 1
            value = jnp.where(keep, polynomial(tab, step, cur, square), 0.0)
            for ref, (lo, hi, first, last) in zip(refs, cuts):
                if lo <= e < hi and first <= m < last:
                    ref[e - lo, m - first] = value


def finish_kernel(tab, part_ref, cur_ref, y_ref):
    w = BAND + STEPS - 1
    low = low_half()
    row0 = tab[PLACE] * 4
    y_ref[...] = jnp.zeros_like(y_ref)
    for e in range(4):
        i = tab[PERM + row0 + e]
        for m in range(w + 2):
            cur = cur_ref[e, m - 1] if 1 <= m <= w + 1 else jnp.zeros((8, 128), F32)
            square = total(part_ref, e, m)
            value = polynomial(tab, STEPS - 1, cur, square)
            turned = swap_halves(value)
            for half in (0, 1):
                v = 2 * m + half
                if v == 0:
                    continue
                j = (i + v + 64 - (w + 2)) & 63
                sj = tab[INV + j]
                odd = sj & 1
                piece = jnp.where(odd == half, value, turned)
                piece = jnp.where(bit(tab, STEPS, i, j) == 1, piece, 0.0)
                side = jnp.where(low, 0, 1) == odd
                c, t = sj >> 3, (sj & 7) >> 1
                y_ref[c, e, t] = jnp.where(side, piece, y_ref[c, e, t])


def join_kernel(y_ref, out_ref):
    for c in range(8):
        for e in range(4):
            for t in range(4):
                out_ref[e * 64 + c * 8 : e * 64 + c * 8 + 8, t * 128 : (t + 1) * 128] = y_ref[c, e, t]


def tables(masks, branch, perm):
    r = lax.axis_index("row")
    z = lax.axis_index("col")
    h = lax.axis_index("layer")
    ids = jnp.arange(64, dtype=jnp.int32)
    inverse = jnp.sum(jnp.where(perm[:, None] == ids[None, :], ids[:, None], 0), axis=0)
    shifts = jnp.arange(32, dtype=jnp.int32)
    bits = jnp.sum(masks.reshape(6, 64, 2, 32) << shifts, axis=-1, dtype=jnp.int32)
    pos = jnp.sum(jnp.where(jnp.asarray(RING) == r, jnp.arange(16), 0))
    place = jnp.stack([r, z * 2 + h, r // 4, r % 4, h, pos, z, z]).astype(jnp.int32)
    return jnp.concatenate(
        [perm, inverse.astype(jnp.int32), branch, jnp.zeros((3,), jnp.int32), bits.reshape(-1), place]
    )


def reduce_group(own, oth):
    (pair,) = call(pair_kernel, [own.shape], [own, core_swap(oth)])
    return exchange(pair, "col")


def group_swap(value, k):
    return permute(value, GROUP, [(i, i ^ k) for i in range(8)])


def shards(density, masks, branch, perm):
    split = call(split_kernel, [(4, 4, 8, 128)] * 8, [density])
    split = [split[0]] + [group_swap(split[k], k) for k in range(1, 8)]
    tab = tables(masks, branch, perm)
    (rows,) = call(
        compact_kernel,
        [(4, BAND + 1, 8, 128)],
        split,
        [pltpu.VMEM((8, 4, 4, 8, 128), F32)],
        tab=tab,
    )
    gathered = gather_rows(rows)
    for step in range(STEPS - 1):
        w = BAND + step
        left, count = geometry(w)
        rows = (4 + 2 * w) * 8
        part = (4, 4, w + 2, 8, 128)
        scratch = [
            pltpu.VMEM((rows, count * 128), BF16),
            pltpu.VMEM((rows, count * 128), BF16),
            pltpu.VMEM((32, 8, count * 128), F32),
        ]
        if step == 0:
            strips = 4 + 2 * w
            scratch += [pltpu.VMEM((strips, w + 1, 8, 128), F32), pltpu.SemaphoreType.DMA((strips,))]
            own, oth, cur = call(
                first_step_kernel,
                [part, part, (4, w + 1, 8, 128)],
                [gathered],
                scratch,
                tab=tab,
                here=(0,),
            )
        else:
            kernel = lambda *refs, w=w, pieces=pieces: step_kernel(w, pieces, *refs)
            own, oth = call(kernel, [part, part], [cur] + around, scratch, tab=tab)
        parts = reduce_group(own, oth)
        pieces = halo_pieces(w + 1) if step < STEPS - 2 else []
        cuts = [(0, 4, 0, w + 2)]
        for _, cut in pieces:
            if cut not in cuts:
                cuts.append(cut)
        kernel = lambda *refs, step=step, cuts=cuts: close_kernel(step, cuts, *refs)
        shapes = [(hi - lo, last - first, 8, 128) for lo, hi, first, last in cuts]
        sent = call(kernel, shapes, [parts, cur], tab=tab)
        cur = sent[0]
        around = [ring_shift(sent[cuts.index(cut)], d) for d, cut in pieces]
    gathered = gather_rows(cur)
    w = BAND + STEPS - 1
    part = (4, 4, w + 2, 8, 128)
    scratch = [
        pltpu.VMEM(((2 * w + 2) * 8, (w + 2) * 128), BF16),
        pltpu.VMEM(((2 * w + 2) * 8, (w + 2) * 128), BF16),
        pltpu.VMEM((8, 8, (w + 2) * 128), F32),
    ]
    own, oth, cur = call(
        last_step_kernel, [part, part, (4, w + 1, 8, 128)], [gathered], scratch, tab=tab
    )
    parts = reduce_group(own, oth)
    (full,) = call(finish_kernel, [(8, 4, 4, 8, 128)], [parts, cur], tab=tab)
    full = exchange(full, GROUP)
    (out,) = call(join_kernel, [(256, 512)], [full])
    return out


def solution(mesh):
    return jax.shard_map(
        shards,
        mesh=mesh,
        in_specs=(P("row", GROUP), P(), P(), P()),
        out_specs=P("row", GROUP),
        check_vma=False,
    )
```

```python
import jax
import jax.numpy as jnp
from jax import lax
from jax.experimental import pallas as pl
from jax.experimental.pallas import tpu as pltpu
from jax.sharding import PartitionSpec as P

STEPS = 5
BAND = 6
NB = 64
GROUP = ("col", "layer")
PERM, INV, BRANCH, BITS, PLACE = 0, 64, 128, 136, 136 + 6 * 128
F32, BF16 = jnp.float32, jnp.bfloat16


def ring_xy(pos):
    a, b = pos // 2, pos % 2
    return (a, b) if a < 4 else (7 - a, 3 - b)


RING = [ring_xy(p)[0] * 4 + ring_xy(p)[1] for p in range(16)]


def permute(value, axes, pairs):
    flat = value.reshape(-1, 128)
    return lax.ppermute(flat, axes, pairs).reshape(value.shape)


def ring_shift(value, k):
    return permute(value, "row", [(RING[p], RING[(p + k) % 16]) for p in range(16)])


def xy_shift(value, dx, dy):
    return permute(
        value, "row", [(i, ((i // 4 + dx) % 4) * 4 + (i % 4 + dy) % 4) for i in range(16)]
    )


def z_swap(value, k):
    return permute(value, "col", [(i, i ^ k) for i in range(4)])


def core_swap(value):
    return permute(value, "layer", [(0, 1), (1, 0)])


def low_half():
    return lax.broadcasted_iota(jnp.int32, (8, 128), 1) < 64


def swap_halves(tile):
    return pltpu.roll(tile, 64, 1)


def bit(tab, s, i, j):
    word = tab[BITS + s * 128 + i * 2 + lax.shift_right_logical(j, 5)]
    return lax.shift_right_logical(word, j & 31) & 1


def shifted(tiles, d, count):
    n = len(tiles)
    get = lambda seq, t: seq[t] if 0 <= t < n else None
    if d % 2 == 0:
        return [get(tiles, m - d // 2) for m in range(count)]
    q = (d - 1) // 2
    low = low_half()
    turned = [swap_halves(t) for t in tiles]
    out = []
    for m in range(count):
        a, b = get(turned, m - q - 1), get(turned, m - q)
        if a is None and b is None:
            out.append(None)
        else:
            zero = jnp.zeros((8, 128), F32)
            out.append(jnp.where(low, zero if a is None else a, zero if b is None else b))
    return out


def store_split(hi_ref, lo_ref, row, first, second):
    zero = jnp.zeros((8, 128), F32)
    for m, (a, b) in enumerate(zip(first, second)):
        both = jnp.concatenate([zero if a is None else a, zero if b is None else b], axis=0)
        hi = both.astype(BF16)
        hi_ref[row : row + 16, m * 128 : (m + 1) * 128] = hi
        lo_ref[row : row + 16, m * 128 : (m + 1) * 128] = (both - hi.astype(F32)).astype(BF16)


def tdot(a, b):
    return lax.dot_general(a, b, (((0,), (0,)), ((), ())), preferred_element_type=F32)


def product(hi_ref, lo_ref, start, width):
    xh = hi_ref[:, start : start + width]
    xl = lo_ref[:, start : start + width]
    zh = hi_ref[...]
    return tdot(xh, zh) + tdot(xh, lo_ref[...]) + tdot(xl, zh)


def call(kernel, outs, args, scratch=(), tab=None):
    vmem = pl.BlockSpec(memory_space=pltpu.VMEM)
    table = [] if tab is None else [pl.BlockSpec(memory_space=pltpu.SMEM)]
    return pl.pallas_call(
        kernel,
        out_shape=[jax.ShapeDtypeStruct(o, F32) for o in outs],
        in_specs=table + [vmem] * len(args),
        out_specs=[vmem] * len(outs),
        scratch_shapes=list(scratch),
        compiler_params=pltpu.CompilerParams(vmem_limit_bytes=48 * 1024 * 1024),
    )(*([] if tab is None else [tab]), *args)


def split_kernel(d_ref, own_ref, oth_ref):
    z, h = lax.axis_index("col"), lax.axis_index("layer")
    for k in range(4):
        for ref, core in ((own_ref, h), (oth_ref, 1 - h)):
            for e in range(4):
                start = pl.multiple_of(e * 64 + (2 * (z ^ k) + core) * 8, 8)
                rows = d_ref[pl.ds(start, 8), :]
                for t in range(4):
                    ref[k, e, t] = rows[:, t * 128 : (t + 1) * 128]


def pack_kernel(own_ref, got_ref, *outs):
    for k in range(4):
        outs[k][0] = own_ref[k]
        outs[k][1] = got_ref[k]


def compact_kernel(tab, *refs):
    ins, (a_ref, b_ref, x_ref) = refs[:4], refs[4:]
    for k in range(4):
        x_ref[k] = ins[k][...]
    low = low_half()
    row0 = tab[PLACE] * 4
    z, h = tab[PLACE + 6], tab[PLACE + 4]
    for e in range(4):
        i = tab[PERM + row0 + e]
        out_ref = a_ref if e < 2 else b_ref
        halves = []
        for t in range(2 * BAND + 2):
            if t > 2 * BAND:
                halves.append(jnp.zeros((8, 128), F32))
                continue
            j = (i + t - BAND) & 63
            sj = tab[INV + j]
            tile = x_ref[(sj >> 4) ^ z, ((sj >> 3) & 1) ^ h, e, (sj & 7) >> 1]
            tile = jnp.where((sj & 1) == (t & 1), tile, swap_halves(tile))
            halves.append(jnp.where(bit(tab, 0, i, j) == 1, tile, 0.0))
        for t in range(BAND + 1):
            out_ref[e % 2, t] = jnp.where(low, halves[2 * t], halves[2 * t + 1])


def gather_rows(half_a, half_b):
    near_a = [xy_shift(half_a, k, 0) for k in (1, 3, 2)]
    near_b = [xy_shift(half_b, 0, k) for k in (1, 3, 2)]
    half_a, half_b, *near = lax.optimization_barrier((half_a, half_b, *near_a, *near_b))
    a = jnp.stack([half_a, near[0], near[2], near[1]])
    b = jnp.stack([half_b, near[3], near[5], near[4]])
    a, b = lax.optimization_barrier((a, b))
    far_a = [xy_shift(a, 0, k) for k in (1, 3, 2)]
    far_b = [xy_shift(b, k, 0) for k in (1, 3, 2)]
    return [a, far_a[0], far_a[2], far_a[1], b, far_b[0], far_b[2], far_b[1]]


def collect(ins, g_ref):
    for n in range(8):
        g_ref[n] = ins[n][...]


def seat(tab, r, e):
    dx = (tab[PLACE + 2] - (r >> 2)) & 3
    dy = (tab[PLACE + 3] - (r & 3)) & 3
    first = e < 2
    return jnp.where(first, dy, 4 + dx), jnp.where(first, dx, dy), e & 1


def write_slabs(tab, p_ref, own_ref, oth_ref, e, base, d, tiles):
    z, h = tab[PLACE + 6], tab[PLACE + 4]
    low = low_half()
    for zz in range(4):
        for ref, core in ((own_ref, h), (oth_ref, 1 - h)):
            rows = p_ref[base + 2 * (z ^ zz) + core]
            if d % 2 == 0:
                for m in range(tiles):
                    at = (d // 2 + m) * 128
                    ref[zz, e, m] = rows[:, at : at + 128]
            else:
                q = d // 2
                turned = []
                for m in range(tiles + 1):
                    at = (q + m) * 128
                    if at < rows.shape[1]:
                        turned.append(swap_halves(rows[:, at : at + 128]))
                    else:
                        turned.append(jnp.zeros((8, 128), F32))
                for m in range(tiles):
                    ref[zz, e, m] = jnp.where(low, turned[m], turned[m + 1])


def geometry(w):
    left = w + 1 + (w + 1) % 2
    return left, (left + 4 + w + 1 + 1) // 2


def step_body(tab, strips, w, own_ref, oth_ref, hi_ref, lo_ref, p_ref):
    left, count = geometry(w)
    nk = 4 + 2 * w
    for a in range(0, nk, 2):
        pair = []
        for b in (a, a + 1):
            tiles, first = strips(b)
            pair.append(shifted(tiles, left - 2 * w + b + 2 * first, count))
        store_split(hi_ref, lo_ref, a * 8, pair[0], pair[1])
    p_ref[...] = product(hi_ref, lo_ref, left * 64, 256).reshape(32, 8, count * 128)
    for e in range(4):
        write_slabs(tab, p_ref, own_ref, oth_ref, e, e * 8, left - (w + 1) + e, w + 2)


def first_step_kernel(tab, *refs):
    ins, (own_ref, oth_ref, cur_ref, hi_ref, lo_ref, p_ref, g_ref) = refs[:8], refs[8:]
    collect(ins, g_ref)
    w = BAND
    base = tab[PLACE + 5] * 4 + 64 - w

    def strips(b):
        sk = tab[INV + ((base + b) & 63)]
        u, v, e = seat(tab, sk >> 2, sk & 3)
        strip = g_ref[u, v, e]
        if w <= b < w + 4:
            cur_ref[b - w] = strip
        return [strip[t] for t in range(w + 1)], 0

    step_body(tab, strips, w, own_ref, oth_ref, hi_ref, lo_ref, p_ref)


def step_kernel(w, pieces, tab, *refs):
    n = 1 + len(pieces)
    ins, (own_ref, oth_ref, hi_ref, lo_ref, p_ref) = refs[:n], refs[n:]

    def strips(b):
        off = b - w
        if 0 <= off < 4:
            return [ins[0][off, t] for t in range(w + 1)], 0
        d = (-off + 3) // 4 if off < 0 else -(off // 4)
        at = [piece[0] for piece in pieces].index(d)
        _, (lo, hi, first, last) = pieces[at]
        row = off + 4 * d - lo
        return [ins[1 + at][row, t] for t in range(last - first)], first

    step_body(tab, strips, w, own_ref, oth_ref, hi_ref, lo_ref, p_ref)


def halo_pieces(w):
    out = []
    for d in range(1, (w + 3) // 4 + 1):
        n = min(4, w - 4 * (d - 1))
        out.append((d, (4 - n, 4, 2 * (d - 1), w + 1)))
        out.append((-d, (0, n, 0, w + 1 - 2 * (d - 1))))
    return out


def last_step_kernel(tab, *refs):
    ins, (own_ref, oth_ref, cur_ref, hi_ref, lo_ref, p_ref, g_ref) = refs[:8], refs[8:]
    collect(ins, g_ref)
    w = BAND + STEPS - 1
    row0 = tab[PLACE] * 4
    left, count = w + 2, w + 2
    for e in range(4):
        i = tab[PERM + row0 + e]

        def strips(b):
            k = (i + b - w) & 63
            pos = k >> 2
            a, odd = pos >> 1, pos & 1
            r = jnp.where(a < 4, a * 4 + odd, (7 - a) * 4 + 3 - odd)
            u, v, ee = seat(tab, r, k & 3)
            strip = g_ref[u, v, ee]
            if b == w:
                cur_ref[e] = strip
            return [strip[t] for t in range(w + 1)]

        for a in range(0, 2 * w + 2, 2):
            one = shifted(strips(a), left - 2 * w + a, count)
            two = [None] * count
            if a + 1 <= 2 * w:
                two = shifted(strips(a + 1), left - 2 * w + a + 1, count)
            store_split(hi_ref, lo_ref, a * 8, one, two)
        p_ref[...] = product(hi_ref, lo_ref, left * 64, 64).reshape(8, 8, count * 128)
        write_slabs(tab, p_ref, own_ref, oth_ref, e, 0, 0, count)


def pair_kernel(own_ref, got_ref, *outs):
    for k in range(4):
        outs[k][...] = own_ref[k] + got_ref[k]


def total(parts, e, m):
    return (parts[0][e, m] + parts[1][e, m]) + (parts[2][e, m] + parts[3][e, m])


def polynomial(tab, step, cur, square):
    return jnp.where(tab[BRANCH + step] == 1, 2.0 * cur - square, square)


def close_kernel(step, cuts, tab, p0, p1, p2, p3, cur_ref, *refs):
    w = BAND + step
    low = low_half()
    i0 = tab[PLACE + 5] * 4
    for e in range(4):
        i = i0 + e
        turned = [swap_halves(cur_ref[e, t]) for t in range(w + 1)]
        zero = jnp.zeros((8, 128), F32)
        for m in range(w + 2):
            before = turned[m - 1] if m >= 1 else zero
            after = turned[m] if m <= w else zero
            cur = jnp.where(low, before, after)
            square = total((p0, p1, p2, p3), e, m)
            one = bit(tab, step + 1, i, (i + 2 * m + 63 - w) & 63)
            two = 0
            if 2 * m + 1 <= 2 * w + 2:
                two = bit(tab, step + 1, i, (i + 2 * m + 64 - w) & 63)
            keep = jnp.where(low, one, two) == 1
            value = jnp.where(keep, polynomial(tab, step, cur, square), 0.0)
            for ref, (lo, hi, first, last) in zip(refs, cuts):
                if lo <= e < hi and first <= m < last:
                    ref[e - lo, m - first] = value


def finish_kernel(tab, p0, p1, p2, p3, cur_ref, own_ref, oth_ref, y_ref):
    w = BAND + STEPS - 1
    low = low_half()
    row0 = tab[PLACE] * 4
    z, h = tab[PLACE + 6], tab[PLACE + 4]
    y_ref[...] = jnp.zeros_like(y_ref)
    for e in range(4):
        i = tab[PERM + row0 + e]
        for m in range(w + 2):
            cur = cur_ref[e, m - 1] if 1 <= m <= w + 1 else jnp.zeros((8, 128), F32)
            square = total((p0, p1, p2, p3), e, m)
            value = polynomial(tab, STEPS - 1, cur, square)
            turned = swap_halves(value)
            for half in (0, 1):
                v = 2 * m + half
                if v == 0:
                    continue
                j = (i + v + 64 - (w + 2)) & 63
                sj = tab[INV + j]
                odd = sj & 1
                piece = jnp.where(odd == half, value, turned)
                piece = jnp.where(bit(tab, STEPS, i, j) == 1, piece, 0.0)
                side = jnp.where(low, 0, 1) == odd
                at = ((sj >> 3) & 1) ^ h, (sj >> 4) ^ z, e, (sj & 7) >> 1
                y_ref[at] = jnp.where(side, piece, y_ref[at])
    own_ref[...] = y_ref[0]
    oth_ref[...] = y_ref[1]


def join_kernel(y0, y1, y2, y3, out_ref):
    z, h = lax.axis_index("col"), lax.axis_index("layer")
    for k, y_ref in enumerate((y0, y1, y2, y3)):
        for core in (0, 1):
            for e in range(4):
                start = pl.multiple_of(e * 64 + (2 * (z ^ k) + (core ^ h)) * 8, 8)
                for t in range(4):
                    out_ref[pl.ds(start, 8), t * 128 : (t + 1) * 128] = y_ref[core, e, t]


def tables(masks, branch, perm):
    r = lax.axis_index("row")
    z = lax.axis_index("col")
    h = lax.axis_index("layer")
    ids = jnp.arange(64, dtype=jnp.int32)
    inverse = jnp.sum(jnp.where(perm[:, None] == ids[None, :], ids[:, None], 0), axis=0)
    shifts = jnp.arange(32, dtype=jnp.int32)
    bits = jnp.sum(masks.reshape(6, 64, 2, 32) << shifts, axis=-1, dtype=jnp.int32)
    pos = jnp.sum(jnp.where(jnp.asarray(RING) == r, jnp.arange(16), 0))
    place = jnp.stack([r, z * 2 + h, r // 4, r % 4, h, pos, z, z]).astype(jnp.int32)
    return jnp.concatenate(
        [perm, inverse.astype(jnp.int32), branch, jnp.zeros((3,), jnp.int32), bits.reshape(-1), place]
    )


def z_exchange(parts):
    return [parts[0]] + [z_swap(parts[k], k) for k in (1, 2, 3)]


def reduce_group(own, oth):
    return z_exchange(call(pair_kernel, [own.shape[1:]] * 4, [own, core_swap(oth)]))


def spread_group(own, oth):
    shape = (2,) + own.shape[1:]
    return z_exchange(call(pack_kernel, [shape] * 4, [own, core_swap(oth)]))


def shards(density, masks, branch, perm):
    slabs = (4, 4, 4, 8, 128)
    split = spread_group(*call(split_kernel, [slabs] * 2, [density]))
    tab = tables(masks, branch, perm)
    halves = call(
        compact_kernel,
        [(2, BAND + 1, 8, 128)] * 2,
        split,
        [pltpu.VMEM((4, 2, 4, 4, 8, 128), F32)],
        tab=tab,
    )
    gathered = gather_rows(*halves)
    for step in range(STEPS - 1):
        w = BAND + step
        left, count = geometry(w)
        rows = (4 + 2 * w) * 8
        part = (4, 4, w + 2, 8, 128)
        scratch = [
            pltpu.VMEM((rows, count * 128), BF16),
            pltpu.VMEM((rows, count * 128), BF16),
            pltpu.VMEM((32, 8, count * 128), F32),
        ]
        if step == 0:
            scratch.append(pltpu.VMEM((8, 4, 2, w + 1, 8, 128), F32))
            own, oth, cur = call(
                first_step_kernel, [part, part, (4, w + 1, 8, 128)], gathered, scratch, tab=tab
            )
        else:
            kernel = lambda *refs, w=w, pieces=pieces: step_kernel(w, pieces, *refs)
            own, oth = call(kernel, [part, part], [cur] + around, scratch, tab=tab)
        parts = reduce_group(own, oth)
        pieces = halo_pieces(w + 1) if step < STEPS - 2 else []
        cuts = [(0, 4, 0, w + 2)] if pieces else [(0, 2, 0, w + 2), (2, 4, 0, w + 2)]
        for _, cut in pieces:
            if cut not in cuts:
                cuts.append(cut)
        kernel = lambda *refs, step=step, cuts=cuts: close_kernel(step, cuts, *refs)
        shapes = [(hi - lo, last - first, 8, 128) for lo, hi, first, last in cuts]
        sent = call(kernel, shapes, parts + [cur], tab=tab)
        cur = sent[0]
        around = [ring_shift(sent[cuts.index(cut)], d) for d, cut in pieces]
        cur, *around = lax.optimization_barrier((cur, *around))
    gathered = gather_rows(*sent)
    w = BAND + STEPS - 1
    part = (4, 4, w + 2, 8, 128)
    scratch = [
        pltpu.VMEM(((2 * w + 2) * 8, (w + 2) * 128), BF16),
        pltpu.VMEM(((2 * w + 2) * 8, (w + 2) * 128), BF16),
        pltpu.VMEM((8, 8, (w + 2) * 128), F32),
        pltpu.VMEM((8, 4, 2, w + 1, 8, 128), F32),
    ]
    own, oth, cur = call(
        last_step_kernel, [part, part, (4, w + 1, 8, 128)], gathered, scratch, tab=tab
    )
    parts = reduce_group(own, oth)
    own, oth = call(
        finish_kernel, [slabs] * 2, parts + [cur], [pltpu.VMEM((2,) + slabs, F32)], tab=tab
    )
    (out,) = call(join_kernel, [(256, 512)], spread_group(own, oth))
    return out


def solution(mesh):
    return jax.shard_map(
        shards,
        mesh=mesh,
        in_specs=(P("row", GROUP), P(), P(), P()),
        out_specs=P("row", GROUP),
        check_vma=False,
    )
```

```python
import jax
import jax.numpy as jnp
from jax import lax
from jax.experimental import pallas as pl
from jax.experimental.pallas import tpu as pltpu
from jax.sharding import PartitionSpec as P

STEPS = 5
BAND = 6
NB = 64
GROUP = ("col", "layer")
PERM, INV, BRANCH, BITS, PLACE = 0, 64, 128, 136, 136 + 6 * 128
F32, BF16 = jnp.float32, jnp.bfloat16


def ring_xy(pos):
    a, b = pos // 2, pos % 2
    return (a, b) if a < 4 else (7 - a, 3 - b)


RING = [ring_xy(p)[0] * 4 + ring_xy(p)[1] for p in range(16)]


def permute(value, axes, pairs):
    flat = value.reshape(-1, 128)
    return lax.ppermute(flat, axes, pairs).reshape(value.shape)


def ring_shift(value, k):
    return permute(value, "row", [(RING[p], RING[(p + k) % 16]) for p in range(16)])


def xy_shift(value, dx, dy):
    return permute(
        value, "row", [(i, ((i // 4 + dx) % 4) * 4 + (i % 4 + dy) % 4) for i in range(16)]
    )


def z_swap(value, k):
    return permute(value, "col", [(i, i ^ k) for i in range(4)])


def core_swap(value):
    return permute(value, "layer", [(0, 1), (1, 0)])


def low_half():
    return lax.broadcasted_iota(jnp.int32, (8, 128), 1) < 64


def swap_halves(tile):
    return pltpu.roll(tile, 64, 1)


def bit(tab, s, i, j):
    word = tab[BITS + s * 128 + i * 2 + lax.shift_right_logical(j, 5)]
    return lax.shift_right_logical(word, j & 31) & 1


def shifted(tiles, d, count):
    n = len(tiles)
    get = lambda seq, t: seq[t] if 0 <= t < n else None
    if d % 2 == 0:
        return [get(tiles, m - d // 2) for m in range(count)]
    q = (d - 1) // 2
    low = low_half()
    turned = [swap_halves(t) for t in tiles]
    out = []
    for m in range(count):
        a, b = get(turned, m - q - 1), get(turned, m - q)
        if a is None and b is None:
            out.append(None)
        else:
            zero = jnp.zeros((8, 128), F32)
            out.append(jnp.where(low, zero if a is None else a, zero if b is None else b))
    return out


def store_split(hi_ref, lo_ref, row, first, second):
    zero = jnp.zeros((8, 128), F32)
    for m, (a, b) in enumerate(zip(first, second)):
        both = jnp.concatenate([zero if a is None else a, zero if b is None else b], axis=0)
        hi = both.astype(BF16)
        hi_ref[row : row + 16, m * 128 : (m + 1) * 128] = hi
        lo_ref[row : row + 16, m * 128 : (m + 1) * 128] = (both - hi.astype(F32)).astype(BF16)


def tdot(a, b):
    return lax.dot_general(a, b, (((0,), (0,)), ((), ())), preferred_element_type=F32)


def product(hi_ref, lo_ref, start, width):
    xh = hi_ref[:, start : start + width]
    xl = lo_ref[:, start : start + width]
    zh = hi_ref[...]
    return tdot(xh, zh) + tdot(xh, lo_ref[...]) + tdot(xl, zh)


def call(kernel, outs, args, scratch=(), tab=None):
    vmem = pl.BlockSpec(memory_space=pltpu.VMEM)
    table = [] if tab is None else [pl.BlockSpec(memory_space=pltpu.SMEM)]
    return pl.pallas_call(
        kernel,
        out_shape=[jax.ShapeDtypeStruct(o, F32) for o in outs],
        in_specs=table + [vmem] * len(args),
        out_specs=[vmem] * len(outs),
        scratch_shapes=list(scratch),
        compiler_params=pltpu.CompilerParams(vmem_limit_bytes=48 * 1024 * 1024),
    )(*([] if tab is None else [tab]), *args)


def split_kernel(d_ref, own_ref, oth_ref):
    z, h = lax.axis_index("col"), lax.axis_index("layer")
    for k in range(4):
        for ref, core in ((own_ref, h), (oth_ref, 1 - h)):
            for e in range(4):
                start = pl.multiple_of(e * 64 + (2 * (z ^ k) + core) * 8, 8)
                rows = d_ref[pl.ds(start, 8), :]
                for t in range(4):
                    ref[k, e, t] = rows[:, t * 128 : (t + 1) * 128]


def pack_kernel(own_ref, got_ref, *outs):
    for k in range(4):
        outs[k][0] = own_ref[k]
        outs[k][1] = got_ref[k]


def compact_kernel(tab, *refs):
    ins, (a_ref, b_ref, x_ref) = refs[:4], refs[4:]
    for k in range(4):
        x_ref[k] = ins[k][...]
    low = low_half()
    row0 = tab[PLACE] * 4
    z, h = tab[PLACE + 6], tab[PLACE + 4]
    for e in range(4):
        i = tab[PERM + row0 + e]
        out_ref = a_ref if e < 2 else b_ref
        halves = []
        for t in range(2 * BAND + 2):
            if t > 2 * BAND:
                halves.append(jnp.zeros((8, 128), F32))
                continue
            j = (i + t - BAND) & 63
            sj = tab[INV + j]
            tile = x_ref[(sj >> 4) ^ z, ((sj >> 3) & 1) ^ h, e, (sj & 7) >> 1]
            tile = jnp.where((sj & 1) == (t & 1), tile, swap_halves(tile))
            halves.append(jnp.where(bit(tab, 0, i, j) == 1, tile, 0.0))
        for t in range(BAND + 1):
            out_ref[e % 2, t] = jnp.where(low, halves[2 * t], halves[2 * t + 1])


LINES = [[x * 4 + y for x in range(4)] for y in range(4)]


def gather_x(value):
    flat = value.reshape(-1, 128)
    out = lax.all_gather(flat, "row", axis=0, tiled=True, axis_index_groups=LINES)
    return out.reshape((4,) + value.shape)


def gather_rows(half_a, half_b, small):
    near_b = [xy_shift(half_b, 0, k) for k in (1, 3, 2)]
    a = gather_x(half_a)
    a, half_b, *near = lax.optimization_barrier((a, half_b, *near_b))
    b = jnp.stack([half_b, near[0], near[2], near[1]])
    a, b = lax.optimization_barrier((a, b))
    far_a = [xy_shift(a, 0, k) for k in (1, 3, 2)]
    far_a = [a, far_a[0], far_a[2], far_a[1]]
    if small:
        return far_a + [gather_x(b)]
    far_b = [xy_shift(b, k, 0) for k in (1, 3, 2)]
    return far_a + [b, far_b[0], far_b[2], far_b[1]]


def collect(ins, g_ref):
    for n in range(4):
        g_ref[n] = ins[n][...]
    if len(ins) == 5:
        g_ref[4:8] = ins[4][...]
    else:
        for n in range(4, 8):
            g_ref[n] = ins[n][...]


def seat(tab, r, e, small):
    x = r >> 2
    dx = x if small else (tab[PLACE + 2] - x) & 3
    dy = (tab[PLACE + 3] - (r & 3)) & 3
    first = e < 2
    return jnp.where(first, dy, 4 + dx), jnp.where(first, x, dy), e & 1


def write_slabs(tab, p_ref, own_ref, oth_ref, e, base, d, tiles):
    z, h = tab[PLACE + 6], tab[PLACE + 4]
    low = low_half()
    for zz in range(4):
        for ref, core in ((own_ref, h), (oth_ref, 1 - h)):
            rows = p_ref[base + 2 * (z ^ zz) + core]
            if d % 2 == 0:
                for m in range(tiles):
                    at = (d // 2 + m) * 128
                    ref[zz, e, m] = rows[:, at : at + 128]
            else:
                q = d // 2
                turned = []
                for m in range(tiles + 1):
                    at = (q + m) * 128
                    if at < rows.shape[1]:
                        turned.append(swap_halves(rows[:, at : at + 128]))
                    else:
                        turned.append(jnp.zeros((8, 128), F32))
                for m in range(tiles):
                    ref[zz, e, m] = jnp.where(low, turned[m], turned[m + 1])


def geometry(w):
    left = w + 1 + (w + 1) % 2
    return left, (left + 4 + w + 1 + 1) // 2


def step_body(tab, strips, w, own_ref, oth_ref, hi_ref, lo_ref, p_ref):
    left, count = geometry(w)
    nk = 4 + 2 * w
    for a in range(0, nk, 2):
        pair = []
        for b in (a, a + 1):
            tiles, first = strips(b)
            pair.append(shifted(tiles, left - 2 * w + b + 2 * first, count))
        store_split(hi_ref, lo_ref, a * 8, pair[0], pair[1])
    p_ref[...] = product(hi_ref, lo_ref, left * 64, 256).reshape(32, 8, count * 128)
    for e in range(4):
        write_slabs(tab, p_ref, own_ref, oth_ref, e, e * 8, left - (w + 1) + e, w + 2)


def first_step_kernel(tab, *refs):
    ins, (own_ref, oth_ref, cur_ref, hi_ref, lo_ref, p_ref, g_ref) = refs[:5], refs[5:]
    collect(ins, g_ref)
    w = BAND
    base = tab[PLACE + 5] * 4 + 64 - w

    def strips(b):
        sk = tab[INV + ((base + b) & 63)]
        u, v, e = seat(tab, sk >> 2, sk & 3, True)
        strip = g_ref[u, v, e]
        if w <= b < w + 4:
            cur_ref[b - w] = strip
        return [strip[t] for t in range(w + 1)], 0

    step_body(tab, strips, w, own_ref, oth_ref, hi_ref, lo_ref, p_ref)


def step_kernel(w, pieces, tab, *refs):
    n = 1 + len(pieces)
    ins, (own_ref, oth_ref, hi_ref, lo_ref, p_ref) = refs[:n], refs[n:]

    def strips(b):
        off = b - w
        if 0 <= off < 4:
            return [ins[0][off, t] for t in range(w + 1)], 0
        d = (-off + 3) // 4 if off < 0 else -(off // 4)
        at = [piece[0] for piece in pieces].index(d)
        _, (lo, hi, first, last) = pieces[at]
        row = off + 4 * d - lo
        return [ins[1 + at][row, t] for t in range(last - first)], first

    step_body(tab, strips, w, own_ref, oth_ref, hi_ref, lo_ref, p_ref)


def halo_pieces(w):
    out = []
    for d in range(1, (w + 3) // 4 + 1):
        n = min(4, w - 4 * (d - 1))
        out.append((d, (4 - n, 4, 2 * (d - 1), w + 1)))
        out.append((-d, (0, n, 0, w + 1 - 2 * (d - 1))))
    return out


def last_step_kernel(tab, *refs):
    ins, (own_ref, oth_ref, cur_ref, hi_ref, lo_ref, p_ref, g_ref) = refs[:8], refs[8:]
    collect(ins, g_ref)
    w = BAND + STEPS - 1
    row0 = tab[PLACE] * 4
    left, count = w + 2, w + 2
    for e in range(4):
        i = tab[PERM + row0 + e]

        def strips(b):
            k = (i + b - w) & 63
            pos = k >> 2
            a, odd = pos >> 1, pos & 1
            r = jnp.where(a < 4, a * 4 + odd, (7 - a) * 4 + 3 - odd)
            u, v, ee = seat(tab, r, k & 3, False)
            strip = g_ref[u, v, ee]
            if b == w:
                cur_ref[e] = strip
            return [strip[t] for t in range(w + 1)]

        for a in range(0, 2 * w + 2, 2):
            one = shifted(strips(a), left - 2 * w + a, count)
            two = [None] * count
            if a + 1 <= 2 * w:
                two = shifted(strips(a + 1), left - 2 * w + a + 1, count)
            store_split(hi_ref, lo_ref, a * 8, one, two)
        p_ref[...] = product(hi_ref, lo_ref, left * 64, 64).reshape(8, 8, count * 128)
        write_slabs(tab, p_ref, own_ref, oth_ref, e, 0, 0, count)


def pair_kernel(own_ref, got_ref, *outs):
    for k in range(4):
        outs[k][...] = own_ref[k] + got_ref[k]


def total(parts, e, m):
    return (parts[0][e, m] + parts[1][e, m]) + (parts[2][e, m] + parts[3][e, m])


def polynomial(tab, step, cur, square):
    return jnp.where(tab[BRANCH + step] == 1, 2.0 * cur - square, square)


def close_kernel(step, cuts, tab, p0, p1, p2, p3, cur_ref, *refs):
    w = BAND + step
    low = low_half()
    i0 = tab[PLACE + 5] * 4
    for e in range(4):
        i = i0 + e
        turned = [swap_halves(cur_ref[e, t]) for t in range(w + 1)]
        zero = jnp.zeros((8, 128), F32)
        for m in range(w + 2):
            before = turned[m - 1] if m >= 1 else zero
            after = turned[m] if m <= w else zero
            cur = jnp.where(low, before, after)
            square = total((p0, p1, p2, p3), e, m)
            one = bit(tab, step + 1, i, (i + 2 * m + 63 - w) & 63)
            two = 0
            if 2 * m + 1 <= 2 * w + 2:
                two = bit(tab, step + 1, i, (i + 2 * m + 64 - w) & 63)
            keep = jnp.where(low, one, two) == 1
            value = jnp.where(keep, polynomial(tab, step, cur, square), 0.0)
            for ref, (lo, hi, first, last) in zip(refs, cuts):
                if lo <= e < hi and first <= m < last:
                    ref[e - lo, m - first] = value


def finish_kernel(tab, p0, p1, p2, p3, cur_ref, own_ref, oth_ref, y_ref):
    w = BAND + STEPS - 1
    low = low_half()
    row0 = tab[PLACE] * 4
    z, h = tab[PLACE + 6], tab[PLACE + 4]
    y_ref[...] = jnp.zeros_like(y_ref)
    for e in range(4):
        i = tab[PERM + row0 + e]
        for m in range(w + 2):
            cur = cur_ref[e, m - 1] if 1 <= m <= w + 1 else jnp.zeros((8, 128), F32)
            square = total((p0, p1, p2, p3), e, m)
            value = polynomial(tab, STEPS - 1, cur, square)
            turned = swap_halves(value)
            for half in (0, 1):
                v = 2 * m + half
                if v == 0:
                    continue
                j = (i + v + 64 - (w + 2)) & 63
                sj = tab[INV + j]
                odd = sj & 1
                piece = jnp.where(odd == half, value, turned)
                piece = jnp.where(bit(tab, STEPS, i, j) == 1, piece, 0.0)
                side = jnp.where(low, 0, 1) == odd
                at = ((sj >> 3) & 1) ^ h, (sj >> 4) ^ z, e, (sj & 7) >> 1
                y_ref[at] = jnp.where(side, piece, y_ref[at])
    own_ref[...] = y_ref[0]
    oth_ref[...] = y_ref[1]


def join_kernel(y0, y1, y2, y3, out_ref):
    z, h = lax.axis_index("col"), lax.axis_index("layer")
    for k, y_ref in enumerate((y0, y1, y2, y3)):
        for core in (0, 1):
            for e in range(4):
                start = pl.multiple_of(e * 64 + (2 * (z ^ k) + (core ^ h)) * 8, 8)
                for t in range(4):
                    out_ref[pl.ds(start, 8), t * 128 : (t + 1) * 128] = y_ref[core, e, t]


def tables(masks, branch, perm):
    r = lax.axis_index("row")
    z = lax.axis_index("col")
    h = lax.axis_index("layer")
    ids = jnp.arange(64, dtype=jnp.int32)
    inverse = jnp.sum(jnp.where(perm[:, None] == ids[None, :], ids[:, None], 0), axis=0)
    shifts = jnp.arange(32, dtype=jnp.int32)
    bits = jnp.sum(masks.reshape(6, 64, 2, 32) << shifts, axis=-1, dtype=jnp.int32)
    pos = jnp.sum(jnp.where(jnp.asarray(RING) == r, jnp.arange(16), 0))
    place = jnp.stack([r, z * 2 + h, r // 4, r % 4, h, pos, z, z]).astype(jnp.int32)
    return jnp.concatenate(
        [perm, inverse.astype(jnp.int32), branch, jnp.zeros((3,), jnp.int32), bits.reshape(-1), place]
    )


def z_exchange(parts):
    return [parts[0]] + [z_swap(parts[k], k) for k in (1, 2, 3)]


def reduce_group(own, oth):
    return z_exchange(call(pair_kernel, [own.shape[1:]] * 4, [own, core_swap(oth)]))


def spread_group(own, oth):
    shape = (2,) + own.shape[1:]
    return z_exchange(call(pack_kernel, [shape] * 4, [own, core_swap(oth)]))


def shards(density, masks, branch, perm):
    slabs = (4, 4, 4, 8, 128)
    split = spread_group(*call(split_kernel, [slabs] * 2, [density]))
    tab = tables(masks, branch, perm)
    halves = call(
        compact_kernel,
        [(2, BAND + 1, 8, 128)] * 2,
        split,
        [pltpu.VMEM((4, 2, 4, 4, 8, 128), F32)],
        tab=tab,
    )
    gathered = gather_rows(*halves, True)
    for step in range(STEPS - 1):
        w = BAND + step
        left, count = geometry(w)
        rows = (4 + 2 * w) * 8
        part = (4, 4, w + 2, 8, 128)
        scratch = [
            pltpu.VMEM((rows, count * 128), BF16),
            pltpu.VMEM((rows, count * 128), BF16),
            pltpu.VMEM((32, 8, count * 128), F32),
        ]
        if step == 0:
            scratch.append(pltpu.VMEM((8, 4, 2, w + 1, 8, 128), F32))
            own, oth, cur = call(
                first_step_kernel, [part, part, (4, w + 1, 8, 128)], gathered, scratch, tab=tab
            )
        else:
            kernel = lambda *refs, w=w, pieces=pieces: step_kernel(w, pieces, *refs)
            own, oth = call(kernel, [part, part], [cur] + around, scratch, tab=tab)
        parts = reduce_group(own, oth)
        pieces = halo_pieces(w + 1) if step < STEPS - 2 else []
        cuts = [(0, 4, 0, w + 2)] if pieces else [(0, 2, 0, w + 2), (2, 4, 0, w + 2)]
        for _, cut in pieces:
            if cut not in cuts:
                cuts.append(cut)
        kernel = lambda *refs, step=step, cuts=cuts: close_kernel(step, cuts, *refs)
        shapes = [(hi - lo, last - first, 8, 128) for lo, hi, first, last in cuts]
        sent = call(kernel, shapes, parts + [cur], tab=tab)
        cur = sent[0]
        around = [ring_shift(sent[cuts.index(cut)], d) for d, cut in pieces]
        cur, *around = lax.optimization_barrier((cur, *around))
    gathered = gather_rows(*sent, False)
    w = BAND + STEPS - 1
    part = (4, 4, w + 2, 8, 128)
    scratch = [
        pltpu.VMEM(((2 * w + 2) * 8, (w + 2) * 128), BF16),
        pltpu.VMEM(((2 * w + 2) * 8, (w + 2) * 128), BF16),
        pltpu.VMEM((8, 8, (w + 2) * 128), F32),
        pltpu.VMEM((8, 4, 2, w + 1, 8, 128), F32),
    ]
    own, oth, cur = call(
        last_step_kernel, [part, part, (4, w + 1, 8, 128)], gathered, scratch, tab=tab
    )
    parts = reduce_group(own, oth)
    own, oth = call(
        finish_kernel, [slabs] * 2, parts + [cur], [pltpu.VMEM((2,) + slabs, F32)], tab=tab
    )
    (out,) = call(join_kernel, [(256, 512)], spread_group(own, oth))
    return out


def solution(mesh):
    return jax.shard_map(
        shards,
        mesh=mesh,
        in_specs=(P("row", GROUP), P(), P(), P()),
        out_specs=P("row", GROUP),
        check_vma=False,
    )
```

```python
import jax
import jax.numpy as jnp
from jax import lax
from jax.experimental import pallas as pl
from jax.experimental.pallas import tpu as pltpu
from jax.sharding import PartitionSpec as P

STEPS = 5
BAND = 6
NB = 64
GROUP = ("col", "layer")
PERM, INV, BRANCH, BITS, PLACE = 0, 64, 128, 136, 136 + 6 * 128
F32, BF16 = jnp.float32, jnp.bfloat16


def ring_xy(pos):
    a, b = pos // 2, pos % 2
    return (a, b) if a < 4 else (7 - a, 3 - b)


RING = [ring_xy(p)[0] * 4 + ring_xy(p)[1] for p in range(16)]


def permute(value, axes, pairs):
    flat = value.reshape(-1, 128)
    return lax.ppermute(flat, axes, pairs).reshape(value.shape)


def ring_shift(value, k):
    return permute(value, "row", [(RING[p], RING[(p + k) % 16]) for p in range(16)])


def line_shift(value, k, swapped):
    pairs = []
    for i in range(16):
        for core in (0, 1):
            x, y = i // 4, i % 4
            x, y = (x, (y + k) % 4) if core ^ swapped else ((x + k) % 4, y)
            pairs.append((i * 2 + core, (x * 4 + y) * 2 + core))
    return permute(value, ("row", "layer"), pairs)


def z_swap(value, k):
    return permute(value, "col", [(i, i ^ k) for i in range(4)])


def core_swap(value):
    return permute(value, "layer", [(0, 1), (1, 0)])


def low_half():
    return lax.broadcasted_iota(jnp.int32, (8, 128), 1) < 64


def swap_halves(tile):
    return pltpu.roll(tile, 64, 1)


def bit(tab, s, i, j):
    word = tab[BITS + s * 128 + i * 2 + lax.shift_right_logical(j, 5)]
    return lax.shift_right_logical(word, j & 31) & 1


def shifted(tiles, d, count):
    n = len(tiles)
    get = lambda seq, t: seq[t] if 0 <= t < n else None
    if d % 2 == 0:
        return [get(tiles, m - d // 2) for m in range(count)]
    q = (d - 1) // 2
    low = low_half()
    turned = [swap_halves(t) for t in tiles]
    out = []
    for m in range(count):
        a, b = get(turned, m - q - 1), get(turned, m - q)
        if a is None and b is None:
            out.append(None)
        else:
            zero = jnp.zeros((8, 128), F32)
            out.append(jnp.where(low, zero if a is None else a, zero if b is None else b))
    return out


def store_split(hi_ref, lo_ref, row, first, second):
    zero = jnp.zeros((8, 128), F32)
    for m, (a, b) in enumerate(zip(first, second)):
        both = jnp.concatenate([zero if a is None else a, zero if b is None else b], axis=0)
        hi = both.astype(BF16)
        hi_ref[row : row + 16, m * 128 : (m + 1) * 128] = hi
        lo_ref[row : row + 16, m * 128 : (m + 1) * 128] = (both - hi.astype(F32)).astype(BF16)


def tdot(a, b):
    return lax.dot_general(a, b, (((0,), (0,)), ((), ())), preferred_element_type=F32)


def product(hi_ref, lo_ref, start, width):
    xh = hi_ref[:, start : start + width]
    xl = lo_ref[:, start : start + width]
    zh = hi_ref[...]
    return tdot(xh, zh) + tdot(xh, lo_ref[...]) + tdot(xl, zh)


def call(kernel, outs, args, scratch=(), tab=None):
    vmem = pl.BlockSpec(memory_space=pltpu.VMEM)
    table = [] if tab is None else [pl.BlockSpec(memory_space=pltpu.SMEM)]
    return pl.pallas_call(
        kernel,
        out_shape=[jax.ShapeDtypeStruct(o, F32) for o in outs],
        in_specs=table + [vmem] * len(args),
        out_specs=[vmem] * len(outs),
        scratch_shapes=list(scratch),
        compiler_params=pltpu.CompilerParams(vmem_limit_bytes=48 * 1024 * 1024),
    )(*([] if tab is None else [tab]), *args)


def split_kernel(d_ref, own_ref, oth_ref):
    z, h = lax.axis_index("col"), lax.axis_index("layer")
    for k in range(4):
        for ref, core in ((own_ref, h), (oth_ref, 1 - h)):
            for e in range(4):
                start = pl.multiple_of(e * 64 + (2 * (z ^ k) + core) * 8, 8)
                rows = d_ref[pl.ds(start, 8), :]
                for t in range(4):
                    ref[k, e, t] = rows[:, t * 128 : (t + 1) * 128]


def pack_kernel(own_ref, got_ref, *outs):
    for k in range(4):
        outs[k][0] = own_ref[k]
        outs[k][1] = got_ref[k]


def compact_kernel(tab, *refs):
    ins, (out_ref, x_ref) = refs[:4], refs[4:]
    for k in range(4):
        x_ref[k] = ins[k][...]
    low = low_half()
    row0 = tab[PLACE] * 4
    z, h = tab[PLACE + 6], tab[PLACE + 4]
    for e in range(4):
        i = tab[PERM + row0 + e]
        halves = []
        for t in range(2 * BAND + 2):
            if t > 2 * BAND:
                halves.append(jnp.zeros((8, 128), F32))
                continue
            j = (i + t - BAND) & 63
            sj = tab[INV + j]
            tile = x_ref[(sj >> 4) ^ z, ((sj >> 3) & 1) ^ h, e, (sj & 7) >> 1]
            tile = jnp.where((sj & 1) == (t & 1), tile, swap_halves(tile))
            halves.append(jnp.where(bit(tab, 0, i, j) == 1, tile, 0.0))
        for t in range(BAND + 1):
            out_ref[e, t] = jnp.where(low, halves[2 * t], halves[2 * t + 1])


def gather_rows(rows):
    near = [line_shift(rows, k, 0) for k in (1, 3, 2)]
    rows, *near = lax.optimization_barrier((rows, *near))
    line = jnp.stack([rows, near[0], near[2], near[1]])
    line = lax.optimization_barrier(line)
    far = [line_shift(line, k, 1) for k in (1, 3, 2)]
    return [line, far[0], far[2], far[1]]


def collect(ins, g_ref):
    for n in range(4):
        g_ref[n] = ins[n][...]


def seat(tab, r, e):
    dx = (tab[PLACE + 2] - (r >> 2)) & 3
    dy = (tab[PLACE + 3] - (r & 3)) & 3
    first = tab[PLACE + 4] == 0
    return jnp.where(first, dy, dx), jnp.where(first, dx, dy), e


def write_slabs(tab, p_ref, own_ref, oth_ref, e, base, d, tiles):
    z, h = tab[PLACE + 6], tab[PLACE + 4]
    low = low_half()
    for zz in range(4):
        for ref, core in ((own_ref, h), (oth_ref, 1 - h)):
            rows = p_ref[base + 2 * (z ^ zz) + core]
            if d % 2 == 0:
                for m in range(tiles):
                    at = (d // 2 + m) * 128
                    ref[zz, e, m] = rows[:, at : at + 128]
            else:
                q = d // 2
                turned = []
                for m in range(tiles + 1):
                    at = (q + m) * 128
                    if at < rows.shape[1]:
                        turned.append(swap_halves(rows[:, at : at + 128]))
                    else:
                        turned.append(jnp.zeros((8, 128), F32))
                for m in range(tiles):
                    ref[zz, e, m] = jnp.where(low, turned[m], turned[m + 1])


def geometry(w):
    left = w + 1 + (w + 1) % 2
    return left, (left + 4 + w + 1 + 1) // 2


def step_body(tab, strips, w, own_ref, oth_ref, hi_ref, lo_ref, p_ref):
    left, count = geometry(w)
    nk = 4 + 2 * w
    for a in range(0, nk, 2):
        pair = []
        for b in (a, a + 1):
            tiles, first = strips(b)
            pair.append(shifted(tiles, left - 2 * w + b + 2 * first, count))
        store_split(hi_ref, lo_ref, a * 8, pair[0], pair[1])
    p_ref[...] = product(hi_ref, lo_ref, left * 64, 256).reshape(32, 8, count * 128)
    for e in range(4):
        write_slabs(tab, p_ref, own_ref, oth_ref, e, e * 8, left - (w + 1) + e, w + 2)


def first_step_kernel(tab, *refs):
    ins, (own_ref, oth_ref, cur_ref, hi_ref, lo_ref, p_ref, g_ref) = refs[:4], refs[4:]
    collect(ins, g_ref)
    w = BAND
    base = tab[PLACE + 5] * 4 + 64 - w

    def strips(b):
        sk = tab[INV + ((base + b) & 63)]
        u, v, e = seat(tab, sk >> 2, sk & 3)
        strip = g_ref[u, v, e]
        if w <= b < w + 4:
            cur_ref[b - w] = strip
        return [strip[t] for t in range(w + 1)], 0

    step_body(tab, strips, w, own_ref, oth_ref, hi_ref, lo_ref, p_ref)


def step_kernel(w, pieces, tab, *refs):
    n = 1 + len(pieces)
    ins, (own_ref, oth_ref, hi_ref, lo_ref, p_ref) = refs[:n], refs[n:]

    def strips(b):
        off = b - w
        if 0 <= off < 4:
            return [ins[0][off, t] for t in range(w + 1)], 0
        d = (-off + 3) // 4 if off < 0 else -(off // 4)
        at = [piece[0] for piece in pieces].index(d)
        _, (lo, hi, first, last) = pieces[at]
        row = off + 4 * d - lo
        return [ins[1 + at][row, t] for t in range(last - first)], first

    step_body(tab, strips, w, own_ref, oth_ref, hi_ref, lo_ref, p_ref)


def halo_pieces(w):
    out = []
    for d in range(1, (w + 3) // 4 + 1):
        n = min(4, w - 4 * (d - 1))
        out.append((d, (4 - n, 4, 2 * (d - 1), w + 1)))
        out.append((-d, (0, n, 0, w + 1 - 2 * (d - 1))))
    return out


def last_step_kernel(tab, *refs):
    ins, (own_ref, oth_ref, cur_ref, hi_ref, lo_ref, p_ref, g_ref) = refs[:4], refs[4:]
    collect(ins, g_ref)
    w = BAND + STEPS - 1
    row0 = tab[PLACE] * 4
    left, count = w + 2, w + 2
    for e in range(4):
        i = tab[PERM + row0 + e]

        def strips(b):
            k = (i + b - w) & 63
            pos = k >> 2
            a, odd = pos >> 1, pos & 1
            r = jnp.where(a < 4, a * 4 + odd, (7 - a) * 4 + 3 - odd)
            u, v, ee = seat(tab, r, k & 3)
            strip = g_ref[u, v, ee]
            if b == w:
                cur_ref[e] = strip
            return [strip[t] for t in range(w + 1)]

        for a in range(0, 2 * w + 2, 2):
            one = shifted(strips(a), left - 2 * w + a, count)
            two = [None] * count
            if a + 1 <= 2 * w:
                two = shifted(strips(a + 1), left - 2 * w + a + 1, count)
            store_split(hi_ref, lo_ref, a * 8, one, two)
        p_ref[...] = product(hi_ref, lo_ref, left * 64, 64).reshape(8, 8, count * 128)
        write_slabs(tab, p_ref, own_ref, oth_ref, e, 0, 0, count)


def pair_kernel(own_ref, got_ref, *outs):
    for k in range(4):
        outs[k][...] = own_ref[k] + got_ref[k]


def total(parts, e, m):
    return (parts[0][e, m] + parts[1][e, m]) + (parts[2][e, m] + parts[3][e, m])


def polynomial(tab, step, cur, square):
    return jnp.where(tab[BRANCH + step] == 1, 2.0 * cur - square, square)


def close_kernel(step, cuts, tab, p0, p1, p2, p3, cur_ref, *refs):
    w = BAND + step
    low = low_half()
    i0 = tab[PLACE + 5] * 4
    for e in range(4):
        i = i0 + e
        turned = [swap_halves(cur_ref[e, t]) for t in range(w + 1)]
        zero = jnp.zeros((8, 128), F32)
        for m in range(w + 2):
            before = turned[m - 1] if m >= 1 else zero
            after = turned[m] if m <= w else zero
            cur = jnp.where(low, before, after)
            square = total((p0, p1, p2, p3), e, m)
            one = bit(tab, step + 1, i, (i + 2 * m + 63 - w) & 63)
            two = 0
            if 2 * m + 1 <= 2 * w + 2:
                two = bit(tab, step + 1, i, (i + 2 * m + 64 - w) & 63)
            keep = jnp.where(low, one, two) == 1
            value = jnp.where(keep, polynomial(tab, step, cur, square), 0.0)
            for ref, (lo, hi, first, last) in zip(refs, cuts):
                if lo <= e < hi and first <= m < last:
                    ref[e - lo, m - first] = value


def finish_kernel(tab, p0, p1, p2, p3, cur_ref, own_ref, oth_ref, y_ref):
    w = BAND + STEPS - 1
    low = low_half()
    row0 = tab[PLACE] * 4
    z, h = tab[PLACE + 6], tab[PLACE + 4]
    y_ref[...] = jnp.zeros_like(y_ref)
    for e in range(4):
        i = tab[PERM + row0 + e]
        for m in range(w + 2):
            cur = cur_ref[e, m - 1] if 1 <= m <= w + 1 else jnp.zeros((8, 128), F32)
            square = total((p0, p1, p2, p3), e, m)
            value = polynomial(tab, STEPS - 1, cur, square)
            turned = swap_halves(value)
            for half in (0, 1):
                v = 2 * m + half
                if v == 0:
                    continue
                j = (i + v + 64 - (w + 2)) & 63
                sj = tab[INV + j]
                odd = sj & 1
                piece = jnp.where(odd == half, value, turned)
                piece = jnp.where(bit(tab, STEPS, i, j) == 1, piece, 0.0)
                side = jnp.where(low, 0, 1) == odd
                at = ((sj >> 3) & 1) ^ h, (sj >> 4) ^ z, e, (sj & 7) >> 1
                y_ref[at] = jnp.where(side, piece, y_ref[at])
    own_ref[...] = y_ref[0]
    oth_ref[...] = y_ref[1]


def join_kernel(y0, y1, y2, y3, out_ref):
    z, h = lax.axis_index("col"), lax.axis_index("layer")
    for k, y_ref in enumerate((y0, y1, y2, y3)):
        for core in (0, 1):
            for e in range(4):
                start = pl.multiple_of(e * 64 + (2 * (z ^ k) + (core ^ h)) * 8, 8)
                for t in range(4):
                    out_ref[pl.ds(start, 8), t * 128 : (t + 1) * 128] = y_ref[core, e, t]


def tables(masks, branch, perm):
    r = lax.axis_index("row")
    z = lax.axis_index("col")
    h = lax.axis_index("layer")
    ids = jnp.arange(64, dtype=jnp.int32)
    inverse = jnp.sum(jnp.where(perm[:, None] == ids[None, :], ids[:, None], 0), axis=0)
    shifts = jnp.arange(32, dtype=jnp.int32)
    bits = jnp.sum(masks.reshape(6, 64, 2, 32) << shifts, axis=-1, dtype=jnp.int32)
    pos = jnp.sum(jnp.where(jnp.asarray(RING) == r, jnp.arange(16), 0))
    place = jnp.stack([r, z * 2 + h, r // 4, r % 4, h, pos, z, z]).astype(jnp.int32)
    return jnp.concatenate(
        [perm, inverse.astype(jnp.int32), branch, jnp.zeros((3,), jnp.int32), bits.reshape(-1), place]
    )


def z_exchange(parts):
    return [parts[0]] + [z_swap(parts[k], k) for k in (1, 2, 3)]


def reduce_group(own, oth):
    return z_exchange(call(pair_kernel, [own.shape[1:]] * 4, [own, core_swap(oth)]))


def spread_group(own, oth):
    shape = (2,) + own.shape[1:]
    return z_exchange(call(pack_kernel, [shape] * 4, [own, core_swap(oth)]))


def shards(density, masks, branch, perm):
    slabs = (4, 4, 4, 8, 128)
    split = spread_group(*call(split_kernel, [slabs] * 2, [density]))
    tab = tables(masks, branch, perm)
    (rows,) = call(
        compact_kernel,
        [(4, BAND + 1, 8, 128)],
        split,
        [pltpu.VMEM((4, 2, 4, 4, 8, 128), F32)],
        tab=tab,
    )
    gathered = gather_rows(rows)
    for step in range(STEPS - 1):
        w = BAND + step
        left, count = geometry(w)
        depth = (4 + 2 * w) * 8
        part = (4, 4, w + 2, 8, 128)
        scratch = [
            pltpu.VMEM((depth, count * 128), BF16),
            pltpu.VMEM((depth, count * 128), BF16),
            pltpu.VMEM((32, 8, count * 128), F32),
        ]
        if step == 0:
            scratch.append(pltpu.VMEM((4, 4, 4, w + 1, 8, 128), F32))
            own, oth, cur = call(
                first_step_kernel, [part, part, (4, w + 1, 8, 128)], gathered, scratch, tab=tab
            )
        else:
            kernel = lambda *refs, w=w, pieces=pieces: step_kernel(w, pieces, *refs)
            own, oth = call(kernel, [part, part], [cur] + around, scratch, tab=tab)
        parts = reduce_group(own, oth)
        pieces = halo_pieces(w + 1) if step < STEPS - 2 else []
        cuts = [(0, 4, 0, w + 2)]
        for _, cut in pieces:
            if cut not in cuts:
                cuts.append(cut)
        kernel = lambda *refs, step=step, cuts=cuts: close_kernel(step, cuts, *refs)
        shapes = [(hi - lo, last - first, 8, 128) for lo, hi, first, last in cuts]
        sent = call(kernel, shapes, parts + [cur], tab=tab)
        cur = sent[0]
        around = [ring_shift(sent[cuts.index(cut)], d) for d, cut in pieces]
        cur, *around = lax.optimization_barrier((cur, *around))
    gathered = gather_rows(cur)
    w = BAND + STEPS - 1
    part = (4, 4, w + 2, 8, 128)
    scratch = [
        pltpu.VMEM(((2 * w + 2) * 8, (w + 2) * 128), BF16),
        pltpu.VMEM(((2 * w + 2) * 8, (w + 2) * 128), BF16),
        pltpu.VMEM((8, 8, (w + 2) * 128), F32),
        pltpu.VMEM((4, 4, 4, w + 1, 8, 128), F32),
    ]
    own, oth, cur = call(
        last_step_kernel, [part, part, (4, w + 1, 8, 128)], gathered, scratch, tab=tab
    )
    parts = reduce_group(own, oth)
    own, oth = call(
        finish_kernel, [slabs] * 2, parts + [cur], [pltpu.VMEM((2,) + slabs, F32)], tab=tab
    )
    (out,) = call(join_kernel, [(256, 512)], spread_group(own, oth))
    return out


def solution(mesh):
    return jax.shard_map(
        shards,
        mesh=mesh,
        in_specs=(P("row", GROUP), P(), P(), P()),
        out_specs=P("row", GROUP),
        check_vma=False,
    )
```

```python
import jax
import jax.numpy as jnp
from jax import lax
from jax.experimental import pallas as pl
from jax.experimental.pallas import tpu as pltpu
from jax.sharding import PartitionSpec as P

STEPS = 5
BAND = 6
NB = 64
GROUP = ("col", "layer")
PERM, INV, BRANCH, BITS, PLACE = 0, 64, 128, 136, 136 + 6 * 128
F32, BF16 = jnp.float32, jnp.bfloat16


def ring_xy(pos):
    a, b = pos // 2, pos % 2
    return (a, b) if a < 4 else (7 - a, 3 - b)


RING = [ring_xy(p)[0] * 4 + ring_xy(p)[1] for p in range(16)]


SLOTS = ((0, 2, 1, 3), (0, 2, 3, 1))


def permute(value, axes, pairs):
    flat = value.reshape(-1, 128)
    return lax.ppermute(flat, axes, pairs).reshape(value.shape)


def ring_shift(value, k):
    return permute(value, "row", [(RING[p], RING[(p + k) % 16]) for p in range(16)])


def line_shift(value, k, swapped):
    pairs = []
    for i in range(16):
        for core in (0, 1):
            x, y = i // 4, i % 4
            x, y = (x, (y + k) % 4) if core ^ swapped else ((x + k) % 4, y)
            pairs.append((i * 2 + core, (x * 4 + y) * 2 + core))
    return permute(value, ("row", "layer"), pairs)


def z_swap(value, slot):
    pairs = [(z * 2 + h, (z ^ SLOTS[h][slot]) * 2 + h) for z in range(4) for h in (0, 1)]
    return permute(value, GROUP, pairs)


def slot_of(z, h, slot):
    first, second = SLOTS[0][slot], SLOTS[1][slot]
    return z ^ (first if first == second else jnp.where(h == 0, first, second))


def slot_with(apart, h):
    swapped = jnp.where(apart == 3, 1, jnp.where(apart == 1, 3, apart))
    apart = jnp.where(h == 0, apart, swapped)
    return jnp.where(apart == 2, 1, jnp.where(apart == 1, 2, apart))


def core_swap(value):
    return permute(value, "layer", [(0, 1), (1, 0)])


def low_half():
    return lax.broadcasted_iota(jnp.int32, (8, 128), 1) < 64


def swap_halves(tile):
    return pltpu.roll(tile, 64, 1)


def bit(tab, s, i, j):
    word = tab[BITS + s * 128 + i * 2 + lax.shift_right_logical(j, 5)]
    return lax.shift_right_logical(word, j & 31) & 1


def shifted(tiles, d, count):
    n = len(tiles)
    get = lambda seq, t: seq[t] if 0 <= t < n else None
    if d % 2 == 0:
        return [get(tiles, m - d // 2) for m in range(count)]
    q = (d - 1) // 2
    low = low_half()
    turned = [swap_halves(t) for t in tiles]
    out = []
    for m in range(count):
        a, b = get(turned, m - q - 1), get(turned, m - q)
        if a is None and b is None:
            out.append(None)
        else:
            zero = jnp.zeros((8, 128), F32)
            out.append(jnp.where(low, zero if a is None else a, zero if b is None else b))
    return out


def store_split(hi_ref, lo_ref, row, first, second):
    zero = jnp.zeros((8, 128), F32)
    for m, (a, b) in enumerate(zip(first, second)):
        both = jnp.concatenate([zero if a is None else a, zero if b is None else b], axis=0)
        hi = both.astype(BF16)
        hi_ref[row : row + 16, m * 128 : (m + 1) * 128] = hi
        lo_ref[row : row + 16, m * 128 : (m + 1) * 128] = (both - hi.astype(F32)).astype(BF16)


def tdot(a, b):
    return lax.dot_general(a, b, (((0,), (0,)), ((), ())), preferred_element_type=F32)


def product(hi_ref, lo_ref, start, width):
    xh = hi_ref[:, start : start + width]
    xl = lo_ref[:, start : start + width]
    zh = hi_ref[...]
    return tdot(xh, zh) + tdot(xh, lo_ref[...]) + tdot(xl, zh)


def call(kernel, outs, args, scratch=(), tab=None):
    vmem = pl.BlockSpec(memory_space=pltpu.VMEM)
    table = [] if tab is None else [pl.BlockSpec(memory_space=pltpu.SMEM)]
    return pl.pallas_call(
        kernel,
        out_shape=[jax.ShapeDtypeStruct(o, F32) for o in outs],
        in_specs=table + [vmem] * len(args),
        out_specs=[vmem] * len(outs),
        scratch_shapes=list(scratch),
        compiler_params=pltpu.CompilerParams(vmem_limit_bytes=48 * 1024 * 1024),
    )(*([] if tab is None else [tab]), *args)


def split_kernel(d_ref, own_ref, oth_ref):
    z, h = lax.axis_index("col"), lax.axis_index("layer")
    for k in range(4):
        for ref, core in ((own_ref, h), (oth_ref, 1 - h)):
            for e in range(4):
                start = pl.multiple_of(e * 64 + (2 * slot_of(z, core, k) + core) * 8, 8)
                rows = d_ref[pl.ds(start, 8), :]
                for t in range(4):
                    ref[k, e, t] = rows[:, t * 128 : (t + 1) * 128]


def pack_kernel(own_ref, got_ref, *outs):
    for k in range(4):
        outs[k][0] = own_ref[k]
        outs[k][1] = got_ref[k]


def compact_kernel(tab, *refs):
    ins, (keep_ref, out_ref, x_ref) = refs[:4], refs[4:]
    for k in range(4):
        x_ref[k] = ins[k][...]
    low = low_half()
    row0 = tab[PLACE] * 4
    z, h = tab[PLACE + 6], tab[PLACE + 4]
    for e in range(4):
        i = tab[PERM + row0 + e]
        halves = []
        for t in range(2 * BAND + 2):
            if t > 2 * BAND:
                halves.append(jnp.zeros((8, 128), F32))
                continue
            j = (i + t - BAND) & 63
            sj = tab[INV + j]
            tile = x_ref[slot_with((sj >> 4) ^ z, h), ((sj >> 3) & 1) ^ h, e, (sj & 7) >> 1]
            halves.append(jnp.where((sj & 1) == (t & 1), tile, swap_halves(tile)))
        for t in range(BAND + 1):
            out_ref[e, t] = jnp.where(low, halves[2 * t], halves[2 * t + 1]) * keep_ref[e, t]


def gather_rows(rows):
    near = [line_shift(rows, k, 0) for k in (1, 3, 2)]
    rows, *near = lax.optimization_barrier((rows, *near))
    line = jnp.stack([rows, near[0], near[2], near[1]])
    line = lax.optimization_barrier(line)
    far = [line_shift(line, k, 1) for k in (1, 3, 2)]
    return [line, far[0], far[2], far[1]]


def collect(ins, g_ref):
    for n in range(4):
        g_ref[n] = ins[n][...]


def seat(tab, r, e):
    dx = (tab[PLACE + 2] - (r >> 2)) & 3
    dy = (tab[PLACE + 3] - (r & 3)) & 3
    first = tab[PLACE + 4] == 0
    return jnp.where(first, dy, dx), jnp.where(first, dx, dy), e


def write_slabs(tab, p_ref, own_ref, oth_ref, e, base, d, tiles):
    z, h = tab[PLACE + 6], tab[PLACE + 4]
    low = low_half()
    for zz in range(4):
        for ref, core in ((own_ref, h), (oth_ref, 1 - h)):
            rows = p_ref[base + 2 * slot_of(z, core, zz) + core]
            if d % 2 == 0:
                for m in range(tiles):
                    at = (d // 2 + m) * 128
                    ref[zz, e, m] = rows[:, at : at + 128]
            else:
                q = d // 2
                turned = []
                for m in range(tiles + 1):
                    at = (q + m) * 128
                    if at < rows.shape[1]:
                        turned.append(swap_halves(rows[:, at : at + 128]))
                    else:
                        turned.append(jnp.zeros((8, 128), F32))
                for m in range(tiles):
                    ref[zz, e, m] = jnp.where(low, turned[m], turned[m + 1])


def geometry(w):
    left = w + 1 + (w + 1) % 2
    return left, (left + 4 + w + 1 + 1) // 2


def step_body(tab, strips, w, own_ref, oth_ref, hi_ref, lo_ref, p_ref):
    left, count = geometry(w)
    nk = 4 + 2 * w
    for a in range(0, nk, 2):
        pair = []
        for b in (a, a + 1):
            tiles, first = strips(b)
            pair.append(shifted(tiles, left - 2 * w + b + 2 * first, count))
        store_split(hi_ref, lo_ref, a * 8, pair[0], pair[1])
    p_ref[...] = product(hi_ref, lo_ref, left * 64, 256).reshape(32, 8, count * 128)
    for e in range(4):
        write_slabs(tab, p_ref, own_ref, oth_ref, e, e * 8, left - (w + 1) + e, w + 2)


def first_step_kernel(tab, *refs):
    ins, (own_ref, oth_ref, cur_ref, hi_ref, lo_ref, p_ref, g_ref) = refs[:4], refs[4:]
    collect(ins, g_ref)
    w = BAND
    base = tab[PLACE + 5] * 4 + 64 - w

    def strips(b):
        sk = tab[INV + ((base + b) & 63)]
        u, v, e = seat(tab, sk >> 2, sk & 3)
        strip = g_ref[u, v, e]
        if w <= b < w + 4:
            cur_ref[b - w] = strip
        return [strip[t] for t in range(w + 1)], 0

    step_body(tab, strips, w, own_ref, oth_ref, hi_ref, lo_ref, p_ref)


def step_kernel(w, pieces, tab, *refs):
    n = 1 + len(pieces)
    ins, (own_ref, oth_ref, hi_ref, lo_ref, p_ref) = refs[:n], refs[n:]

    def strips(b):
        off = b - w
        if 0 <= off < 4:
            return [ins[0][off, t] for t in range(w + 1)], 0
        d = (-off + 3) // 4 if off < 0 else -(off // 4)
        at = [piece[0] for piece in pieces].index(d)
        _, (lo, hi, first, last) = pieces[at]
        row = off + 4 * d - lo
        return [ins[1 + at][row, t] for t in range(last - first)], first

    step_body(tab, strips, w, own_ref, oth_ref, hi_ref, lo_ref, p_ref)


def halo_pieces(w):
    out = []
    for d in range(1, (w + 3) // 4 + 1):
        n = min(4, w - 4 * (d - 1))
        out.append((d, (4 - n, 4, 2 * (d - 1), w + 1)))
        out.append((-d, (0, n, 0, w + 1 - 2 * (d - 1))))
    return out


def last_step_kernel(tab, *refs):
    ins, (own_ref, oth_ref, cur_ref, hi_ref, lo_ref, p_ref, g_ref) = refs[:4], refs[4:]
    collect(ins, g_ref)
    w = BAND + STEPS - 1
    row0 = tab[PLACE] * 4
    left, count = w + 2, w + 2
    for e in range(4):
        i = tab[PERM + row0 + e]

        def strips(b):
            k = (i + b - w) & 63
            pos = k >> 2
            a, odd = pos >> 1, pos & 1
            r = jnp.where(a < 4, a * 4 + odd, (7 - a) * 4 + 3 - odd)
            u, v, ee = seat(tab, r, k & 3)
            strip = g_ref[u, v, ee]
            if b == w:
                cur_ref[e] = strip
            return [strip[t] for t in range(w + 1)]

        for a in range(0, 2 * w + 2, 2):
            one = shifted(strips(a), left - 2 * w + a, count)
            two = [None] * count
            if a + 1 <= 2 * w:
                two = shifted(strips(a + 1), left - 2 * w + a + 1, count)
            store_split(hi_ref, lo_ref, a * 8, one, two)
        p_ref[...] = product(hi_ref, lo_ref, left * 64, 64).reshape(8, 8, count * 128)
        write_slabs(tab, p_ref, own_ref, oth_ref, e, 0, 0, count)


def pair_kernel(own_ref, got_ref, *outs):
    for k in range(4):
        outs[k][...] = own_ref[k] + got_ref[k]


def total(parts, e, m):
    return (parts[0][e, m] + parts[1][e, m]) + (parts[2][e, m] + parts[3][e, m])


def polynomial(tab, step, cur, square):
    return jnp.where(tab[BRANCH + step] == 1, 2.0 * cur - square, square)


def keep_kernel(tab, *refs):
    low = low_half()
    for s, ref in enumerate(refs):
        w = BAND + s
        margin = w + 1 if s == STEPS else w
        for e in range(4):
            i = tab[PLACE + 5] * 4 + e if 0 < s < STEPS else tab[PERM + tab[PLACE] * 4 + e]
            for m in range(ref.shape[1]):
                sides = []
                for v in (2 * m - margin, 2 * m + 1 - margin):
                    sides.append(bit(tab, s, i, (i + v + 64) & 63) if -w <= v <= w else 0)
                ref[e, m] = jnp.where(low, sides[0], sides[1]).astype(F32)


def close_kernel(step, cuts, tab, p0, p1, p2, p3, cur_ref, keep_ref, *refs):
    w = BAND + step
    low = low_half()
    for e in range(4):
        turned = [swap_halves(cur_ref[e, t]) for t in range(w + 1)]
        zero = jnp.zeros((8, 128), F32)
        for m in range(w + 2):
            before = turned[m - 1] if m >= 1 else zero
            after = turned[m] if m <= w else zero
            cur = jnp.where(low, before, after)
            square = total((p0, p1, p2, p3), e, m)
            value = polynomial(tab, step, cur, square) * keep_ref[e, m]
            for ref, (lo, hi, first, last) in zip(refs, cuts):
                if lo <= e < hi and first <= m < last:
                    ref[e - lo, m - first] = value


def finish_kernel(tab, p0, p1, p2, p3, cur_ref, keep_ref, own_ref, oth_ref, y_ref):
    w = BAND + STEPS - 1
    low = low_half()
    row0 = tab[PLACE] * 4
    z, h = tab[PLACE + 6], tab[PLACE + 4]
    y_ref[...] = jnp.zeros_like(y_ref)
    for e in range(4):
        i = tab[PERM + row0 + e]
        for m in range(w + 2):
            cur = cur_ref[e, m - 1] if 1 <= m <= w + 1 else jnp.zeros((8, 128), F32)
            square = total((p0, p1, p2, p3), e, m)
            value = polynomial(tab, STEPS - 1, cur, square) * keep_ref[e, m]
            turned = swap_halves(value)
            for half in (0, 1):
                v = 2 * m + half
                if v == 0:
                    continue
                j = (i + v + 64 - (w + 2)) & 63
                sj = tab[INV + j]
                odd = sj & 1
                piece = jnp.where(odd == half, value, turned)
                side = jnp.where(low, 0, 1) == odd
                core = (sj >> 3) & 1
                at = core ^ h, slot_with((sj >> 4) ^ z, core), e, (sj & 7) >> 1
                y_ref[at] = jnp.where(side, piece, y_ref[at])
    own_ref[...] = y_ref[0]
    oth_ref[...] = y_ref[1]


def join_kernel(y0, y1, y2, y3, out_ref):
    z, h = lax.axis_index("col"), lax.axis_index("layer")
    for k, y_ref in enumerate((y0, y1, y2, y3)):
        for core in (0, 1):
            for e in range(4):
                start = pl.multiple_of(e * 64 + (2 * slot_of(z, h, k) + (core ^ h)) * 8, 8)
                for t in range(4):
                    out_ref[pl.ds(start, 8), t * 128 : (t + 1) * 128] = y_ref[core, e, t]


def tables(masks, branch, perm):
    r = lax.axis_index("row")
    z = lax.axis_index("col")
    h = lax.axis_index("layer")
    ids = jnp.arange(64, dtype=jnp.int32)
    inverse = jnp.sum(jnp.where(perm[:, None] == ids[None, :], ids[:, None], 0), axis=0)
    shifts = jnp.arange(32, dtype=jnp.int32)
    bits = jnp.sum(masks.reshape(6, 64, 2, 32) << shifts, axis=-1, dtype=jnp.int32)
    pos = jnp.sum(jnp.where(jnp.asarray(RING) == r, jnp.arange(16), 0))
    place = jnp.stack([r, z * 2 + h, r // 4, r % 4, h, pos, z, z]).astype(jnp.int32)
    return jnp.concatenate(
        [perm, inverse.astype(jnp.int32), branch, jnp.zeros((3,), jnp.int32), bits.reshape(-1), place]
    )


def z_exchange(parts):
    return [parts[0]] + [z_swap(parts[k], k) for k in (1, 2, 3)]


def reduce_group(own, oth):
    return z_exchange(call(pair_kernel, [own.shape[1:]] * 4, [own, core_swap(oth)]))


def spread_group(own, oth):
    shape = (2,) + own.shape[1:]
    return z_exchange(call(pack_kernel, [shape] * 4, [own, core_swap(oth)]))


def shards(density, masks, branch, perm):
    slabs = (4, 4, 4, 8, 128)
    split = spread_group(*call(split_kernel, [slabs] * 2, [density]))
    tab = tables(masks, branch, perm)
    tiles = [BAND + s + 1 for s in range(STEPS)] + [BAND + STEPS + 1]
    keep = call(keep_kernel, [(4, n, 8, 128) for n in tiles], [], tab=tab)
    (rows,) = call(
        compact_kernel,
        [(4, BAND + 1, 8, 128)],
        split + [keep[0]],
        [pltpu.VMEM((4, 2, 4, 4, 8, 128), F32)],
        tab=tab,
    )
    gathered = gather_rows(rows)
    for step in range(STEPS - 1):
        w = BAND + step
        left, count = geometry(w)
        depth = (4 + 2 * w) * 8
        part = (4, 4, w + 2, 8, 128)
        scratch = [
            pltpu.VMEM((depth, count * 128), BF16),
            pltpu.VMEM((depth, count * 128), BF16),
            pltpu.VMEM((32, 8, count * 128), F32),
        ]
        if step == 0:
            scratch.append(pltpu.VMEM((4, 4, 4, w + 1, 8, 128), F32))
            own, oth, cur = call(
                first_step_kernel, [part, part, (4, w + 1, 8, 128)], gathered, scratch, tab=tab
            )
        else:
            kernel = lambda *refs, w=w, pieces=pieces: step_kernel(w, pieces, *refs)
            own, oth = call(kernel, [part, part], [cur] + around, scratch, tab=tab)
        parts = reduce_group(own, oth)
        pieces = halo_pieces(w + 1) if step < STEPS - 2 else []
        cuts = [(0, 4, 0, w + 2)]
        for _, cut in pieces:
            if cut not in cuts:
                cuts.append(cut)
        kernel = lambda *refs, step=step, cuts=cuts: close_kernel(step, cuts, *refs)
        shapes = [(hi - lo, last - first, 8, 128) for lo, hi, first, last in cuts]
        sent = call(kernel, shapes, parts + [cur, keep[step + 1]], tab=tab)
        cur = sent[0]
        around = [ring_shift(sent[cuts.index(cut)], d) for d, cut in pieces]
        cur, *around = lax.optimization_barrier((cur, *around))
    gathered = gather_rows(cur)
    w = BAND + STEPS - 1
    part = (4, 4, w + 2, 8, 128)
    scratch = [
        pltpu.VMEM(((2 * w + 2) * 8, (w + 2) * 128), BF16),
        pltpu.VMEM(((2 * w + 2) * 8, (w + 2) * 128), BF16),
        pltpu.VMEM((8, 8, (w + 2) * 128), F32),
        pltpu.VMEM((4, 4, 4, w + 1, 8, 128), F32),
    ]
    own, oth, cur = call(
        last_step_kernel, [part, part, (4, w + 1, 8, 128)], gathered, scratch, tab=tab
    )
    parts = reduce_group(own, oth)
    own, oth = call(
        finish_kernel, [slabs] * 2, parts + [cur, keep[STEPS]], [pltpu.VMEM((2,) + slabs, F32)], tab=tab
    )
    (out,) = call(join_kernel, [(256, 512)], spread_group(own, oth))
    return out


def solution(mesh):
    return jax.shard_map(
        shards,
        mesh=mesh,
        in_specs=(P("row", GROUP), P(), P(), P()),
        out_specs=P("row", GROUP),
        check_vma=False,
    )
```

```python
import jax
import jax.numpy as jnp
from jax import lax
from jax.experimental import pallas as pl
from jax.experimental.pallas import tpu as pltpu
from jax.sharding import PartitionSpec as P

STEPS = 5
BAND = 6
NB = 64
GROUP = ("col", "layer")
PERM, INV, BRANCH, BITS, PLACE = 0, 64, 128, 136, 136 + 6 * 128
F32, BF16 = jnp.float32, jnp.bfloat16


def ring_xy(pos):
    a, b = pos // 2, pos % 2
    return (a, b) if a < 4 else (7 - a, 3 - b)


RING = [ring_xy(p)[0] * 4 + ring_xy(p)[1] for p in range(16)]


SLOTS = ((0, 2, 1, 3), (0, 2, 3, 1))


def permute(value, axes, pairs):
    flat = value.reshape(-1, 128)
    return lax.ppermute(flat, axes, pairs).reshape(value.shape)


def ring_shift(value, k):
    return permute(value, "row", [(RING[p], RING[(p + k) % 16]) for p in range(16)])


def line_shift(value, k, swapped):
    pairs = []
    for i in range(16):
        for core in (0, 1):
            x, y = i // 4, i % 4
            x, y = (x, (y + k) % 4) if core ^ swapped else ((x + k) % 4, y)
            pairs.append((i * 2 + core, (x * 4 + y) * 2 + core))
    return permute(value, ("row", "layer"), pairs)


def z_swap(value, slot):
    pairs = [(z * 2 + h, (z ^ SLOTS[h][slot]) * 2 + h) for z in range(4) for h in (0, 1)]
    return permute(value, GROUP, pairs)


def slot_of(z, h, slot):
    first, second = SLOTS[0][slot], SLOTS[1][slot]
    return z ^ (first if first == second else jnp.where(h == 0, first, second))


def slot_with(apart, h):
    swapped = jnp.where(apart == 3, 1, jnp.where(apart == 1, 3, apart))
    apart = jnp.where(h == 0, apart, swapped)
    return jnp.where(apart == 2, 1, jnp.where(apart == 1, 2, apart))


def core_swap(value):
    return permute(value, "layer", [(0, 1), (1, 0)])


def low_half():
    return lax.broadcasted_iota(jnp.int32, (8, 128), 1) < 64


def swap_halves(tile):
    return pltpu.roll(tile, 64, 1)


def bit(tab, s, i, j):
    word = tab[BITS + s * 128 + i * 2 + lax.shift_right_logical(j, 5)]
    return lax.shift_right_logical(word, j & 31) & 1


def shifted(tiles, d, count):
    n = len(tiles)
    get = lambda seq, t: seq[t] if 0 <= t < n else None
    if d % 2 == 0:
        return [get(tiles, m - d // 2) for m in range(count)]
    q = (d - 1) // 2
    low = low_half()
    turned = [swap_halves(t) for t in tiles]
    out = []
    for m in range(count):
        a, b = get(turned, m - q - 1), get(turned, m - q)
        if a is None and b is None:
            out.append(None)
        else:
            zero = jnp.zeros((8, 128), F32)
            out.append(jnp.where(low, zero if a is None else a, zero if b is None else b))
    return out


def store_split(hi_ref, lo_ref, row, first, second):
    zero = jnp.zeros((8, 128), F32)
    for m, (a, b) in enumerate(zip(first, second)):
        both = jnp.concatenate([zero if a is None else a, zero if b is None else b], axis=0)
        hi = both.astype(BF16)
        hi_ref[row : row + 16, m * 128 : (m + 1) * 128] = hi
        lo_ref[row : row + 16, m * 128 : (m + 1) * 128] = (both - hi.astype(F32)).astype(BF16)


def tdot(a, b):
    return lax.dot_general(a, b, (((0,), (0,)), ((), ())), preferred_element_type=F32)


def product(hi_ref, lo_ref, start, width):
    xh = hi_ref[:, start : start + width]
    xl = lo_ref[:, start : start + width]
    zh = hi_ref[...]
    return tdot(xh, zh) + tdot(xh, lo_ref[...]) + tdot(xl, zh)


def call(kernel, outs, args, scratch=(), tab=None):
    vmem = pl.BlockSpec(memory_space=pltpu.VMEM)
    table = [] if tab is None else [pl.BlockSpec(memory_space=pltpu.SMEM)]
    return pl.pallas_call(
        kernel,
        out_shape=[jax.ShapeDtypeStruct(o, F32) for o in outs],
        in_specs=table + [vmem] * len(args),
        out_specs=[vmem] * len(outs),
        scratch_shapes=list(scratch),
        compiler_params=pltpu.CompilerParams(vmem_limit_bytes=48 * 1024 * 1024),
    )(*([] if tab is None else [tab]), *args)


def split_kernel(d_ref, own_ref, oth_ref):
    z, h = lax.axis_index("col"), lax.axis_index("layer")
    for k in range(4):
        for ref, core in ((own_ref, h), (oth_ref, 1 - h)):
            for e in range(4):
                start = pl.multiple_of(e * 64 + (2 * slot_of(z, core, k) + core) * 8, 8)
                rows = d_ref[pl.ds(start, 8), :]
                for t in range(4):
                    ref[k, e, t] = rows[:, t * 128 : (t + 1) * 128]


def pack_kernel(own_ref, got_ref, *outs):
    for k in range(4):
        outs[k][0] = own_ref[k]
        outs[k][1] = got_ref[k]


def compact_kernel(tab, *refs):
    ins, (keep_ref, out_ref, x_ref) = refs[:4], refs[4:]
    for k in range(4):
        x_ref[k] = ins[k][...]
    low = low_half()
    row0 = tab[PLACE] * 4
    z, h = tab[PLACE + 6], tab[PLACE + 4]
    for e in range(4):
        i = tab[PERM + row0 + e]
        halves = []
        for t in range(2 * BAND + 2):
            if t > 2 * BAND:
                halves.append(jnp.zeros((8, 128), F32))
                continue
            j = (i + t - BAND) & 63
            sj = tab[INV + j]
            tile = x_ref[slot_with((sj >> 4) ^ z, h), ((sj >> 3) & 1) ^ h, e, (sj & 7) >> 1]
            halves.append(jnp.where((sj & 1) == (t & 1), tile, swap_halves(tile)))
        for t in range(BAND + 1):
            out_ref[e, t] = jnp.where(low, halves[2 * t], halves[2 * t + 1]) * keep_ref[e, t]


def gather_rows(rows):
    near = [line_shift(rows, k, 0) for k in (1, 3, 2)]
    rows, *near = lax.optimization_barrier((rows, *near))
    line = jnp.stack([rows, near[0], near[2], near[1]])
    line = lax.optimization_barrier(line)
    far = [line_shift(line, k, 1) for k in (1, 3, 2)]
    line, *far = lax.optimization_barrier((line, *far))
    return [line, far[0], far[2], far[1]]


def collect(ins, g_ref):
    for n in range(4):
        g_ref[n] = ins[n][...]


def seat(tab, r, e):
    dx = (tab[PLACE + 2] - (r >> 2)) & 3
    dy = (tab[PLACE + 3] - (r & 3)) & 3
    first = tab[PLACE + 4] == 0
    return jnp.where(first, dy, dx), jnp.where(first, dx, dy), e


def write_slabs(p_ref, own_ref, oth_ref, e, base, d, tiles):
    z, h = lax.axis_index("col"), lax.axis_index("layer")
    low = low_half()
    for zz in range(4):
        for ref, core in ((own_ref, h), (oth_ref, 1 - h)):
            rows = p_ref[base + 2 * slot_of(z, core, zz) + core]
            if d % 2 == 0:
                for m in range(tiles):
                    at = (d // 2 + m) * 128
                    ref[zz, e, m] = rows[:, at : at + 128]
            else:
                q = d // 2
                turned = []
                for m in range(tiles + 1):
                    at = (q + m) * 128
                    if at < rows.shape[1]:
                        turned.append(swap_halves(rows[:, at : at + 128]))
                    else:
                        turned.append(jnp.zeros((8, 128), F32))
                for m in range(tiles):
                    ref[zz, e, m] = jnp.where(low, turned[m], turned[m + 1])


def geometry(w):
    left = w + 1 + (w + 1) % 2
    return left, (left + 4 + w + 1 + 1) // 2


def step_body(strips, w, own_ref, oth_ref, hi_ref, lo_ref, p_ref):
    left, count = geometry(w)
    nk = 4 + 2 * w
    for a in range(0, nk, 2):
        pair = []
        for b in (a, a + 1):
            tiles, first = strips(b)
            pair.append(shifted(tiles, left - 2 * w + b + 2 * first, count))
        store_split(hi_ref, lo_ref, a * 8, pair[0], pair[1])
    p_ref[...] = product(hi_ref, lo_ref, left * 64, 256).reshape(32, 8, count * 128)
    for e in range(4):
        write_slabs(p_ref, own_ref, oth_ref, e, e * 8, left - (w + 1) + e, w + 2)


def first_step_kernel(tab, *refs):
    ins, (own_ref, oth_ref, cur_ref, hi_ref, lo_ref, p_ref, g_ref) = refs[:4], refs[4:]
    collect(ins, g_ref)
    w = BAND
    base = tab[PLACE + 5] * 4 + 64 - w

    def strips(b):
        sk = tab[INV + ((base + b) & 63)]
        u, v, e = seat(tab, sk >> 2, sk & 3)
        strip = g_ref[u, v, e]
        if w <= b < w + 4:
            cur_ref[b - w] = strip
        return [strip[t] for t in range(w + 1)], 0

    step_body(strips, w, own_ref, oth_ref, hi_ref, lo_ref, p_ref)


def step_kernel(w, pieces, *refs):
    n = 1 + len(pieces)
    ins, (own_ref, oth_ref, hi_ref, lo_ref, p_ref) = refs[:n], refs[n:]

    def strips(b):
        off = b - w
        if 0 <= off < 4:
            return [ins[0][off, t] for t in range(w + 1)], 0
        d = (-off + 3) // 4 if off < 0 else -(off // 4)
        at = [piece[0] for piece in pieces].index(d)
        _, (lo, hi, first, last) = pieces[at]
        row = off + 4 * d - lo
        return [ins[1 + at][row, t] for t in range(last - first)], first

    step_body(strips, w, own_ref, oth_ref, hi_ref, lo_ref, p_ref)


def halo_pieces(w):
    out = []
    for d in range(1, (w + 3) // 4 + 1):
        n = min(4, w - 4 * (d - 1))
        out.append((d, (4 - n, 4, 2 * (d - 1), w + 1)))
        out.append((-d, (0, n, 0, w + 1 - 2 * (d - 1))))
    return out


def last_step_kernel(tab, *refs):
    ins, (own_ref, oth_ref, cur_ref, hi_ref, lo_ref, p_ref, g_ref) = refs[:4], refs[4:]
    collect(ins, g_ref)
    w = BAND + STEPS - 1
    row0 = tab[PLACE] * 4
    left, count = w + 2, w + 2
    for e in range(4):
        i = tab[PERM + row0 + e]

        def strips(b):
            k = (i + b - w) & 63
            pos = k >> 2
            a, odd = pos >> 1, pos & 1
            r = jnp.where(a < 4, a * 4 + odd, (7 - a) * 4 + 3 - odd)
            u, v, ee = seat(tab, r, k & 3)
            strip = g_ref[u, v, ee]
            if b == w:
                cur_ref[e] = strip
            return [strip[t] for t in range(w + 1)]

        for a in range(0, 2 * w + 2, 2):
            one = shifted(strips(a), left - 2 * w + a, count)
            two = [None] * count
            if a + 1 <= 2 * w:
                two = shifted(strips(a + 1), left - 2 * w + a + 1, count)
            store_split(hi_ref, lo_ref, a * 8, one, two)
        p_ref[...] = product(hi_ref, lo_ref, left * 64, 64).reshape(8, 8, count * 128)
        write_slabs(p_ref, own_ref, oth_ref, e, 0, 0, count)


def pair_kernel(own_ref, got_ref, *outs):
    for k in range(4):
        outs[k][...] = own_ref[k] + got_ref[k]


def total(parts, e, m):
    return (parts[0][e, m] + parts[1][e, m]) + (parts[2][e, m] + parts[3][e, m])


def polynomial(coef_ref, step, cur, square):
    return coef_ref[step, 0] * cur + coef_ref[step, 1] * square


def keep_kernel(tab, *refs):
    low = low_half()
    refs, coef_ref = refs[:-1], refs[-1]
    for s in range(STEPS):
        twice = tab[BRANCH + s] == 1
        coef_ref[s, 0] = jnp.full((8, 128), jnp.where(twice, 2.0, 0.0), F32)
        coef_ref[s, 1] = jnp.full((8, 128), jnp.where(twice, -1.0, 1.0), F32)
    for s, ref in enumerate(refs):
        w = BAND + s
        margin = w + 1 if s == STEPS else w
        for e in range(4):
            i = tab[PLACE + 5] * 4 + e if 0 < s < STEPS else tab[PERM + tab[PLACE] * 4 + e]
            for m in range(ref.shape[1]):
                sides = []
                for v in (2 * m - margin, 2 * m + 1 - margin):
                    sides.append(bit(tab, s, i, (i + v + 64) & 63) if -w <= v <= w else 0)
                ref[e, m] = jnp.where(low, sides[0], sides[1]).astype(F32)


def close_kernel(step, cuts, p0, p1, p2, p3, cur_ref, keep_ref, coef_ref, *refs):
    w = BAND + step
    low = low_half()
    for e in range(4):
        turned = [swap_halves(cur_ref[e, t]) for t in range(w + 1)]
        zero = jnp.zeros((8, 128), F32)
        for m in range(w + 2):
            before = turned[m - 1] if m >= 1 else zero
            after = turned[m] if m <= w else zero
            cur = jnp.where(low, before, after)
            square = total((p0, p1, p2, p3), e, m)
            value = polynomial(coef_ref, step, cur, square) * keep_ref[e, m]
            for ref, (lo, hi, first, last) in zip(refs, cuts):
                if lo <= e < hi and first <= m < last:
                    ref[e - lo, m - first] = value


def finish_kernel(tab, p0, p1, p2, p3, cur_ref, keep_ref, coef_ref, own_ref, oth_ref, y_ref):
    w = BAND + STEPS - 1
    low = low_half()
    row0 = tab[PLACE] * 4
    z, h = tab[PLACE + 6], tab[PLACE + 4]
    y_ref[...] = jnp.zeros_like(y_ref)
    for e in range(4):
        i = tab[PERM + row0 + e]
        for m in range(w + 2):
            cur = cur_ref[e, m - 1] if 1 <= m <= w + 1 else jnp.zeros((8, 128), F32)
            square = total((p0, p1, p2, p3), e, m)
            value = polynomial(coef_ref, STEPS - 1, cur, square) * keep_ref[e, m]
            turned = swap_halves(value)
            for half in (0, 1):
                v = 2 * m + half
                if v == 0:
                    continue
                j = (i + v + 64 - (w + 2)) & 63
                sj = tab[INV + j]
                odd = sj & 1
                piece = jnp.where(odd == half, value, turned)
                side = jnp.where(low, 0, 1) == odd
                core = (sj >> 3) & 1
                at = core ^ h, slot_with((sj >> 4) ^ z, core), e, (sj & 7) >> 1
                y_ref[at] = jnp.where(side, piece, y_ref[at])
    own_ref[...] = y_ref[0]
    oth_ref[...] = y_ref[1]


def join_kernel(y0, y1, y2, y3, out_ref):
    z, h = lax.axis_index("col"), lax.axis_index("layer")
    for k, y_ref in enumerate((y0, y1, y2, y3)):
        for core in (0, 1):
            for e in range(4):
                start = pl.multiple_of(e * 64 + (2 * slot_of(z, h, k) + (core ^ h)) * 8, 8)
                for t in range(4):
                    out_ref[pl.ds(start, 8), t * 128 : (t + 1) * 128] = y_ref[core, e, t]


def tables(masks, branch, perm):
    r = lax.axis_index("row")
    z = lax.axis_index("col")
    h = lax.axis_index("layer")
    ids = jnp.arange(64, dtype=jnp.int32)
    inverse = jnp.sum(jnp.where(perm[:, None] == ids[None, :], ids[:, None], 0), axis=0)
    shifts = jnp.arange(32, dtype=jnp.int32)
    bits = jnp.sum(masks.reshape(6, 64, 2, 32) << shifts, axis=-1, dtype=jnp.int32)
    pos = jnp.sum(jnp.where(jnp.asarray(RING) == r, jnp.arange(16), 0))
    place = jnp.stack([r, z * 2 + h, r // 4, r % 4, h, pos, z, z]).astype(jnp.int32)
    return jnp.concatenate(
        [perm, inverse.astype(jnp.int32), branch, jnp.zeros((3,), jnp.int32), bits.reshape(-1), place]
    )


def z_exchange(parts):
    return [parts[0]] + [z_swap(parts[k], k) for k in (1, 2, 3)]


def reduce_group(own, oth):
    return z_exchange(call(pair_kernel, [own.shape[1:]] * 4, [own, core_swap(oth)]))


def spread_group(own, oth):
    shape = (2,) + own.shape[1:]
    return z_exchange(call(pack_kernel, [shape] * 4, [own, core_swap(oth)]))


def shards(density, masks, branch, perm):
    slabs = (4, 4, 4, 8, 128)
    split = spread_group(*call(split_kernel, [slabs] * 2, [density]))
    tab = tables(masks, branch, perm)
    tiles = [BAND + s + 1 for s in range(STEPS)] + [BAND + STEPS + 1]
    shapes = [(4, n, 8, 128) for n in tiles] + [(STEPS, 2, 8, 128)]
    *keep, coef = call(keep_kernel, shapes, [], tab=tab)
    (rows,) = call(
        compact_kernel,
        [(4, BAND + 1, 8, 128)],
        split + [keep[0]],
        [pltpu.VMEM((4, 2, 4, 4, 8, 128), F32)],
        tab=tab,
    )
    gathered = gather_rows(rows)
    for step in range(STEPS - 1):
        w = BAND + step
        left, count = geometry(w)
        depth = (4 + 2 * w) * 8
        part = (4, 4, w + 2, 8, 128)
        scratch = [
            pltpu.VMEM((depth, count * 128), BF16),
            pltpu.VMEM((depth, count * 128), BF16),
            pltpu.VMEM((32, 8, count * 128), F32),
        ]
        if step == 0:
            scratch.append(pltpu.VMEM((4, 4, 4, w + 1, 8, 128), F32))
            own, oth, cur = call(
                first_step_kernel, [part, part, (4, w + 1, 8, 128)], gathered, scratch, tab=tab
            )
        else:
            kernel = lambda *refs, w=w, pieces=pieces: step_kernel(w, pieces, *refs)
            own, oth = call(kernel, [part, part], [cur] + around, scratch)
        parts = reduce_group(own, oth)
        pieces = halo_pieces(w + 1) if step < STEPS - 2 else []
        cuts = [(0, 4, 0, w + 2)]
        for _, cut in pieces:
            if cut not in cuts:
                cuts.append(cut)
        kernel = lambda *refs, step=step, cuts=cuts: close_kernel(step, cuts, *refs)
        shapes = [(hi - lo, last - first, 8, 128) for lo, hi, first, last in cuts]
        sent = call(kernel, shapes, parts + [cur, keep[step + 1], coef])
        cur = sent[0]
        around = [ring_shift(sent[cuts.index(cut)], d) for d, cut in pieces]
        cur, *around = lax.optimization_barrier((cur, *around))
    gathered = gather_rows(cur)
    w = BAND + STEPS - 1
    part = (4, 4, w + 2, 8, 128)
    scratch = [
        pltpu.VMEM(((2 * w + 2) * 8, (w + 2) * 128), BF16),
        pltpu.VMEM(((2 * w + 2) * 8, (w + 2) * 128), BF16),
        pltpu.VMEM((8, 8, (w + 2) * 128), F32),
        pltpu.VMEM((4, 4, 4, w + 1, 8, 128), F32),
    ]
    own, oth, cur = call(
        last_step_kernel, [part, part, (4, w + 1, 8, 128)], gathered, scratch, tab=tab
    )
    parts = reduce_group(own, oth)
    own, oth = call(
        finish_kernel, [slabs] * 2, parts + [cur, keep[STEPS], coef], [pltpu.VMEM((2,) + slabs, F32)], tab=tab
    )
    (out,) = call(join_kernel, [(256, 512)], spread_group(own, oth))
    return out


def solution(mesh):
    return jax.shard_map(
        shards,
        mesh=mesh,
        in_specs=(P("row", GROUP), P(), P(), P()),
        out_specs=P("row", GROUP),
        check_vma=False,
    )
```

```python
import jax
import jax.numpy as jnp
from jax import lax
from jax.experimental import pallas as pl
from jax.experimental.pallas import tpu as pltpu
from jax.sharding import PartitionSpec as P

STEPS = 5
BAND = 6
NB = 64
GROUP = ("col", "layer")
PERM, INV, BRANCH, BITS, PLACE = 0, 64, 128, 136, 136 + 6 * 128
F32, BF16 = jnp.float32, jnp.bfloat16


def ring_xy(pos):
    a, b = pos // 2, pos % 2
    return (a, b) if a < 4 else (7 - a, 3 - b)


RING = [ring_xy(p)[0] * 4 + ring_xy(p)[1] for p in range(16)]


SLOTS = ((0, 2, 1, 3), (0, 2, 3, 1))


def permute(value, axes, pairs):
    flat = value.reshape(-1, 128)
    return lax.ppermute(flat, axes, pairs).reshape(value.shape)


def ring_shift(value, k):
    return permute(value, "row", [(RING[p], RING[(p + k) % 16]) for p in range(16)])


def outward(value, d):
    pairs = []
    for p in range(16):
        pairs.append((RING[p] * 2, RING[(p + d) % 16] * 2))
        pairs.append((RING[p] * 2 + 1, RING[(p - d) % 16] * 2 + 1))
    return permute(value, ("row", "layer"), pairs)


def line_shift(value, k, swapped):
    pairs = []
    for i in range(16):
        for core in (0, 1):
            x, y = i // 4, i % 4
            x, y = (x, (y + k) % 4) if core ^ swapped else ((x + k) % 4, y)
            pairs.append((i * 2 + core, (x * 4 + y) * 2 + core))
    return permute(value, ("row", "layer"), pairs)


def z_swap(value, slot):
    pairs = [(z * 2 + h, (z ^ SLOTS[h][slot]) * 2 + h) for z in range(4) for h in (0, 1)]
    return permute(value, GROUP, pairs)


def slot_of(z, h, slot):
    first, second = SLOTS[0][slot], SLOTS[1][slot]
    return z ^ (first if first == second else jnp.where(h == 0, first, second))


def slot_with(apart, h):
    swapped = jnp.where(apart == 3, 1, jnp.where(apart == 1, 3, apart))
    apart = jnp.where(h == 0, apart, swapped)
    return jnp.where(apart == 2, 1, jnp.where(apart == 1, 2, apart))


def core_swap(value):
    return permute(value, "layer", [(0, 1), (1, 0)])


def low_half():
    return lax.broadcasted_iota(jnp.int32, (8, 128), 1) < 64


def swap_halves(tile):
    return pltpu.roll(tile, 64, 1)


def bit(tab, s, i, j):
    word = tab[BITS + s * 128 + i * 2 + lax.shift_right_logical(j, 5)]
    return lax.shift_right_logical(word, j & 31) & 1


def shifted(tiles, d, count):
    n = len(tiles)
    get = lambda seq, t: seq[t] if 0 <= t < n else None
    if d % 2 == 0:
        return [get(tiles, m - d // 2) for m in range(count)]
    q = (d - 1) // 2
    low = low_half()
    turned = [swap_halves(t) for t in tiles]
    out = []
    for m in range(count):
        a, b = get(turned, m - q - 1), get(turned, m - q)
        if a is None and b is None:
            out.append(None)
        else:
            zero = jnp.zeros((8, 128), F32)
            out.append(jnp.where(low, zero if a is None else a, zero if b is None else b))
    return out


def store_split(hi_ref, lo_ref, row, first, second):
    zero = jnp.zeros((8, 128), F32)
    for m, (a, b) in enumerate(zip(first, second)):
        both = jnp.concatenate([zero if a is None else a, zero if b is None else b], axis=0)
        hi = both.astype(BF16)
        hi_ref[row : row + 16, m * 128 : (m + 1) * 128] = hi
        lo_ref[row : row + 16, m * 128 : (m + 1) * 128] = (both - hi.astype(F32)).astype(BF16)


def tdot(a, b):
    return lax.dot_general(a, b, (((0,), (0,)), ((), ())), preferred_element_type=F32)


def product(hi_ref, lo_ref, start, width):
    xh = hi_ref[:, start : start + width]
    xl = lo_ref[:, start : start + width]
    zh = hi_ref[...]
    return tdot(xh, zh) + tdot(xh, lo_ref[...]) + tdot(xl, zh)


def call(kernel, outs, args, scratch=(), tab=None):
    vmem = pl.BlockSpec(memory_space=pltpu.VMEM)
    table = [] if tab is None else [pl.BlockSpec(memory_space=pltpu.SMEM)]
    return pl.pallas_call(
        kernel,
        out_shape=[jax.ShapeDtypeStruct(o, F32) for o in outs],
        in_specs=table + [vmem] * len(args),
        out_specs=[vmem] * len(outs),
        scratch_shapes=list(scratch),
        compiler_params=pltpu.CompilerParams(vmem_limit_bytes=48 * 1024 * 1024),
    )(*([] if tab is None else [tab]), *args)


def split_kernel(d_ref, own_ref, oth_ref):
    z, h = lax.axis_index("col"), lax.axis_index("layer")
    for k in range(4):
        for ref, core in ((own_ref, h), (oth_ref, 1 - h)):
            for e in range(4):
                start = pl.multiple_of(e * 64 + (2 * slot_of(z, core, k) + core) * 8, 8)
                rows = d_ref[pl.ds(start, 8), :]
                for t in range(4):
                    ref[k, e, t] = rows[:, t * 128 : (t + 1) * 128]


def pack_kernel(own_ref, got_ref, *outs):
    for k in range(4):
        outs[k][0] = own_ref[k]
        outs[k][1] = got_ref[k]


def compact_kernel(tab, *refs):
    ins, (keep_ref, out_ref, x_ref) = refs[:4], refs[4:]
    for k in range(4):
        x_ref[k] = ins[k][...]
    low = low_half()
    row0 = tab[PLACE] * 4
    z, h = tab[PLACE + 6], tab[PLACE + 4]
    for e in range(4):
        i = tab[PERM + row0 + e]
        halves = []
        for t in range(2 * BAND + 2):
            if t > 2 * BAND:
                halves.append(jnp.zeros((8, 128), F32))
                continue
            j = (i + t - BAND) & 63
            sj = tab[INV + j]
            tile = x_ref[slot_with((sj >> 4) ^ z, h), ((sj >> 3) & 1) ^ h, e, (sj & 7) >> 1]
            halves.append(jnp.where((sj & 1) == (t & 1), tile, swap_halves(tile)))
        for t in range(BAND + 1):
            out_ref[e, t] = jnp.where(low, halves[2 * t], halves[2 * t + 1]) * keep_ref[e, t]


def gather_rows(rows):
    near = [line_shift(rows, k, 0) for k in (1, 3, 2)]
    rows, *near = lax.optimization_barrier((rows, *near))
    line = jnp.stack([rows, near[0], near[2], near[1]])
    line = lax.optimization_barrier(line)
    far = [line_shift(line, k, 1) for k in (1, 3, 2)]
    line, *far = lax.optimization_barrier((line, *far))
    return [line, far[0], far[2], far[1]]


def collect(ins, g_ref):
    for n in range(4):
        g_ref[n] = ins[n][...]


def seat(tab, r, e):
    dx = (tab[PLACE + 2] - (r >> 2)) & 3
    dy = (tab[PLACE + 3] - (r & 3)) & 3
    first = tab[PLACE + 4] == 0
    return jnp.where(first, dy, dx), jnp.where(first, dx, dy), e


def write_slabs(p_ref, own_ref, oth_ref, e, base, d, tiles):
    z, h = lax.axis_index("col"), lax.axis_index("layer")
    low = low_half()
    for zz in range(4):
        for ref, core in ((own_ref, h), (oth_ref, 1 - h)):
            rows = p_ref[base + 2 * slot_of(z, core, zz) + core]
            if d % 2 == 0:
                for m in range(tiles):
                    at = (d // 2 + m) * 128
                    ref[zz, e, m] = rows[:, at : at + 128]
            else:
                q = d // 2
                turned = []
                for m in range(tiles + 1):
                    at = (q + m) * 128
                    if at < rows.shape[1]:
                        turned.append(swap_halves(rows[:, at : at + 128]))
                    else:
                        turned.append(jnp.zeros((8, 128), F32))
                for m in range(tiles):
                    ref[zz, e, m] = jnp.where(low, turned[m], turned[m + 1])


def geometry(w):
    left = w + 1 + (w + 1) % 2
    return left, (left + 4 + w + 1 + 1) // 2


def step_body(strips, w, own_ref, oth_ref, hi_ref, lo_ref, p_ref):
    left, count = geometry(w)
    for a in range(0, len(strips), 2):
        pair = []
        for strip in strips[a : a + 2]:
            b, tiles, first = strip()
            pair.append(shifted(tiles, left - 2 * w + b + 2 * first, count))
        store_split(hi_ref, lo_ref, a * 8, pair[0], pair[1])
    p_ref[...] = product(hi_ref, lo_ref, left * 64, 256).reshape(32, 8, count * 128)
    for e in range(4):
        write_slabs(p_ref, own_ref, oth_ref, e, e * 8, left - (w + 1) + e, w + 2)


def first_step_kernel(tab, *refs):
    ins, (own_ref, oth_ref, cur_ref, hi_ref, lo_ref, p_ref, g_ref) = refs[:4], refs[4:]
    collect(ins, g_ref)
    w = BAND
    base = tab[PLACE + 5] * 4 + 64 - w

    def strip_of(b):
        sk = tab[INV + ((base + b) & 63)]
        u, v, e = seat(tab, sk >> 2, sk & 3)
        strip = g_ref[u, v, e]
        if w <= b < w + 4:
            cur_ref[b - w] = strip
        return b, [strip[t] for t in range(w + 1)], 0

    strips = [lambda b=b: strip_of(b) for b in range(4 + 2 * w)]
    step_body(strips, w, own_ref, oth_ref, hi_ref, lo_ref, p_ref)


def step_kernel(w, pieces, *refs):
    far = outermost(w) is not None
    n = 1 + len(pieces) + far
    ins, (own_ref, oth_ref, hi_ref, lo_ref, p_ref) = refs[:n], refs[n:]

    def strip_of(b):
        off = b - w
        if 0 <= off < 4:
            return b, [ins[0][off, t] for t in range(w + 1)], 0
        d = (-off + 3) // 4 if off < 0 else -(off // 4)
        at = [piece[0] for piece in pieces].index(d)
        _, (lo, hi, first, last) = pieces[at]
        row = off + 4 * d - lo
        return b, [ins[1 + at][row, t] for t in range(last - first)], first

    def far_strip(b, core, slab):
        mine = jnp.where(lax.axis_index("layer") == core, 1.0, 0.0)
        first = 0 if core else w + 1 - far_tiles(w)
        return b, [ins[-1][slab, t] * mine for t in range(far_tiles(w))], first

    last = 4 + 2 * w - 1
    strips = [lambda b=b: strip_of(b) for b in range(far, last + 1 - far)]
    if far:
        for slab in (0, 1):
            strips.append(lambda slab=slab: far_strip(0, 0, slab))
            strips.append(lambda slab=slab: far_strip(last, 1, slab))
    step_body(strips, w, own_ref, oth_ref, hi_ref, lo_ref, p_ref)


def far_tiles(w):
    return w + 1 - 2 * (outermost(w) - 1)


def outermost(w):
    return (w + 3) // 4 if w % 4 == 1 else None


def halo_pieces(w):
    out = []
    for d in range(1, (w + 3) // 4 + 1):
        n = min(4, w - 4 * (d - 1))
        if outermost(w) == d:
            break
        out.append((d, (4 - n, 4, 2 * (d - 1), w + 1)))
        out.append((-d, (0, n, 0, w + 1 - 2 * (d - 1))))
    return out


def last_step_kernel(tab, *refs):
    ins, (own_ref, oth_ref, cur_ref, hi_ref, lo_ref, p_ref, g_ref) = refs[:4], refs[4:]
    collect(ins, g_ref)
    w = BAND + STEPS - 1
    row0 = tab[PLACE] * 4
    left, count = w + 2, w + 2
    for e in range(4):
        i = tab[PERM + row0 + e]

        def strips(b):
            k = (i + b - w) & 63
            pos = k >> 2
            a, odd = pos >> 1, pos & 1
            r = jnp.where(a < 4, a * 4 + odd, (7 - a) * 4 + 3 - odd)
            u, v, ee = seat(tab, r, k & 3)
            strip = g_ref[u, v, ee]
            if b == w:
                cur_ref[e] = strip
            return [strip[t] for t in range(w + 1)]

        for a in range(0, 2 * w + 2, 2):
            one = shifted(strips(a), left - 2 * w + a, count)
            two = [None] * count
            if a + 1 <= 2 * w:
                two = shifted(strips(a + 1), left - 2 * w + a + 1, count)
            store_split(hi_ref, lo_ref, a * 8, one, two)
        p_ref[...] = product(hi_ref, lo_ref, left * 64, 64).reshape(8, 8, count * 128)
        write_slabs(p_ref, own_ref, oth_ref, e, 0, 0, count)


def pair_kernel(own_ref, got_ref, *outs):
    for k in range(4):
        outs[k][...] = own_ref[k] + got_ref[k]


def total(parts, e, m):
    return (parts[0][e, m] + parts[1][e, m]) + (parts[2][e, m] + parts[3][e, m])


def polynomial(coef_ref, step, cur, square):
    return coef_ref[step, 0] * cur + coef_ref[step, 1] * square


def keep_kernel(tab, *refs):
    low = low_half()
    refs, coef_ref = refs[:-1], refs[-1]
    for s in range(STEPS):
        twice = tab[BRANCH + s] == 1
        coef_ref[s, 0] = jnp.full((8, 128), jnp.where(twice, 2.0, 0.0), F32)
        coef_ref[s, 1] = jnp.full((8, 128), jnp.where(twice, -1.0, 1.0), F32)
    for s, ref in enumerate(refs):
        w = BAND + s
        margin = w + 1 if s == STEPS else w
        for e in range(4):
            i = tab[PLACE + 5] * 4 + e if 0 < s < STEPS else tab[PERM + tab[PLACE] * 4 + e]
            for m in range(ref.shape[1]):
                sides = []
                for v in (2 * m - margin, 2 * m + 1 - margin):
                    sides.append(bit(tab, s, i, (i + v + 64) & 63) if -w <= v <= w else 0)
                ref[e, m] = jnp.where(low, sides[0], sides[1]).astype(F32)


def close_kernel(step, cuts, far, p0, p1, p2, p3, cur_ref, keep_ref, coef_ref, *refs):
    w = BAND + step
    low = low_half()
    for e in range(4):
        turned = [swap_halves(cur_ref[e, t]) for t in range(w + 1)]
        zero = jnp.zeros((8, 128), F32)
        for m in range(w + 2):
            before = turned[m - 1] if m >= 1 else zero
            after = turned[m] if m <= w else zero
            cur = jnp.where(low, before, after)
            square = total((p0, p1, p2, p3), e, m)
            value = polynomial(coef_ref, step, cur, square) * keep_ref[e, m]
            for ref, (lo, hi, first, last) in zip(refs, cuts):
                if lo <= e < hi and first <= m < last:
                    ref[e - lo, m - first] = value
            if far and e == 3 and m >= w + 2 - far:
                refs[-1][0, m - (w + 2 - far)] = value
            if far and e == 0 and m < far:
                refs[-1][1, m] = value
    if far:
        own_ref, oth_ref, far_ref = refs[-3:]
        own_ref[...] = far_ref[lax.axis_index("layer")]
        oth_ref[...] = far_ref[1 - lax.axis_index("layer")]


def finish_kernel(tab, p0, p1, p2, p3, cur_ref, keep_ref, coef_ref, own_ref, oth_ref, y_ref):
    w = BAND + STEPS - 1
    low = low_half()
    row0 = tab[PLACE] * 4
    z, h = tab[PLACE + 6], tab[PLACE + 4]
    y_ref[...] = jnp.zeros_like(y_ref)
    for e in range(4):
        i = tab[PERM + row0 + e]
        for m in range(w + 2):
            cur = cur_ref[e, m - 1] if 1 <= m <= w + 1 else jnp.zeros((8, 128), F32)
            square = total((p0, p1, p2, p3), e, m)
            value = polynomial(coef_ref, STEPS - 1, cur, square) * keep_ref[e, m]
            turned = swap_halves(value)
            for half in (0, 1):
                v = 2 * m + half
                if v == 0:
                    continue
                j = (i + v + 64 - (w + 2)) & 63
                sj = tab[INV + j]
                odd = sj & 1
                piece = jnp.where(odd == half, value, turned)
                side = jnp.where(low, 0, 1) == odd
                core = (sj >> 3) & 1
                at = core ^ h, slot_with((sj >> 4) ^ z, core), e, (sj & 7) >> 1
                y_ref[at] = jnp.where(side, piece, y_ref[at])
    own_ref[...] = y_ref[0]
    oth_ref[...] = y_ref[1]


def join_kernel(y0, y1, y2, y3, out_ref):
    z, h = lax.axis_index("col"), lax.axis_index("layer")
    for k, y_ref in enumerate((y0, y1, y2, y3)):
        for core in (0, 1):
            for e in range(4):
                start = pl.multiple_of(e * 64 + (2 * slot_of(z, h, k) + (core ^ h)) * 8, 8)
                for t in range(4):
                    out_ref[pl.ds(start, 8), t * 128 : (t + 1) * 128] = y_ref[core, e, t]


def tables(masks, branch, perm):
    r = lax.axis_index("row")
    z = lax.axis_index("col")
    h = lax.axis_index("layer")
    ids = jnp.arange(64, dtype=jnp.int32)
    inverse = jnp.sum(jnp.where(perm[:, None] == ids[None, :], ids[:, None], 0), axis=0)
    shifts = jnp.arange(32, dtype=jnp.int32)
    bits = jnp.sum(masks.reshape(6, 64, 2, 32) << shifts, axis=-1, dtype=jnp.int32)
    pos = jnp.sum(jnp.where(jnp.asarray(RING) == r, jnp.arange(16), 0))
    place = jnp.stack([r, z * 2 + h, r // 4, r % 4, h, pos, z, z]).astype(jnp.int32)
    return jnp.concatenate(
        [perm, inverse.astype(jnp.int32), branch, jnp.zeros((3,), jnp.int32), bits.reshape(-1), place]
    )


def z_exchange(parts):
    return [parts[0]] + [z_swap(parts[k], k) for k in (1, 2, 3)]


def reduce_group(own, oth):
    return z_exchange(call(pair_kernel, [own.shape[1:]] * 4, [own, core_swap(oth)]))


def spread_group(own, oth):
    shape = (2,) + own.shape[1:]
    return z_exchange(call(pack_kernel, [shape] * 4, [own, core_swap(oth)]))


def shards(density, masks, branch, perm):
    slabs = (4, 4, 4, 8, 128)
    split = spread_group(*call(split_kernel, [slabs] * 2, [density]))
    tab = tables(masks, branch, perm)
    tiles = [BAND + s + 1 for s in range(STEPS)] + [BAND + STEPS + 1]
    shapes = [(4, n, 8, 128) for n in tiles] + [(STEPS, 2, 8, 128)]
    *keep, coef = call(keep_kernel, shapes, [], tab=tab)
    (rows,) = call(
        compact_kernel,
        [(4, BAND + 1, 8, 128)],
        split + [keep[0]],
        [pltpu.VMEM((4, 2, 4, 4, 8, 128), F32)],
        tab=tab,
    )
    gathered = gather_rows(rows)
    for step in range(STEPS - 1):
        w = BAND + step
        left, count = geometry(w)
        depth = (4 + 2 * w + (2 if step and outermost(w) else 0)) * 8
        part = (4, 4, w + 2, 8, 128)
        scratch = [
            pltpu.VMEM((depth, count * 128), BF16),
            pltpu.VMEM((depth, count * 128), BF16),
            pltpu.VMEM((32, 8, count * 128), F32),
        ]
        if step == 0:
            scratch.append(pltpu.VMEM((4, 4, 4, w + 1, 8, 128), F32))
            own, oth, cur = call(
                first_step_kernel, [part, part, (4, w + 1, 8, 128)], gathered, scratch, tab=tab
            )
        else:
            kernel = lambda *refs, w=w, pieces=pieces: step_kernel(w, pieces, *refs)
            own, oth = call(kernel, [part, part], [cur] + around, scratch)
        parts = reduce_group(own, oth)
        pieces = halo_pieces(w + 1) if step < STEPS - 2 else []
        cuts = [(0, 4, 0, w + 2)]
        for _, cut in pieces:
            if cut not in cuts:
                cuts.append(cut)
        far = far_tiles(w + 1) if pieces and outermost(w + 1) else 0
        kernel = lambda *refs, step=step, cuts=cuts, far=far: close_kernel(step, cuts, far, *refs)
        shapes = [(hi - lo, last - first, 8, 128) for lo, hi, first, last in cuts]
        scratch = [pltpu.VMEM((2, far, 8, 128), F32)] if far else []
        shapes += [(far, 8, 128)] * 2 if far else []
        sent = call(kernel, shapes, parts + [cur, keep[step + 1], coef], scratch)
        cur = sent[0]
        around = [ring_shift(sent[cuts.index(cut)], d) for d, cut in pieces]
        if far:
            both = jnp.stack([sent[-2], core_swap(sent[-1])])
            around.append(outward(both, outermost(w + 1)))
        cur, *around = lax.optimization_barrier((cur, *around))
    gathered = gather_rows(cur)
    w = BAND + STEPS - 1
    part = (4, 4, w + 2, 8, 128)
    scratch = [
        pltpu.VMEM(((2 * w + 2) * 8, (w + 2) * 128), BF16),
        pltpu.VMEM(((2 * w + 2) * 8, (w + 2) * 128), BF16),
        pltpu.VMEM((8, 8, (w + 2) * 128), F32),
        pltpu.VMEM((4, 4, 4, w + 1, 8, 128), F32),
    ]
    own, oth, cur = call(
        last_step_kernel, [part, part, (4, w + 1, 8, 128)], gathered, scratch, tab=tab
    )
    parts = reduce_group(own, oth)
    own, oth = call(
        finish_kernel, [slabs] * 2, parts + [cur, keep[STEPS], coef], [pltpu.VMEM((2,) + slabs, F32)], tab=tab
    )
    (out,) = call(join_kernel, [(256, 512)], spread_group(own, oth))
    return out


def solution(mesh):
    return jax.shard_map(
        shards,
        mesh=mesh,
        in_specs=(P("row", GROUP), P(), P(), P()),
        out_specs=P("row", GROUP),
        check_vma=False,
    )
```

```python
import jax
import jax.numpy as jnp
from jax import lax
from jax.experimental import pallas as pl
from jax.experimental.pallas import tpu as pltpu
from jax.sharding import PartitionSpec as P

STEPS = 5
BAND = 6
NB = 64
GROUP = ("col", "layer")
PERM, INV, BRANCH, BITS, PLACE = 0, 64, 128, 136, 136 + 6 * 128
F32, BF16 = jnp.float32, jnp.bfloat16


def ring_xy(pos):
    a, b = pos // 2, pos % 2
    return (a, b) if a < 4 else (7 - a, 3 - b)


RING = [ring_xy(p)[0] * 4 + ring_xy(p)[1] for p in range(16)]


SLOTS = ((0, 2, 1, 3), (0, 2, 3, 1))


def permute(value, axes, pairs):
    flat = value.reshape(-1, 128)
    return lax.ppermute(flat, axes, pairs).reshape(value.shape)


def ring_shift(value, k):
    return permute(value, "row", [(RING[p], RING[(p + k) % 16]) for p in range(16)])


def outward(value, d):
    pairs = []
    for p in range(16):
        pairs.append((RING[p] * 2, RING[(p + d) % 16] * 2))
        pairs.append((RING[p] * 2 + 1, RING[(p - d) % 16] * 2 + 1))
    return permute(value, ("row", "layer"), pairs)


def line_shift(value, k, swapped):
    pairs = []
    for i in range(16):
        for core in (0, 1):
            x, y = i // 4, i % 4
            x, y = (x, (y + k) % 4) if core ^ swapped else ((x + k) % 4, y)
            pairs.append((i * 2 + core, (x * 4 + y) * 2 + core))
    return permute(value, ("row", "layer"), pairs)


def z_swap(value, slot):
    pairs = [(z * 2 + h, (z ^ SLOTS[h][slot]) * 2 + h) for z in range(4) for h in (0, 1)]
    return permute(value, GROUP, pairs)


def slot_of(z, h, slot):
    first, second = SLOTS[0][slot], SLOTS[1][slot]
    return z ^ (first if first == second else jnp.where(h == 0, first, second))


def slot_with(apart, h):
    swapped = jnp.where(apart == 3, 1, jnp.where(apart == 1, 3, apart))
    apart = jnp.where(h == 0, apart, swapped)
    return jnp.where(apart == 2, 1, jnp.where(apart == 1, 2, apart))


def core_swap(value):
    return permute(value, "layer", [(0, 1), (1, 0)])


def low_half():
    return lax.broadcasted_iota(jnp.int32, (8, 128), 1) < 64


def swap_halves(tile):
    return pltpu.roll(tile, 64, 1)


def bit(tab, s, i, j):
    word = tab[BITS + s * 128 + i * 2 + lax.shift_right_logical(j, 5)]
    return lax.shift_right_logical(word, j & 31) & 1


def shifted(tiles, d, count):
    n = len(tiles)
    get = lambda seq, t: seq[t] if 0 <= t < n else None
    if d % 2 == 0:
        return [get(tiles, m - d // 2) for m in range(count)]
    q = (d - 1) // 2
    low = low_half()
    turned = [swap_halves(t) for t in tiles]
    out = []
    for m in range(count):
        a, b = get(turned, m - q - 1), get(turned, m - q)
        if a is None and b is None:
            out.append(None)
        else:
            zero = jnp.zeros((8, 128), F32)
            out.append(jnp.where(low, zero if a is None else a, zero if b is None else b))
    return out


def store_split(hi_ref, lo_ref, row, first, second):
    zero = jnp.zeros((8, 128), F32)
    for m, (a, b) in enumerate(zip(first, second)):
        both = jnp.concatenate([zero if a is None else a, zero if b is None else b], axis=0)
        hi = both.astype(BF16)
        hi_ref[row : row + 16, m * 128 : (m + 1) * 128] = hi
        lo_ref[row : row + 16, m * 128 : (m + 1) * 128] = (both - hi.astype(F32)).astype(BF16)


def tdot(a, b):
    return lax.dot_general(a, b, (((0,), (0,)), ((), ())), preferred_element_type=F32)


def product(hi_ref, lo_ref, start, width):
    xh = hi_ref[:, start : start + width]
    xl = lo_ref[:, start : start + width]
    zh = hi_ref[...]
    return tdot(xh, zh) + tdot(xh, lo_ref[...]) + tdot(xl, zh)


def call(kernel, outs, args, scratch=(), tab=None):
    vmem = pl.BlockSpec(memory_space=pltpu.VMEM)
    table = [] if tab is None else [pl.BlockSpec(memory_space=pltpu.SMEM)]
    return pl.pallas_call(
        kernel,
        out_shape=[jax.ShapeDtypeStruct(o, F32) for o in outs],
        in_specs=table + [vmem] * len(args),
        out_specs=[vmem] * len(outs),
        scratch_shapes=list(scratch),
        compiler_params=pltpu.CompilerParams(vmem_limit_bytes=48 * 1024 * 1024),
    )(*([] if tab is None else [tab]), *args)


def slot_view(pair, slot):
    return pair[0].at[0] if slot == 1 else pair[1].at[(0, None, 1, 2)[slot]]


def split_kernel(d_ref, *refs):
    z, h = lax.axis_index("col"), lax.axis_index("layer")
    for k in range(4):
        for pair, core in ((refs[:2], h), (refs[2:], 1 - h)):
            ref = slot_view(pair, k)
            for e in range(4):
                start = pl.multiple_of(e * 64 + (2 * slot_of(z, core, k) + core) * 8, 8)
                rows = d_ref[pl.ds(start, 8), :]
                for t in range(4):
                    ref[e, t] = rows[:, t * 128 : (t + 1) * 128]


def pack_kernel(own_ref, got_ref, *outs):
    for k, out_ref in enumerate(outs):
        out_ref[0] = own_ref[k]
        out_ref[1] = got_ref[k]


def compact_kernel(tab, *refs):
    ins, (keep_ref, out_ref, x_ref) = refs[:4], refs[4:]
    for k in range(4):
        x_ref[k] = ins[k][...]
    low = low_half()
    row0 = tab[PLACE] * 4
    z, h = tab[PLACE + 6], tab[PLACE + 4]
    for e in range(4):
        i = tab[PERM + row0 + e]
        halves = []
        for t in range(2 * BAND + 2):
            if t > 2 * BAND:
                halves.append(jnp.zeros((8, 128), F32))
                continue
            j = (i + t - BAND) & 63
            sj = tab[INV + j]
            tile = x_ref[slot_with((sj >> 4) ^ z, h), ((sj >> 3) & 1) ^ h, e, (sj & 7) >> 1]
            halves.append(jnp.where((sj & 1) == (t & 1), tile, swap_halves(tile)))
        for t in range(BAND + 1):
            out_ref[e, t] = jnp.where(low, halves[2 * t], halves[2 * t + 1]) * keep_ref[e, t]


def gather_rows(rows):
    near = [line_shift(rows, k, 0) for k in (1, 3, 2)]
    rows, *near = lax.optimization_barrier((rows, *near))
    line = jnp.stack([rows, near[0], near[2], near[1]])
    line = lax.optimization_barrier(line)
    far = [line_shift(line, k, 1) for k in (1, 3, 2)]
    line, *far = lax.optimization_barrier((line, *far))
    return [line, far[0], far[2], far[1]]


def collect(ins, g_ref):
    for n in range(4):
        g_ref[n] = ins[n][...]


def seat(tab, r, e):
    dx = (tab[PLACE + 2] - (r >> 2)) & 3
    dy = (tab[PLACE + 3] - (r & 3)) & 3
    first = tab[PLACE + 4] == 0
    return jnp.where(first, dy, dx), jnp.where(first, dx, dy), e


def write_slabs(p_ref, own, oth, e, base, d, tiles):
    z, h = lax.axis_index("col"), lax.axis_index("layer")
    low = low_half()
    for zz in range(4):
        for pair, core in ((own, h), (oth, 1 - h)):
            ref = slot_view(pair, zz)
            rows = p_ref[base + 2 * slot_of(z, core, zz) + core]
            if d % 2 == 0:
                for m in range(tiles):
                    at = (d // 2 + m) * 128
                    ref[e, m] = rows[:, at : at + 128]
            else:
                q = d // 2
                turned = []
                for m in range(tiles + 1):
                    at = (q + m) * 128
                    if at < rows.shape[1]:
                        turned.append(swap_halves(rows[:, at : at + 128]))
                    else:
                        turned.append(jnp.zeros((8, 128), F32))
                for m in range(tiles):
                    ref[e, m] = jnp.where(low, turned[m], turned[m + 1])


def geometry(w):
    left = w + 1 + (w + 1) % 2
    return left, (left + 4 + w + 1 + 1) // 2


def step_body(strips, w, own, oth, hi_ref, lo_ref, p_ref):
    left, count = geometry(w)
    for a in range(0, len(strips), 2):
        pair = []
        for strip in strips[a : a + 2]:
            b, tiles, first = strip()
            pair.append(shifted(tiles, left - 2 * w + b + 2 * first, count))
        store_split(hi_ref, lo_ref, a * 8, pair[0], pair[1])
    p_ref[...] = product(hi_ref, lo_ref, left * 64, 256).reshape(32, 8, count * 128)
    for e in range(4):
        write_slabs(p_ref, own, oth, e, e * 8, left - (w + 1) + e, w + 2)


def first_step_kernel(tab, *refs):
    ins, own, oth = refs[:4], refs[4:6], refs[6:8]
    cur_ref, hi_ref, lo_ref, p_ref, g_ref = refs[8:]
    collect(ins, g_ref)
    w = BAND
    base = tab[PLACE + 5] * 4 + 64 - w

    def strip_of(b):
        sk = tab[INV + ((base + b) & 63)]
        u, v, e = seat(tab, sk >> 2, sk & 3)
        strip = g_ref[u, v, e]
        if w <= b < w + 4:
            cur_ref[b - w] = strip
        return b, [strip[t] for t in range(w + 1)], 0

    strips = [lambda b=b: strip_of(b) for b in range(4 + 2 * w)]
    step_body(strips, w, own, oth, hi_ref, lo_ref, p_ref)


def step_kernel(w, pieces, *refs):
    far = outermost(w) is not None
    n = 1 + len(pieces) + far
    ins, own, oth = refs[:n], refs[n : n + 2], refs[n + 2 : n + 4]
    hi_ref, lo_ref, p_ref = refs[n + 4 :]

    def strip_of(b):
        off = b - w
        if 0 <= off < 4:
            return b, [ins[0][off, t] for t in range(w + 1)], 0
        d = (-off + 3) // 4 if off < 0 else -(off // 4)
        at = [piece[0] for piece in pieces].index(d)
        _, (lo, hi, first, last) = pieces[at]
        row = off + 4 * d - lo
        return b, [ins[1 + at][row, t] for t in range(last - first)], first

    def far_strip(b, core, slab):
        mine = jnp.where(lax.axis_index("layer") == core, 1.0, 0.0)
        first = 0 if core else w + 1 - far_tiles(w)
        return b, [ins[-1][slab, t] * mine for t in range(far_tiles(w))], first

    last = 4 + 2 * w - 1
    strips = [lambda b=b: strip_of(b) for b in range(far, last + 1 - far)]
    if far:
        for slab in (0, 1):
            strips.append(lambda slab=slab: far_strip(0, 0, slab))
            strips.append(lambda slab=slab: far_strip(last, 1, slab))
    step_body(strips, w, own, oth, hi_ref, lo_ref, p_ref)


def far_tiles(w):
    return w + 1 - 2 * (outermost(w) - 1)


def outermost(w):
    return (w + 3) // 4 if w % 4 == 1 else None


def halo_pieces(w):
    out = []
    for d in range(1, (w + 3) // 4 + 1):
        n = min(4, w - 4 * (d - 1))
        if outermost(w) == d:
            break
        out.append((d, (4 - n, 4, 2 * (d - 1), w + 1)))
        out.append((-d, (0, n, 0, w + 1 - 2 * (d - 1))))
    return out


def last_step_kernel(tab, *refs):
    ins, own, oth = refs[:4], refs[4:6], refs[6:8]
    cur_ref, hi_ref, lo_ref, p_ref, g_ref = refs[8:]
    collect(ins, g_ref)
    w = BAND + STEPS - 1
    row0 = tab[PLACE] * 4
    left, count = w + 2, w + 2
    for e in range(4):
        i = tab[PERM + row0 + e]

        def strips(b):
            k = (i + b - w) & 63
            pos = k >> 2
            a, odd = pos >> 1, pos & 1
            r = jnp.where(a < 4, a * 4 + odd, (7 - a) * 4 + 3 - odd)
            u, v, ee = seat(tab, r, k & 3)
            strip = g_ref[u, v, ee]
            if b == w:
                cur_ref[e] = strip
            return [strip[t] for t in range(w + 1)]

        for a in range(0, 2 * w + 2, 2):
            one = shifted(strips(a), left - 2 * w + a, count)
            two = [None] * count
            if a + 1 <= 2 * w:
                two = shifted(strips(a + 1), left - 2 * w + a + 1, count)
            store_split(hi_ref, lo_ref, a * 8, one, two)
        p_ref[...] = product(hi_ref, lo_ref, left * 64, 64).reshape(8, 8, count * 128)
        write_slabs(p_ref, own, oth, e, 0, 0, count)


def pair_kernel(own_ref, got_ref, *outs):
    for k, out_ref in enumerate(outs):
        out_ref[...] = own_ref[k] + got_ref[k]


def total(parts, e, m):
    return (parts[0][e, m] + parts[1][e, m]) + (parts[2][e, m] + parts[3][e, m])


def polynomial(coef_ref, step, cur, square):
    return coef_ref[step, 0] * cur + coef_ref[step, 1] * square


def keep_kernel(tab, *refs):
    low = low_half()
    refs, coef_ref = refs[:-1], refs[-1]
    for s in range(STEPS):
        twice = tab[BRANCH + s] == 1
        coef_ref[s, 0] = jnp.full((8, 128), jnp.where(twice, 2.0, 0.0), F32)
        coef_ref[s, 1] = jnp.full((8, 128), jnp.where(twice, -1.0, 1.0), F32)
    for s, ref in enumerate(refs):
        w = BAND + s
        margin = w + 1 if s == STEPS else w
        for e in range(4):
            i = tab[PLACE + 5] * 4 + e if 0 < s < STEPS else tab[PERM + tab[PLACE] * 4 + e]
            for m in range(ref.shape[1]):
                sides = []
                for v in (2 * m - margin, 2 * m + 1 - margin):
                    sides.append(bit(tab, s, i, (i + v + 64) & 63) if -w <= v <= w else 0)
                ref[e, m] = jnp.where(low, sides[0], sides[1]).astype(F32)


def close_kernel(step, cuts, far, p0, p1, p2, p3, cur_ref, keep_ref, coef_ref, *refs):
    w = BAND + step
    low = low_half()
    for e in range(4):
        turned = [swap_halves(cur_ref[e, t]) for t in range(w + 1)]
        zero = jnp.zeros((8, 128), F32)
        for m in range(w + 2):
            before = turned[m - 1] if m >= 1 else zero
            after = turned[m] if m <= w else zero
            cur = jnp.where(low, before, after)
            square = total((p0, p1, p2, p3), e, m)
            value = polynomial(coef_ref, step, cur, square) * keep_ref[e, m]
            for ref, (lo, hi, first, last) in zip(refs, cuts):
                if lo <= e < hi and first <= m < last:
                    ref[e - lo, m - first] = value
            if far and e == 3 and m >= w + 2 - far:
                refs[-1][0, m - (w + 2 - far)] = value
            if far and e == 0 and m < far:
                refs[-1][1, m] = value
    if far:
        own_ref, oth_ref, far_ref = refs[-3:]
        own_ref[...] = far_ref[lax.axis_index("layer")]
        oth_ref[...] = far_ref[1 - lax.axis_index("layer")]


def finish_kernel(tab, p0, p1, p2, p3, cur_ref, keep_ref, coef_ref, *refs):
    w = BAND + STEPS - 1
    low = low_half()
    row0 = tab[PLACE] * 4
    z, h = tab[PLACE + 6], tab[PLACE + 4]
    own, oth, y_ref = refs[:2], refs[2:4], refs[4]
    y_ref[...] = jnp.zeros_like(y_ref)
    for e in range(4):
        i = tab[PERM + row0 + e]
        for m in range(w + 2):
            cur = cur_ref[e, m - 1] if 1 <= m <= w + 1 else jnp.zeros((8, 128), F32)
            square = total((p0, p1, p2, p3), e, m)
            value = polynomial(coef_ref, STEPS - 1, cur, square) * keep_ref[e, m]
            turned = swap_halves(value)
            for half in (0, 1):
                v = 2 * m + half
                if v == 0:
                    continue
                j = (i + v + 64 - (w + 2)) & 63
                sj = tab[INV + j]
                odd = sj & 1
                piece = jnp.where(odd == half, value, turned)
                side = jnp.where(low, 0, 1) == odd
                core = (sj >> 3) & 1
                at = core ^ h, slot_with((sj >> 4) ^ z, core), e, (sj & 7) >> 1
                y_ref[at] = jnp.where(side, piece, y_ref[at])
    for slot in range(4):
        slot_view(own, slot)[...] = y_ref[0, slot]
        slot_view(oth, slot)[...] = y_ref[1, slot]


def join_kernel(y0, y1, y2, y3, out_ref):
    z, h = lax.axis_index("col"), lax.axis_index("layer")
    for k, y_ref in enumerate((y0, y1, y2, y3)):
        for core in (0, 1):
            for e in range(4):
                start = pl.multiple_of(e * 64 + (2 * slot_of(z, h, k) + (core ^ h)) * 8, 8)
                for t in range(4):
                    out_ref[pl.ds(start, 8), t * 128 : (t + 1) * 128] = y_ref[core, e, t]


def tables(masks, branch, perm):
    r = lax.axis_index("row")
    z = lax.axis_index("col")
    h = lax.axis_index("layer")
    ids = jnp.arange(64, dtype=jnp.int32)
    inverse = jnp.sum(jnp.where(perm[:, None] == ids[None, :], ids[:, None], 0), axis=0)
    shifts = jnp.arange(32, dtype=jnp.int32)
    bits = jnp.sum(masks.reshape(6, 64, 2, 32) << shifts, axis=-1, dtype=jnp.int32)
    pos = jnp.sum(jnp.where(jnp.asarray(RING) == r, jnp.arange(16), 0))
    place = jnp.stack([r, z * 2 + h, r // 4, r % 4, h, pos, z, z]).astype(jnp.int32)
    return jnp.concatenate(
        [perm, inverse.astype(jnp.int32), branch, jnp.zeros((3,), jnp.int32), bits.reshape(-1), place]
    )


def z_exchange(kernel, shape, parts):
    first, rest, other_first, other_rest = parts
    other_first, other_rest = core_swap(other_first), core_swap(other_rest)
    (far,) = call(kernel, [shape], [first, other_first])
    far = z_swap(far, 1)
    stay, near, last = call(kernel, [shape] * 3, [rest, other_rest])
    return [stay, far, z_swap(near, 2), z_swap(last, 3)]


def reduce_group(parts):
    return z_exchange(pair_kernel, parts[0].shape[1:], parts)


def spread_group(parts):
    return z_exchange(pack_kernel, (2,) + parts[0].shape[1:], parts)


def in_parts(shape):
    return [(1,) + shape, (3,) + shape] * 2


def shards(density, masks, branch, perm):
    slabs = (4, 4, 8, 128)
    split = spread_group(call(split_kernel, in_parts(slabs), [density]))
    tab = tables(masks, branch, perm)
    tiles = [BAND + s + 1 for s in range(STEPS)] + [BAND + STEPS + 1]
    shapes = [(4, n, 8, 128) for n in tiles] + [(STEPS, 2, 8, 128)]
    *keep, coef = call(keep_kernel, shapes, [], tab=tab)
    (rows,) = call(
        compact_kernel,
        [(4, BAND + 1, 8, 128)],
        split + [keep[0]],
        [pltpu.VMEM((4, 2, 4, 4, 8, 128), F32)],
        tab=tab,
    )
    gathered = gather_rows(rows)
    for step in range(STEPS - 1):
        w = BAND + step
        left, count = geometry(w)
        depth = (4 + 2 * w + (2 if step and outermost(w) else 0)) * 8
        part = in_parts((4, w + 2, 8, 128))
        scratch = [
            pltpu.VMEM((depth, count * 128), BF16),
            pltpu.VMEM((depth, count * 128), BF16),
            pltpu.VMEM((32, 8, count * 128), F32),
        ]
        if step == 0:
            scratch.append(pltpu.VMEM((4, 4, 4, w + 1, 8, 128), F32))
            *sums, cur = call(
                first_step_kernel, part + [(4, w + 1, 8, 128)], gathered, scratch, tab=tab
            )
        else:
            kernel = lambda *refs, w=w, pieces=pieces: step_kernel(w, pieces, *refs)
            sums = call(kernel, part, [cur] + around, scratch)
        parts = reduce_group(sums)
        pieces = halo_pieces(w + 1) if step < STEPS - 2 else []
        cuts = [(0, 4, 0, w + 2)]
        for _, cut in pieces:
            if cut not in cuts:
                cuts.append(cut)
        far = far_tiles(w + 1) if pieces and outermost(w + 1) else 0
        kernel = lambda *refs, step=step, cuts=cuts, far=far: close_kernel(step, cuts, far, *refs)
        shapes = [(hi - lo, last - first, 8, 128) for lo, hi, first, last in cuts]
        scratch = [pltpu.VMEM((2, far, 8, 128), F32)] if far else []
        shapes += [(far, 8, 128)] * 2 if far else []
        sent = call(kernel, shapes, parts + [cur, keep[step + 1], coef], scratch)
        cur = sent[0]
        around = [ring_shift(sent[cuts.index(cut)], d) for d, cut in pieces]
        if far:
            both = jnp.stack([sent[-2], core_swap(sent[-1])])
            around.append(outward(both, outermost(w + 1)))
        cur, *around = lax.optimization_barrier((cur, *around))
    gathered = gather_rows(cur)
    w = BAND + STEPS - 1
    part = in_parts((4, w + 2, 8, 128))
    scratch = [
        pltpu.VMEM(((2 * w + 2) * 8, (w + 2) * 128), BF16),
        pltpu.VMEM(((2 * w + 2) * 8, (w + 2) * 128), BF16),
        pltpu.VMEM((8, 8, (w + 2) * 128), F32),
        pltpu.VMEM((4, 4, 4, w + 1, 8, 128), F32),
    ]
    *sums, cur = call(
        last_step_kernel, part + [(4, w + 1, 8, 128)], gathered, scratch, tab=tab
    )
    parts = reduce_group(sums)
    tiles = call(
        finish_kernel,
        in_parts(slabs),
        parts + [cur, keep[STEPS], coef],
        [pltpu.VMEM((2, 4) + slabs, F32)],
        tab=tab,
    )
    (out,) = call(join_kernel, [(256, 512)], spread_group(tiles))
    return out


def solution(mesh):
    return jax.shard_map(
        shards,
        mesh=mesh,
        in_specs=(P("row", GROUP), P(), P(), P()),
        out_specs=P("row", GROUP),
        check_vma=False,
    )
```

```python
import jax
import jax.numpy as jnp
from jax import lax
from jax.experimental import pallas as pl
from jax.experimental.pallas import tpu as pltpu
from jax.sharding import PartitionSpec as P

STEPS = 5
BAND = 6
NB = 64
GROUP = ("col", "layer")
PERM, INV, BRANCH, BITS, PLACE = 0, 64, 128, 136, 136 + 6 * 128
F32, BF16 = jnp.float32, jnp.bfloat16


def ring_xy(pos):
    a, b = pos // 2, pos % 2
    return (a, b) if a < 4 else (7 - a, 3 - b)


RING = [ring_xy(p)[0] * 4 + ring_xy(p)[1] for p in range(16)]


SLOTS = ((0, 2, 1, 3), (0, 2, 3, 1))


def permute(value, axes, pairs):
    flat = value.reshape(-1, 128)
    return lax.ppermute(flat, axes, pairs).reshape(value.shape)


def outward(value, d):
    pairs = []
    for p in range(16):
        pairs.append((RING[p] * 2, RING[(p + d) % 16] * 2))
        pairs.append((RING[p] * 2 + 1, RING[(p - d) % 16] * 2 + 1))
    return permute(value, ("row", "layer"), pairs)


def line_shift(value, k, swapped):
    pairs = []
    for i in range(16):
        for core in (0, 1):
            x, y = i // 4, i % 4
            x, y = (x, (y + k) % 4) if core ^ swapped else ((x + k) % 4, y)
            pairs.append((i * 2 + core, (x * 4 + y) * 2 + core))
    return permute(value, ("row", "layer"), pairs)


def z_swap(value, slot):
    pairs = [(z * 2 + h, (z ^ SLOTS[h][slot]) * 2 + h) for z in range(4) for h in (0, 1)]
    return permute(value, GROUP, pairs)


def slot_of(z, h, slot):
    first, second = SLOTS[0][slot], SLOTS[1][slot]
    return z ^ (first if first == second else jnp.where(h == 0, first, second))


def slot_with(apart, h):
    swapped = jnp.where(apart == 3, 1, jnp.where(apart == 1, 3, apart))
    apart = jnp.where(h == 0, apart, swapped)
    return jnp.where(apart == 2, 1, jnp.where(apart == 1, 2, apart))


def core_swap(value):
    return permute(value, "layer", [(0, 1), (1, 0)])


def low_half():
    return lax.broadcasted_iota(jnp.int32, (8, 128), 1) < 64


def swap_halves(tile):
    return pltpu.roll(tile, 64, 1)


def bit(tab, s, i, j):
    word = tab[BITS + s * 128 + i * 2 + lax.shift_right_logical(j, 5)]
    return lax.shift_right_logical(word, j & 31) & 1


def shifted(tiles, d, count):
    n = len(tiles)
    get = lambda seq, t: seq[t] if 0 <= t < n else None
    if d % 2 == 0:
        return [get(tiles, m - d // 2) for m in range(count)]
    q = (d - 1) // 2
    low = low_half()
    turned = [swap_halves(t) for t in tiles]
    out = []
    for m in range(count):
        a, b = get(turned, m - q - 1), get(turned, m - q)
        if a is None and b is None:
            out.append(None)
        else:
            zero = jnp.zeros((8, 128), F32)
            out.append(jnp.where(low, zero if a is None else a, zero if b is None else b))
    return out


def store_split(hi_ref, lo_ref, row, first, second):
    zero = jnp.zeros((8, 128), F32)
    for m, (a, b) in enumerate(zip(first, second)):
        both = jnp.concatenate([zero if a is None else a, zero if b is None else b], axis=0)
        hi = both.astype(BF16)
        hi_ref[row : row + 16, m * 128 : (m + 1) * 128] = hi
        lo_ref[row : row + 16, m * 128 : (m + 1) * 128] = (both - hi.astype(F32)).astype(BF16)


def tdot(a, b):
    return lax.dot_general(a, b, (((0,), (0,)), ((), ())), preferred_element_type=F32)


def product(hi_ref, lo_ref, start, width):
    xh = hi_ref[:, start : start + width]
    xl = lo_ref[:, start : start + width]
    zh = hi_ref[...]
    return tdot(xh, zh) + tdot(xh, lo_ref[...]) + tdot(xl, zh)


def call(kernel, outs, args, scratch=(), tab=None):
    vmem = pl.BlockSpec(memory_space=pltpu.VMEM)
    table = [] if tab is None else [pl.BlockSpec(memory_space=pltpu.SMEM)]
    return pl.pallas_call(
        kernel,
        out_shape=[jax.ShapeDtypeStruct(o, F32) for o in outs],
        in_specs=table + [vmem] * len(args),
        out_specs=[vmem] * len(outs),
        scratch_shapes=list(scratch),
        compiler_params=pltpu.CompilerParams(vmem_limit_bytes=48 * 1024 * 1024),
    )(*([] if tab is None else [tab]), *args)


def slot_view(pair, slot):
    return pair[0].at[0] if slot == 1 else pair[1].at[(0, None, 1, 2)[slot]]


def split_kernel(d_ref, *refs):
    z, h = lax.axis_index("col"), lax.axis_index("layer")
    for k in range(4):
        for pair, core in ((refs[:2], h), (refs[2:], 1 - h)):
            ref = slot_view(pair, k)
            for e in range(4):
                start = pl.multiple_of(e * 64 + (2 * slot_of(z, core, k) + core) * 8, 8)
                rows = d_ref[pl.ds(start, 8), :]
                for t in range(4):
                    ref[e, t] = rows[:, t * 128 : (t + 1) * 128]


def pack_kernel(own_ref, got_ref, *outs):
    for k, out_ref in enumerate(outs):
        out_ref[0] = own_ref[k]
        out_ref[1] = got_ref[k]


def compact_kernel(tab, *refs):
    ins, (keep_ref, out_ref, x_ref) = refs[:4], refs[4:]
    for k in range(4):
        x_ref[k] = ins[k][...]
    low = low_half()
    row0 = tab[PLACE] * 4
    z, h = tab[PLACE + 6], tab[PLACE + 4]
    for e in range(4):
        i = tab[PERM + row0 + e]
        halves = []
        for t in range(2 * BAND + 2):
            if t > 2 * BAND:
                halves.append(jnp.zeros((8, 128), F32))
                continue
            j = (i + t - BAND) & 63
            sj = tab[INV + j]
            tile = x_ref[slot_with((sj >> 4) ^ z, h), ((sj >> 3) & 1) ^ h, e, (sj & 7) >> 1]
            halves.append(jnp.where((sj & 1) == (t & 1), tile, swap_halves(tile)))
        for t in range(BAND + 1):
            out_ref[e, t] = jnp.where(low, halves[2 * t], halves[2 * t + 1]) * keep_ref[e, t]


def gather_rows(rows):
    near = [line_shift(rows, k, 0) for k in (1, 3, 2)]
    rows, *near = lax.optimization_barrier((rows, *near))
    line = jnp.stack([rows, near[0], near[2], near[1]])
    line = lax.optimization_barrier(line)
    far = [line_shift(line, k, 1) for k in (1, 3, 2)]
    line, *far = lax.optimization_barrier((line, *far))
    return [line, far[0], far[2], far[1]]


def collect(ins, g_ref):
    for n in range(4):
        g_ref[n] = ins[n][...]


def seat(tab, r, e):
    dx = (tab[PLACE + 2] - (r >> 2)) & 3
    dy = (tab[PLACE + 3] - (r & 3)) & 3
    first = tab[PLACE + 4] == 0
    return jnp.where(first, dy, dx), jnp.where(first, dx, dy), e


def write_slabs(p_ref, own, oth, e, base, d, tiles):
    z, h = lax.axis_index("col"), lax.axis_index("layer")
    low = low_half()
    for zz in range(4):
        for pair, core in ((own, h), (oth, 1 - h)):
            ref = slot_view(pair, zz)
            rows = p_ref[base + 2 * slot_of(z, core, zz) + core]
            if d % 2 == 0:
                for m in range(tiles):
                    at = (d // 2 + m) * 128
                    ref[e, m] = rows[:, at : at + 128]
            else:
                q = d // 2
                turned = []
                for m in range(tiles + 1):
                    at = (q + m) * 128
                    if at < rows.shape[1]:
                        turned.append(swap_halves(rows[:, at : at + 128]))
                    else:
                        turned.append(jnp.zeros((8, 128), F32))
                for m in range(tiles):
                    ref[e, m] = jnp.where(low, turned[m], turned[m + 1])


def geometry(w):
    left = w + 1 + (w + 1) % 2
    return left, (left + 4 + w + 1 + 1) // 2


def step_body(strips, w, own, oth, hi_ref, lo_ref, p_ref):
    left, count = geometry(w)
    for a in range(0, len(strips), 2):
        pair = []
        for strip in strips[a : a + 2]:
            b, tiles, first = strip()
            pair.append(shifted(tiles, left - 2 * w + b + 2 * first, count))
        store_split(hi_ref, lo_ref, a * 8, pair[0], pair[1])
    p_ref[...] = product(hi_ref, lo_ref, left * 64, 256).reshape(32, 8, count * 128)
    for e in range(4):
        write_slabs(p_ref, own, oth, e, e * 8, left - (w + 1) + e, w + 2)


def first_step_kernel(tab, *refs):
    ins, own, oth = refs[:4], refs[4:6], refs[6:8]
    cur_ref, hi_ref, lo_ref, p_ref, g_ref = refs[8:]
    collect(ins, g_ref)
    w = BAND
    base = tab[PLACE + 5] * 4 + 64 - w

    def strip_of(b):
        sk = tab[INV + ((base + b) & 63)]
        u, v, e = seat(tab, sk >> 2, sk & 3)
        strip = g_ref[u, v, e]
        if w <= b < w + 4:
            cur_ref[b - w] = strip
        return b, [strip[t] for t in range(w + 1)], 0

    strips = [lambda b=b: strip_of(b) for b in range(4 + 2 * w)]
    step_body(strips, w, own, oth, hi_ref, lo_ref, p_ref)


def step_kernel(w, pieces, *refs):
    far = outermost(w) is not None
    n = 1 + len(pieces) + far
    ins, own, oth = refs[:n], refs[n : n + 2], refs[n + 2 : n + 4]
    (hi_ref, lo_ref, p_ref), sides = refs[n + 4 : n + 7], refs[n + 7 :]
    h = lax.axis_index("layer")
    for k, side in enumerate(sides):
        side[h] = ins[1 + 2 * k][...]
        side[1 - h] = ins[2 + 2 * k][...]

    def strip_of(b):
        off = b - w
        if 0 <= off < 4:
            return b, [ins[0][off, t] for t in range(w + 1)], 0
        d = (-off + 3) // 4 if off < 0 else -(off // 4)
        at = [piece[0] for piece in pieces].index(d)
        _, (lo, hi, first, last) = pieces[at]
        row = off + 4 * d - lo
        return b, [sides[at // 2][at % 2, row, t] for t in range(last - first)], first

    def far_strip(b, core, slab):
        mine = jnp.where(lax.axis_index("layer") == core, 1.0, 0.0)
        first = 0 if core else w + 1 - far_tiles(w)
        return b, [ins[-1][slab, t] * mine for t in range(far_tiles(w))], first

    last = 4 + 2 * w - 1
    strips = [lambda b=b: strip_of(b) for b in range(far, last + 1 - far)]
    if far:
        for slab in (0, 1):
            strips.append(lambda slab=slab: far_strip(0, 0, slab))
            strips.append(lambda slab=slab: far_strip(last, 1, slab))
    step_body(strips, w, own, oth, hi_ref, lo_ref, p_ref)


def far_tiles(w):
    return w + 1 - 2 * (outermost(w) - 1)


def outermost(w):
    return (w + 3) // 4 if w % 4 == 1 else None


def halo_pieces(w):
    out = []
    for d in range(1, (w + 3) // 4 + 1):
        n = min(4, w - 4 * (d - 1))
        if outermost(w) == d:
            break
        out.append((d, (4 - n, 4, 2 * (d - 1), w + 1)))
        out.append((-d, (0, n, 0, w + 1 - 2 * (d - 1))))
    return out


def last_step_kernel(tab, *refs):
    ins, own, oth = refs[:4], refs[4:6], refs[6:8]
    cur_ref, hi_ref, lo_ref, p_ref, g_ref = refs[8:]
    collect(ins, g_ref)
    w = BAND + STEPS - 1
    row0 = tab[PLACE] * 4
    left, count = w + 2, w + 2
    for e in range(4):
        i = tab[PERM + row0 + e]

        def strips(b):
            k = (i + b - w) & 63
            pos = k >> 2
            a, odd = pos >> 1, pos & 1
            r = jnp.where(a < 4, a * 4 + odd, (7 - a) * 4 + 3 - odd)
            u, v, ee = seat(tab, r, k & 3)
            strip = g_ref[u, v, ee]
            if b == w:
                cur_ref[e] = strip
            return [strip[t] for t in range(w + 1)]

        for a in range(0, 2 * w + 2, 2):
            one = shifted(strips(a), left - 2 * w + a, count)
            two = [None] * count
            if a + 1 <= 2 * w:
                two = shifted(strips(a + 1), left - 2 * w + a + 1, count)
            store_split(hi_ref, lo_ref, a * 8, one, two)
        p_ref[...] = product(hi_ref, lo_ref, left * 64, 64).reshape(8, 8, count * 128)
        write_slabs(p_ref, own, oth, e, 0, 0, count)


def pair_kernel(own_ref, got_ref, *outs):
    for k, out_ref in enumerate(outs):
        out_ref[...] = own_ref[k] + got_ref[k]


def total(parts, e, m):
    return (parts[0][e, m] + parts[1][e, m]) + (parts[2][e, m] + parts[3][e, m])


def polynomial(coef_ref, step, cur, square):
    return coef_ref[step, 0] * cur + coef_ref[step, 1] * square


def keep_kernel(tab, *refs):
    low = low_half()
    refs, coef_ref = refs[:-1], refs[-1]
    for s in range(STEPS):
        twice = tab[BRANCH + s] == 1
        coef_ref[s, 0] = jnp.full((8, 128), jnp.where(twice, 2.0, 0.0), F32)
        coef_ref[s, 1] = jnp.full((8, 128), jnp.where(twice, -1.0, 1.0), F32)
    for s, ref in enumerate(refs):
        w = BAND + s
        margin = w + 1 if s == STEPS else w
        for e in range(4):
            i = tab[PLACE + 5] * 4 + e if 0 < s < STEPS else tab[PERM + tab[PLACE] * 4 + e]
            for m in range(ref.shape[1]):
                sides = []
                for v in (2 * m - margin, 2 * m + 1 - margin):
                    sides.append(bit(tab, s, i, (i + v + 64) & 63) if -w <= v <= w else 0)
                ref[e, m] = jnp.where(low, sides[0], sides[1]).astype(F32)


def close_kernel(step, cuts, far, p0, p1, p2, p3, cur_ref, keep_ref, coef_ref, *refs):
    w = BAND + step
    h = lax.axis_index("layer")
    low = low_half()
    n = len(cuts) + (far > 0)
    out_ref, sent, kept = refs[0], refs[1 : 1 + 2 * n], refs[1 + 2 * n :]
    if far:
        cuts = cuts + [((3, 4, w + 2 - far, w + 2), (0, 1, 0, far))]
    for e in range(4):
        turned = [swap_halves(cur_ref[e, t]) for t in range(w + 1)]
        zero = jnp.zeros((8, 128), F32)
        for m in range(w + 2):
            before = turned[m - 1] if m >= 1 else zero
            after = turned[m] if m <= w else zero
            cur = jnp.where(low, before, after)
            square = total((p0, p1, p2, p3), e, m)
            value = polynomial(coef_ref, step, cur, square) * keep_ref[e, m]
            out_ref[e, m] = value
            for ref, pair in zip(kept, cuts):
                for side, (lo, hi, first, last) in enumerate(pair):
                    if lo <= e < hi and first <= m < last:
                        ref[side, e - lo, m - first] = value
    for k, ref in enumerate(kept):
        sent[2 * k][...] = ref[h]
        sent[2 * k + 1][...] = ref[1 - h]


def finish_kernel(tab, p0, p1, p2, p3, cur_ref, keep_ref, coef_ref, *refs):
    w = BAND + STEPS - 1
    low = low_half()
    row0 = tab[PLACE] * 4
    z, h = tab[PLACE + 6], tab[PLACE + 4]
    own, oth, y_ref = refs[:2], refs[2:4], refs[4]
    y_ref[...] = jnp.zeros_like(y_ref)
    for e in range(4):
        i = tab[PERM + row0 + e]
        for m in range(w + 2):
            cur = cur_ref[e, m - 1] if 1 <= m <= w + 1 else jnp.zeros((8, 128), F32)
            square = total((p0, p1, p2, p3), e, m)
            value = polynomial(coef_ref, STEPS - 1, cur, square) * keep_ref[e, m]
            turned = swap_halves(value)
            for half in (0, 1):
                v = 2 * m + half
                if v == 0:
                    continue
                j = (i + v + 64 - (w + 2)) & 63
                sj = tab[INV + j]
                odd = sj & 1
                piece = jnp.where(odd == half, value, turned)
                side = jnp.where(low, 0, 1) == odd
                core = (sj >> 3) & 1
                at = core ^ h, slot_with((sj >> 4) ^ z, core), e, (sj & 7) >> 1
                y_ref[at] = jnp.where(side, piece, y_ref[at])
    for slot in range(4):
        slot_view(own, slot)[...] = y_ref[0, slot]
        slot_view(oth, slot)[...] = y_ref[1, slot]


def join_kernel(y0, y1, y2, y3, out_ref):
    z, h = lax.axis_index("col"), lax.axis_index("layer")
    for k, y_ref in enumerate((y0, y1, y2, y3)):
        for core in (0, 1):
            for e in range(4):
                start = pl.multiple_of(e * 64 + (2 * slot_of(z, h, k) + (core ^ h)) * 8, 8)
                for t in range(4):
                    out_ref[pl.ds(start, 8), t * 128 : (t + 1) * 128] = y_ref[core, e, t]


def tables(masks, branch, perm):
    r = lax.axis_index("row")
    z = lax.axis_index("col")
    h = lax.axis_index("layer")
    ids = jnp.arange(64, dtype=jnp.int32)
    inverse = jnp.sum(jnp.where(perm[:, None] == ids[None, :], ids[:, None], 0), axis=0)
    shifts = jnp.arange(32, dtype=jnp.int32)
    bits = jnp.sum(masks.reshape(6, 64, 2, 32) << shifts, axis=-1, dtype=jnp.int32)
    pos = jnp.sum(jnp.where(jnp.asarray(RING) == r, jnp.arange(16), 0))
    place = jnp.stack([r, z * 2 + h, r // 4, r % 4, h, pos, z, z]).astype(jnp.int32)
    return jnp.concatenate(
        [perm, inverse.astype(jnp.int32), branch, jnp.zeros((3,), jnp.int32), bits.reshape(-1), place]
    )


def z_exchange(kernel, shape, parts):
    first, rest, other_first, other_rest = parts
    other_first, other_rest = core_swap(other_first), core_swap(other_rest)
    (far,) = call(kernel, [shape], [first, other_first])
    far = z_swap(far, 1)
    stay, near, last = call(kernel, [shape] * 3, [rest, other_rest])
    return [stay, far, z_swap(near, 2), z_swap(last, 3)]


def reduce_group(parts):
    return z_exchange(pair_kernel, parts[0].shape[1:], parts)


def spread_group(parts):
    return z_exchange(pack_kernel, (2,) + parts[0].shape[1:], parts)


def in_parts(shape):
    return [(1,) + shape, (3,) + shape] * 2


def shards(density, masks, branch, perm):
    slabs = (4, 4, 8, 128)
    split = spread_group(call(split_kernel, in_parts(slabs), [density]))
    tab = tables(masks, branch, perm)
    tiles = [BAND + s + 1 for s in range(STEPS)] + [BAND + STEPS + 1]
    shapes = [(4, n, 8, 128) for n in tiles] + [(STEPS, 2, 8, 128)]
    *keep, coef = call(keep_kernel, shapes, [], tab=tab)
    (rows,) = call(
        compact_kernel,
        [(4, BAND + 1, 8, 128)],
        split + [keep[0]],
        [pltpu.VMEM((4, 2, 4, 4, 8, 128), F32)],
        tab=tab,
    )
    gathered = gather_rows(rows)
    for step in range(STEPS - 1):
        w = BAND + step
        left, count = geometry(w)
        depth = (4 + 2 * w + (2 if step and outermost(w) else 0)) * 8
        part = in_parts((4, w + 2, 8, 128))
        scratch = [
            pltpu.VMEM((depth, count * 128), BF16),
            pltpu.VMEM((depth, count * 128), BF16),
            pltpu.VMEM((32, 8, count * 128), F32),
        ]
        if step == 0:
            scratch.append(pltpu.VMEM((4, 4, 4, w + 1, 8, 128), F32))
            *sums, cur = call(
                first_step_kernel, part + [(4, w + 1, 8, 128)], gathered, scratch, tab=tab
            )
        else:
            kernel = lambda *refs, w=w, pieces=pieces: step_kernel(w, pieces, *refs)
            for _, (lo, hi, first, last) in pieces[::2]:
                scratch.append(pltpu.VMEM((2, hi - lo, last - first, 8, 128), F32))
            sums = call(kernel, part, [cur] + around, scratch)
        parts = reduce_group(sums)
        pieces = halo_pieces(w + 1) if step < STEPS - 2 else []
        cuts = [(pieces[k][1], pieces[k + 1][1]) for k in range(2, len(pieces), 2)]
        far = far_tiles(w + 1) if pieces and outermost(w + 1) else 0
        kernel = lambda *refs, step=step, cuts=cuts, far=far: close_kernel(step, cuts, far, *refs)
        shapes = [(hi - lo, last - first, 8, 128) for (lo, hi, first, last), _ in cuts]
        shapes += [(1, far, 8, 128)] if far else []
        outs = [(4, w + 2, 8, 128)] + [shape for shape in shapes for _ in (0, 1)]
        scratch = [pltpu.VMEM((2,) + shape, F32) for shape in shapes]
        cur, *sent = call(kernel, outs, parts + [cur, keep[step + 1], coef], scratch)
        if pieces:
            around = [outward(cur, 1), outward(cur, -1)]
            for k in range(len(cuts)):
                around += [outward(sent[2 * k], k + 2), outward(sent[2 * k + 1], -k - 2)]
            if far:
                both = jnp.stack([sent[-2][0], core_swap(sent[-1])[0]])
                around.append(outward(both, outermost(w + 1)))
            cur, *around = lax.optimization_barrier((cur, *around))
    gathered = gather_rows(cur)
    w = BAND + STEPS - 1
    part = in_parts((4, w + 2, 8, 128))
    scratch = [
        pltpu.VMEM(((2 * w + 2) * 8, (w + 2) * 128), BF16),
        pltpu.VMEM(((2 * w + 2) * 8, (w + 2) * 128), BF16),
        pltpu.VMEM((8, 8, (w + 2) * 128), F32),
        pltpu.VMEM((4, 4, 4, w + 1, 8, 128), F32),
    ]
    *sums, cur = call(
        last_step_kernel, part + [(4, w + 1, 8, 128)], gathered, scratch, tab=tab
    )
    parts = reduce_group(sums)
    tiles = call(
        finish_kernel,
        in_parts(slabs),
        parts + [cur, keep[STEPS], coef],
        [pltpu.VMEM((2, 4) + slabs, F32)],
        tab=tab,
    )
    (out,) = call(join_kernel, [(256, 512)], spread_group(tiles))
    return out


def solution(mesh):
    return jax.shard_map(
        shards,
        mesh=mesh,
        in_specs=(P("row", GROUP), P(), P(), P()),
        out_specs=P("row", GROUP),
        check_vma=False,
    )
```

```python
import jax
import jax.numpy as jnp
from jax import lax
from jax.experimental import pallas as pl
from jax.experimental.pallas import tpu as pltpu
from jax.sharding import PartitionSpec as P

STEPS = 5
BAND = 6
NB = 64
GROUP = ("col", "layer")
PERM, INV, BRANCH, BITS, PLACE = 0, 64, 128, 136, 136 + 6 * 128
F32, BF16 = jnp.float32, jnp.bfloat16


def ring_xy(pos):
    a, b = pos // 2, pos % 2
    return (a, b) if a < 4 else (7 - a, 3 - b)


RING = [ring_xy(p)[0] * 4 + ring_xy(p)[1] for p in range(16)]


SLOTS = ((0, 2, 1, 3), (0, 2, 3, 1))


def permute(value, axes, pairs):
    flat = value.reshape(-1, 128)
    return lax.ppermute(flat, axes, pairs).reshape(value.shape)


def ring_shift(value, k):
    return permute(value, "row", [(RING[p], RING[(p + k) % 16]) for p in range(16)])


def outward(value, d):
    pairs = []
    for p in range(16):
        pairs.append((RING[p] * 2, RING[(p + d) % 16] * 2))
        pairs.append((RING[p] * 2 + 1, RING[(p - d) % 16] * 2 + 1))
    return permute(value, ("row", "layer"), pairs)


def line_shift(value, k, swapped):
    pairs = []
    for i in range(16):
        for core in (0, 1):
            x, y = i // 4, i % 4
            x, y = (x, (y + k) % 4) if core ^ swapped else ((x + k) % 4, y)
            pairs.append((i * 2 + core, (x * 4 + y) * 2 + core))
    return permute(value, ("row", "layer"), pairs)


def z_swap(value, slot):
    pairs = [(z * 2 + h, (z ^ SLOTS[h][slot]) * 2 + h) for z in range(4) for h in (0, 1)]
    return permute(value, GROUP, pairs)


def slot_of(z, h, slot):
    first, second = SLOTS[0][slot], SLOTS[1][slot]
    return z ^ (first if first == second else jnp.where(h == 0, first, second))


def slot_with(apart, h):
    swapped = jnp.where(apart == 3, 1, jnp.where(apart == 1, 3, apart))
    apart = jnp.where(h == 0, apart, swapped)
    return jnp.where(apart == 2, 1, jnp.where(apart == 1, 2, apart))


def core_swap(value):
    return permute(value, "layer", [(0, 1), (1, 0)])


def low_half():
    return lax.broadcasted_iota(jnp.int32, (8, 128), 1) < 64


def swap_halves(tile):
    return pltpu.roll(tile, 64, 1)


def bit(tab, s, i, j):
    word = tab[BITS + s * 128 + i * 2 + lax.shift_right_logical(j, 5)]
    return lax.shift_right_logical(word, j & 31) & 1


def shifted(tiles, d, count):
    n = len(tiles)
    get = lambda seq, t: seq[t] if 0 <= t < n else None
    if d % 2 == 0:
        return [get(tiles, m - d // 2) for m in range(count)]
    q = (d - 1) // 2
    low = low_half()
    turned = [swap_halves(t) for t in tiles]
    out = []
    for m in range(count):
        a, b = get(turned, m - q - 1), get(turned, m - q)
        if a is None and b is None:
            out.append(None)
        else:
            zero = jnp.zeros((8, 128), F32)
            out.append(jnp.where(low, zero if a is None else a, zero if b is None else b))
    return out


def store_split(hi_ref, lo_ref, row, first, second):
    zero = jnp.zeros((8, 128), F32)
    for m, (a, b) in enumerate(zip(first, second)):
        both = jnp.concatenate([zero if a is None else a, zero if b is None else b], axis=0)
        hi = both.astype(BF16)
        hi_ref[row : row + 16, m * 128 : (m + 1) * 128] = hi
        lo_ref[row : row + 16, m * 128 : (m + 1) * 128] = (both - hi.astype(F32)).astype(BF16)


def tdot(a, b):
    return lax.dot_general(a, b, (((0,), (0,)), ((), ())), preferred_element_type=F32)


def product(hi_ref, lo_ref, start, width):
    xh = hi_ref[:, start : start + width]
    xl = lo_ref[:, start : start + width]
    zh = hi_ref[...]
    return tdot(xh, zh) + tdot(xh, lo_ref[...]) + tdot(xl, zh)


def call(kernel, outs, args, scratch=(), tab=None):
    vmem = pl.BlockSpec(memory_space=pltpu.VMEM)
    table, body = [], kernel
    scratch = list(scratch)
    if tab is not None:
        table = [pl.BlockSpec(memory_space=pl.ANY)]
        scratch += [pltpu.SMEM(tab.shape, jnp.int32), pltpu.SemaphoreType.DMA]

        def body(tab_ref, *refs):
            refs, (here, sem) = refs[:-2], refs[-2:]
            copy = pltpu.make_async_copy(tab_ref, here, sem)
            copy.start()

            def arrived():
                copy.wait()
                return here

            kernel(arrived, *refs)

    return pl.pallas_call(
        body,
        out_shape=[jax.ShapeDtypeStruct(o, F32) for o in outs],
        in_specs=table + [vmem] * len(args),
        out_specs=[vmem] * len(outs),
        scratch_shapes=scratch,
        compiler_params=pltpu.CompilerParams(vmem_limit_bytes=48 * 1024 * 1024),
    )(*([] if tab is None else [tab]), *args)


def slot_view(pair, slot):
    return pair[0].at[0] if slot == 1 else pair[1].at[(0, None, 1, 2)[slot]]


def split_kernel(d_ref, *refs):
    z, h = lax.axis_index("col"), lax.axis_index("layer")
    for k in range(4):
        for pair, core in ((refs[:2], h), (refs[2:], 1 - h)):
            ref = slot_view(pair, k)
            for e in range(4):
                start = pl.multiple_of(e * 64 + (2 * slot_of(z, core, k) + core) * 8, 8)
                rows = d_ref[pl.ds(start, 8), :]
                for t in range(4):
                    ref[e, t] = rows[:, t * 128 : (t + 1) * 128]


def pack_kernel(own_ref, got_ref, *outs):
    for k, out_ref in enumerate(outs):
        out_ref[0] = own_ref[k]
        out_ref[1] = got_ref[k]


def compact_kernel(arrived, *refs):
    ins, (keep_ref, out_ref, x_ref) = refs[:4], refs[4:]
    for k in range(4):
        x_ref[k] = ins[k][...]
    tab = arrived()
    low = low_half()
    row0 = tab[PLACE] * 4
    z, h = tab[PLACE + 6], tab[PLACE + 4]
    for e in range(4):
        i = tab[PERM + row0 + e]
        halves = []
        for t in range(2 * BAND + 2):
            if t > 2 * BAND:
                halves.append(jnp.zeros((8, 128), F32))
                continue
            j = (i + t - BAND) & 63
            sj = tab[INV + j]
            tile = x_ref[slot_with((sj >> 4) ^ z, h), ((sj >> 3) & 1) ^ h, e, (sj & 7) >> 1]
            halves.append(jnp.where((sj & 1) == (t & 1), tile, swap_halves(tile)))
        for t in range(BAND + 1):
            out_ref[e, t] = jnp.where(low, halves[2 * t], halves[2 * t + 1]) * keep_ref[e, t]


def gather_rows(rows):
    near = [line_shift(rows, k, 0) for k in (1, 3, 2)]
    rows, *near = lax.optimization_barrier((rows, *near))
    line = jnp.stack([rows, near[0], near[2], near[1]])
    line = lax.optimization_barrier(line)
    far = [line_shift(line, k, 1) for k in (1, 3, 2)]
    line, *far = lax.optimization_barrier((line, *far))
    return [line, far[0], far[2], far[1]]


def collect(ins, g_ref):
    for n in range(4):
        g_ref[n] = ins[n][...]


def seat(tab, r, e):
    dx = (tab[PLACE + 2] - (r >> 2)) & 3
    dy = (tab[PLACE + 3] - (r & 3)) & 3
    first = tab[PLACE + 4] == 0
    return jnp.where(first, dy, dx), jnp.where(first, dx, dy), e


def write_slabs(p_ref, own, oth, e, base, d, tiles):
    z, h = lax.axis_index("col"), lax.axis_index("layer")
    low = low_half()
    for zz in range(4):
        for pair, core in ((own, h), (oth, 1 - h)):
            ref = slot_view(pair, zz)
            rows = p_ref[base + 2 * slot_of(z, core, zz) + core]
            if d % 2 == 0:
                for m in range(tiles):
                    at = (d // 2 + m) * 128
                    ref[e, m] = rows[:, at : at + 128]
            else:
                q = d // 2
                turned = []
                for m in range(tiles + 1):
                    at = (q + m) * 128
                    if at < rows.shape[1]:
                        turned.append(swap_halves(rows[:, at : at + 128]))
                    else:
                        turned.append(jnp.zeros((8, 128), F32))
                for m in range(tiles):
                    ref[e, m] = jnp.where(low, turned[m], turned[m + 1])


def geometry(w):
    left = w + 1 + (w + 1) % 2
    return left, (left + 4 + w + 1 + 1) // 2


def step_body(strips, w, own, oth, hi_ref, lo_ref, p_ref):
    left, count = geometry(w)
    for a in range(0, len(strips), 2):
        pair = []
        for strip in strips[a : a + 2]:
            b, tiles, first = strip()
            pair.append(shifted(tiles, left - 2 * w + b + 2 * first, count))
        store_split(hi_ref, lo_ref, a * 8, pair[0], pair[1])
    p_ref[...] = product(hi_ref, lo_ref, left * 64, 256).reshape(32, 8, count * 128)
    for e in range(4):
        write_slabs(p_ref, own, oth, e, e * 8, left - (w + 1) + e, w + 2)


def first_step_kernel(arrived, *refs):
    ins, own, oth = refs[:4], refs[4:6], refs[6:8]
    cur_ref, hi_ref, lo_ref, p_ref, g_ref = refs[8:]
    collect(ins, g_ref)
    tab = arrived()
    w = BAND
    base = tab[PLACE + 5] * 4 + 64 - w

    def strip_of(b):
        sk = tab[INV + ((base + b) & 63)]
        u, v, e = seat(tab, sk >> 2, sk & 3)
        strip = g_ref[u, v, e]
        if w <= b < w + 4:
            cur_ref[b - w] = strip
        return b, [strip[t] for t in range(w + 1)], 0

    strips = [lambda b=b: strip_of(b) for b in range(4 + 2 * w)]
    step_body(strips, w, own, oth, hi_ref, lo_ref, p_ref)


def step_kernel(w, pieces, *refs):
    far = outermost(w) is not None
    n = 1 + len(pieces) + far
    ins, own, oth = refs[:n], refs[n : n + 2], refs[n + 2 : n + 4]
    hi_ref, lo_ref, p_ref = refs[n + 4 :]

    def strip_of(b):
        off = b - w
        if 0 <= off < 4:
            return b, [ins[0][off, t] for t in range(w + 1)], 0
        d = (-off + 3) // 4 if off < 0 else -(off // 4)
        at = [piece[0] for piece in pieces].index(d)
        _, (lo, hi, first, last) = pieces[at]
        row = off + 4 * d - lo
        return b, [ins[1 + at][row, t] for t in range(last - first)], first

    def far_strip(b, core, slab):
        mine = jnp.where(lax.axis_index("layer") == core, 1.0, 0.0)
        first = 0 if core else w + 1 - far_tiles(w)
        return b, [ins[-1][slab, t] * mine for t in range(far_tiles(w))], first

    last = 4 + 2 * w - 1
    strips = [lambda b=b: strip_of(b) for b in range(far, last + 1 - far)]
    if far:
        for slab in (0, 1):
            strips.append(lambda slab=slab: far_strip(0, 0, slab))
            strips.append(lambda slab=slab: far_strip(last, 1, slab))
    step_body(strips, w, own, oth, hi_ref, lo_ref, p_ref)


def far_tiles(w):
    return w + 1 - 2 * (outermost(w) - 1)


def outermost(w):
    return (w + 3) // 4 if w % 4 == 1 else None


def halo_pieces(w):
    out = []
    for d in range(1, (w + 3) // 4 + 1):
        n = min(4, w - 4 * (d - 1))
        if outermost(w) == d:
            break
        out.append((d, (4 - n, 4, 2 * (d - 1), w + 1)))
        out.append((-d, (0, n, 0, w + 1 - 2 * (d - 1))))
    return out


def last_step_kernel(arrived, *refs):
    ins, own, oth = refs[:4], refs[4:6], refs[6:8]
    cur_ref, hi_ref, lo_ref, p_ref, g_ref = refs[8:]
    collect(ins, g_ref)
    tab = arrived()
    w = BAND + STEPS - 1
    row0 = tab[PLACE] * 4
    left, count = w + 2, w + 2
    for e in range(4):
        i = tab[PERM + row0 + e]

        def strips(b):
            k = (i + b - w) & 63
            pos = k >> 2
            a, odd = pos >> 1, pos & 1
            r = jnp.where(a < 4, a * 4 + odd, (7 - a) * 4 + 3 - odd)
            u, v, ee = seat(tab, r, k & 3)
            strip = g_ref[u, v, ee]
            if b == w:
                cur_ref[e] = strip
            return [strip[t] for t in range(w + 1)]

        for a in range(0, 2 * w + 2, 2):
            one = shifted(strips(a), left - 2 * w + a, count)
            two = [None] * count
            if a + 1 <= 2 * w:
                two = shifted(strips(a + 1), left - 2 * w + a + 1, count)
            store_split(hi_ref, lo_ref, a * 8, one, two)
        p_ref[...] = product(hi_ref, lo_ref, left * 64, 64).reshape(8, 8, count * 128)
        write_slabs(p_ref, own, oth, e, 0, 0, count)


def pair_kernel(own_ref, got_ref, *outs):
    for k, out_ref in enumerate(outs):
        out_ref[...] = own_ref[k] + got_ref[k]


def total(parts, e, m):
    return (parts[0][e, m] + parts[1][e, m]) + (parts[2][e, m] + parts[3][e, m])


def polynomial(coef_ref, step, cur, square):
    return coef_ref[step, 0] * cur + coef_ref[step, 1] * square


def keep_kernel(arrived, *refs):
    low = low_half()
    refs, coef_ref = refs[:-1], refs[-1]
    tab = arrived()
    for s in range(STEPS):
        twice = tab[BRANCH + s] == 1
        coef_ref[s, 0] = jnp.full((8, 128), jnp.where(twice, 2.0, 0.0), F32)
        coef_ref[s, 1] = jnp.full((8, 128), jnp.where(twice, -1.0, 1.0), F32)
    for s, ref in enumerate(refs):
        w = BAND + s
        margin = w + 1 if s == STEPS else w
        for e in range(4):
            i = tab[PLACE + 5] * 4 + e if 0 < s < STEPS else tab[PERM + tab[PLACE] * 4 + e]
            for m in range(ref.shape[1]):
                sides = []
                for v in (2 * m - margin, 2 * m + 1 - margin):
                    sides.append(bit(tab, s, i, (i + v + 64) & 63) if -w <= v <= w else 0)
                ref[e, m] = jnp.where(low, sides[0], sides[1]).astype(F32)


def close_kernel(step, cuts, far, p0, p1, p2, p3, cur_ref, keep_ref, coef_ref, *refs):
    w = BAND + step
    low = low_half()
    for e in range(4):
        turned = [swap_halves(cur_ref[e, t]) for t in range(w + 1)]
        zero = jnp.zeros((8, 128), F32)
        for m in range(w + 2):
            before = turned[m - 1] if m >= 1 else zero
            after = turned[m] if m <= w else zero
            cur = jnp.where(low, before, after)
            square = total((p0, p1, p2, p3), e, m)
            value = polynomial(coef_ref, step, cur, square) * keep_ref[e, m]
            for ref, (lo, hi, first, last) in zip(refs, cuts):
                if lo <= e < hi and first <= m < last:
                    ref[e - lo, m - first] = value
            if far and e == 3 and m >= w + 2 - far:
                refs[-1][0, m - (w + 2 - far)] = value
            if far and e == 0 and m < far:
                refs[-1][1, m] = value
    if far:
        own_ref, oth_ref, far_ref = refs[-3:]
        own_ref[...] = far_ref[lax.axis_index("layer")]
        oth_ref[...] = far_ref[1 - lax.axis_index("layer")]


def finish_kernel(arrived, p0, p1, p2, p3, cur_ref, keep_ref, coef_ref, *refs):
    w = BAND + STEPS - 1
    low = low_half()
    own, oth, y_ref, v_ref = refs[:2], refs[2:4], refs[4], refs[5]
    y_ref[...] = jnp.zeros_like(y_ref)
    for e in range(4):
        for m in range(w + 2):
            cur = cur_ref[e, m - 1] if 1 <= m <= w + 1 else jnp.zeros((8, 128), F32)
            square = total((p0, p1, p2, p3), e, m)
            value = polynomial(coef_ref, STEPS - 1, cur, square) * keep_ref[e, m]
            v_ref[0, e, m] = value
            v_ref[1, e, m] = swap_halves(value)
    tab = arrived()
    row0 = tab[PLACE] * 4
    z, h = tab[PLACE + 6], tab[PLACE + 4]
    for e in range(4):
        i = tab[PERM + row0 + e]
        for v in range(1, 2 * w + 4):
            j = (i + v + 64 - (w + 2)) & 63
            sj = tab[INV + j]
            odd, core = sj & 1, (sj >> 3) & 1
            piece = v_ref[odd ^ (v & 1), e, v // 2]
            side = jnp.where(low, 0, 1) == odd
            at = core ^ h, slot_with((sj >> 4) ^ z, core), e, (sj & 7) >> 1
            y_ref[at] = jnp.where(side, piece, y_ref[at])
    for slot in range(4):
        slot_view(own, slot)[...] = y_ref[0, slot]
        slot_view(oth, slot)[...] = y_ref[1, slot]


def join_kernel(y0, y1, y2, y3, out_ref):
    z, h = lax.axis_index("col"), lax.axis_index("layer")
    for k, y_ref in enumerate((y0, y1, y2, y3)):
        for core in (0, 1):
            for e in range(4):
                start = pl.multiple_of(e * 64 + (2 * slot_of(z, h, k) + (core ^ h)) * 8, 8)
                for t in range(4):
                    out_ref[pl.ds(start, 8), t * 128 : (t + 1) * 128] = y_ref[core, e, t]


def tables(masks, branch, perm):
    r = lax.axis_index("row")
    z = lax.axis_index("col")
    h = lax.axis_index("layer")
    ids = jnp.arange(64, dtype=jnp.int32)
    inverse = jnp.sum(jnp.where(perm[:, None] == ids[None, :], ids[:, None], 0), axis=0)
    shifts = jnp.arange(32, dtype=jnp.int32)
    bits = jnp.sum(masks.reshape(6, 64, 2, 32) << shifts, axis=-1, dtype=jnp.int32)
    pos = jnp.sum(jnp.where(jnp.asarray(RING) == r, jnp.arange(16), 0))
    place = jnp.stack([r, z * 2 + h, r // 4, r % 4, h, pos, z, z]).astype(jnp.int32)
    return jnp.concatenate(
        [
            perm,
            inverse.astype(jnp.int32),
            branch,
            jnp.zeros((3,), jnp.int32),
            bits.reshape(-1),
            place,
            jnp.zeros((1024 - PLACE - 8,), jnp.int32),
        ]
    )


def z_exchange(kernel, shape, parts):
    first, rest, other_first, other_rest = parts
    other_first, other_rest = core_swap(other_first), core_swap(other_rest)
    (far,) = call(kernel, [shape], [first, other_first])
    far = z_swap(far, 1)
    stay, near, last = call(kernel, [shape] * 3, [rest, other_rest])
    return [stay, far, z_swap(near, 2), z_swap(last, 3)]


def reduce_group(parts):
    return z_exchange(pair_kernel, parts[0].shape[1:], parts)


def spread_group(parts):
    return z_exchange(pack_kernel, (2,) + parts[0].shape[1:], parts)


def in_parts(shape):
    return [(1,) + shape, (3,) + shape] * 2


def shards(density, masks, branch, perm):
    slabs = (4, 4, 8, 128)
    split = spread_group(call(split_kernel, in_parts(slabs), [density]))
    tab = tables(masks, branch, perm)
    tiles = [BAND + s + 1 for s in range(STEPS)] + [BAND + STEPS + 1]
    shapes = [(4, n, 8, 128) for n in tiles] + [(STEPS, 2, 8, 128)]
    *keep, coef = call(keep_kernel, shapes, [], tab=tab)
    (rows,) = call(
        compact_kernel,
        [(4, BAND + 1, 8, 128)],
        split + [keep[0]],
        [pltpu.VMEM((4, 2, 4, 4, 8, 128), F32)],
        tab=tab,
    )
    gathered = gather_rows(rows)
    for step in range(STEPS - 1):
        w = BAND + step
        left, count = geometry(w)
        depth = (4 + 2 * w + (2 if step and outermost(w) else 0)) * 8
        part = in_parts((4, w + 2, 8, 128))
        scratch = [
            pltpu.VMEM((depth, count * 128), BF16),
            pltpu.VMEM((depth, count * 128), BF16),
            pltpu.VMEM((32, 8, count * 128), F32),
        ]
        if step == 0:
            scratch.append(pltpu.VMEM((4, 4, 4, w + 1, 8, 128), F32))
            *sums, cur = call(
                first_step_kernel, part + [(4, w + 1, 8, 128)], gathered, scratch, tab=tab
            )
        else:
            kernel = lambda *refs, w=w, pieces=pieces: step_kernel(w, pieces, *refs)
            sums = call(kernel, part, [cur] + around, scratch)
        parts = reduce_group(sums)
        pieces = halo_pieces(w + 1) if step < STEPS - 2 else []
        cuts = [(0, 4, 0, w + 2)]
        for _, cut in pieces:
            if cut not in cuts:
                cuts.append(cut)
        far = far_tiles(w + 1) if pieces and outermost(w + 1) else 0
        kernel = lambda *refs, step=step, cuts=cuts, far=far: close_kernel(step, cuts, far, *refs)
        shapes = [(hi - lo, last - first, 8, 128) for lo, hi, first, last in cuts]
        scratch = [pltpu.VMEM((2, far, 8, 128), F32)] if far else []
        shapes += [(far, 8, 128)] * 2 if far else []
        sent = call(kernel, shapes, parts + [cur, keep[step + 1], coef], scratch)
        cur = sent[0]
        around = [ring_shift(sent[cuts.index(cut)], d) for d, cut in pieces]
        if far:
            both = jnp.stack([sent[-2], core_swap(sent[-1])])
            around.append(outward(both, outermost(w + 1)))
        cur, *around = lax.optimization_barrier((cur, *around))
    gathered = gather_rows(cur)
    w = BAND + STEPS - 1
    part = in_parts((4, w + 2, 8, 128))
    scratch = [
        pltpu.VMEM(((2 * w + 2) * 8, (w + 2) * 128), BF16),
        pltpu.VMEM(((2 * w + 2) * 8, (w + 2) * 128), BF16),
        pltpu.VMEM((8, 8, (w + 2) * 128), F32),
        pltpu.VMEM((4, 4, 4, w + 1, 8, 128), F32),
    ]
    *sums, cur = call(
        last_step_kernel, part + [(4, w + 1, 8, 128)], gathered, scratch, tab=tab
    )
    parts = reduce_group(sums)
    tiles = call(
        finish_kernel,
        in_parts(slabs),
        parts + [cur, keep[STEPS], coef],
        [pltpu.VMEM((2, 4) + slabs, F32), pltpu.VMEM((2, 4, w + 2, 8, 128), F32)],
        tab=tab,
    )
    (out,) = call(join_kernel, [(256, 512)], spread_group(tiles))
    return out


def solution(mesh):
    return jax.shard_map(
        shards,
        mesh=mesh,
        in_specs=(P("row", GROUP), P(), P(), P()),
        out_specs=P("row", GROUP),
        check_vma=False,
    )
```

```python
import jax
import jax.numpy as jnp
from jax import lax
from jax.experimental import pallas as pl
from jax.experimental.pallas import tpu as pltpu
from jax.sharding import PartitionSpec as P

STEPS = 5
BAND = 6
NB = 64
GROUP = ("col", "layer")
PERM, INV, BRANCH, BITS, PLACE = 0, 64, 128, 136, 136 + 6 * 128
F32, BF16 = jnp.float32, jnp.bfloat16


def ring_xy(pos):
    a, b = pos // 2, pos % 2
    return (a, b) if a < 4 else (7 - a, 3 - b)


RING = [ring_xy(p)[0] * 4 + ring_xy(p)[1] for p in range(16)]


SLOTS = ((0, 2, 1, 3), (0, 2, 3, 1))


def permute(value, axes, pairs):
    flat = value.reshape(-1, 128)
    return lax.ppermute(flat, axes, pairs).reshape(value.shape)


def ring_shift(value, k):
    return permute(value, "row", [(RING[p], RING[(p + k) % 16]) for p in range(16)])


def outward(value, d):
    pairs = []
    for p in range(16):
        pairs.append((RING[p] * 2, RING[(p + d) % 16] * 2))
        pairs.append((RING[p] * 2 + 1, RING[(p - d) % 16] * 2 + 1))
    return permute(value, ("row", "layer"), pairs)


def line_shift(value, k, swapped):
    pairs = []
    for i in range(16):
        for core in (0, 1):
            x, y = i // 4, i % 4
            x, y = (x, (y + k) % 4) if core ^ swapped else ((x + k) % 4, y)
            pairs.append((i * 2 + core, (x * 4 + y) * 2 + core))
    return permute(value, ("row", "layer"), pairs)


def z_swap(value, slot):
    pairs = [(z * 2 + h, (z ^ SLOTS[h][slot]) * 2 + h) for z in range(4) for h in (0, 1)]
    return permute(value, GROUP, pairs)


def slot_of(z, h, slot):
    first, second = SLOTS[0][slot], SLOTS[1][slot]
    return z ^ (first if first == second else jnp.where(h == 0, first, second))


def slot_with(apart, h):
    swapped = jnp.where(apart == 3, 1, jnp.where(apart == 1, 3, apart))
    apart = jnp.where(h == 0, apart, swapped)
    return jnp.where(apart == 2, 1, jnp.where(apart == 1, 2, apart))


def core_swap(value):
    return permute(value, "layer", [(0, 1), (1, 0)])


def low_half():
    return lax.broadcasted_iota(jnp.int32, (8, 128), 1) < 64


def swap_halves(tile):
    return pltpu.roll(tile, 64, 1)


def bit(tab, s, i, j):
    word = tab[BITS + s * 128 + i * 2 + lax.shift_right_logical(j, 5)]
    return lax.shift_right_logical(word, j & 31) & 1


def shifted(tiles, d, count):
    n = len(tiles)
    get = lambda seq, t: seq[t] if 0 <= t < n else None
    if d % 2 == 0:
        return [get(tiles, m - d // 2) for m in range(count)]
    q = (d - 1) // 2
    low = low_half()
    turned = [swap_halves(t) for t in tiles]
    out = []
    for m in range(count):
        a, b = get(turned, m - q - 1), get(turned, m - q)
        if a is None and b is None:
            out.append(None)
        else:
            zero = jnp.zeros((8, 128), F32)
            out.append(jnp.where(low, zero if a is None else a, zero if b is None else b))
    return out


def store_split(hi_ref, lo_ref, row, first, second):
    zero = jnp.zeros((8, 128), F32)
    for m, (a, b) in enumerate(zip(first, second)):
        both = jnp.concatenate([zero if a is None else a, zero if b is None else b], axis=0)
        hi = both.astype(BF16)
        hi_ref[row : row + 16, m * 128 : (m + 1) * 128] = hi
        lo_ref[row : row + 16, m * 128 : (m + 1) * 128] = (both - hi.astype(F32)).astype(BF16)


def tdot(a, b):
    return lax.dot_general(a, b, (((0,), (0,)), ((), ())), preferred_element_type=F32)


def product(hi_ref, lo_ref, start, width):
    xh = hi_ref[:, start : start + width]
    xl = lo_ref[:, start : start + width]
    zh = hi_ref[...]
    return tdot(xh, zh) + tdot(xh, lo_ref[...]) + tdot(xl, zh)


def call(kernel, outs, args, scratch=(), tab=None):
    vmem = pl.BlockSpec(memory_space=pltpu.VMEM)
    table = [] if tab is None else [pl.BlockSpec(memory_space=pltpu.SMEM)]
    return pl.pallas_call(
        kernel,
        out_shape=[jax.ShapeDtypeStruct(o, F32) for o in outs],
        in_specs=table + [vmem] * len(args),
        out_specs=[vmem] * len(outs),
        scratch_shapes=list(scratch),
        compiler_params=pltpu.CompilerParams(vmem_limit_bytes=48 * 1024 * 1024),
    )(*([] if tab is None else [tab]), *args)


def slot_view(pair, slot):
    return pair[0].at[0] if slot == 1 else pair[1].at[(0, None, 1, 2)[slot]]


def split_kernel(d_ref, *refs):
    z, h = lax.axis_index("col"), lax.axis_index("layer")
    for k in range(4):
        for pair, core in ((refs[:2], h), (refs[2:], 1 - h)):
            ref = slot_view(pair, k)
            for e in range(4):
                start = pl.multiple_of(e * 64 + (2 * slot_of(z, core, k) + core) * 8, 8)
                rows = d_ref[pl.ds(start, 8), :]
                for t in range(4):
                    ref[e, t] = rows[:, t * 128 : (t + 1) * 128]


def pack_kernel(own_ref, got_ref, *outs):
    for k, out_ref in enumerate(outs):
        out_ref[0] = own_ref[k]
        out_ref[1] = got_ref[k]


def compact_kernel(tab, *refs):
    ins, (keep_ref, out_ref, x_ref) = refs[:4], refs[4:]
    for k in range(4):
        x_ref[k] = ins[k][...]
    low = low_half()
    row0 = tab[PLACE] * 4
    z, h = tab[PLACE + 6], tab[PLACE + 4]
    for e in range(4):
        i = tab[PERM + row0 + e]
        halves = []
        for t in range(2 * BAND + 2):
            if t > 2 * BAND:
                halves.append(jnp.zeros((8, 128), F32))
                continue
            j = (i + t - BAND) & 63
            sj = tab[INV + j]
            tile = x_ref[slot_with((sj >> 4) ^ z, h), ((sj >> 3) & 1) ^ h, e, (sj & 7) >> 1]
            halves.append(jnp.where((sj & 1) == (t & 1), tile, swap_halves(tile)))
        for t in range(BAND + 1):
            out_ref[e, t] = jnp.where(low, halves[2 * t], halves[2 * t + 1]) * keep_ref[e, t]


def gather_rows(rows):
    near = [line_shift(rows, k, 0) for k in (3, 1, 2)]
    rows, *near = lax.optimization_barrier((rows, *near))
    line = jnp.stack([rows, near[1], near[2], near[0]])
    line = lax.optimization_barrier(line)
    far = [line_shift(line, k, 1) for k in (3, 1, 2)]
    line, *far = lax.optimization_barrier((line, *far))
    return [line, far[1], far[2], far[0]]


def collect(ins, g_ref):
    for n in range(4):
        g_ref[n] = ins[n][...]


def seat(tab, r, e):
    dx = (tab[PLACE + 2] - (r >> 2)) & 3
    dy = (tab[PLACE + 3] - (r & 3)) & 3
    first = tab[PLACE + 4] == 0
    return jnp.where(first, dy, dx), jnp.where(first, dx, dy), e


def write_slabs(p_ref, own, oth, e, base, d, tiles):
    z, h = lax.axis_index("col"), lax.axis_index("layer")
    low = low_half()
    for zz in range(4):
        for pair, core in ((own, h), (oth, 1 - h)):
            ref = slot_view(pair, zz)
            rows = p_ref[base + 2 * slot_of(z, core, zz) + core]
            if d % 2 == 0:
                for m in range(tiles):
                    at = (d // 2 + m) * 128
                    ref[e, m] = rows[:, at : at + 128]
            else:
                q = d // 2
                turned = []
                for m in range(tiles + 1):
                    at = (q + m) * 128
                    if at < rows.shape[1]:
                        turned.append(swap_halves(rows[:, at : at + 128]))
                    else:
                        turned.append(jnp.zeros((8, 128), F32))
                for m in range(tiles):
                    ref[e, m] = jnp.where(low, turned[m], turned[m + 1])


def geometry(w):
    left = w + 1 + (w + 1) % 2
    return left, (left + 4 + w + 1 + 1) // 2


def step_body(strips, w, own, oth, hi_ref, lo_ref, p_ref):
    left, count = geometry(w)
    for a in range(0, len(strips), 2):
        pair = []
        for strip in strips[a : a + 2]:
            b, tiles, first = strip()
            pair.append(shifted(tiles, left - 2 * w + b + 2 * first, count))
        store_split(hi_ref, lo_ref, a * 8, pair[0], pair[1])
    p_ref[...] = product(hi_ref, lo_ref, left * 64, 256).reshape(32, 8, count * 128)
    for e in range(4):
        write_slabs(p_ref, own, oth, e, e * 8, left - (w + 1) + e, w + 2)


def first_step_kernel(tab, *refs):
    ins, own, oth = refs[:4], refs[4:6], refs[6:8]
    cur_ref, hi_ref, lo_ref, p_ref, g_ref = refs[8:]
    collect(ins, g_ref)
    w = BAND
    base = tab[PLACE + 5] * 4 + 64 - w

    def strip_of(b):
        sk = tab[INV + ((base + b) & 63)]
        u, v, e = seat(tab, sk >> 2, sk & 3)
        strip = g_ref[u, v, e]
        if w <= b < w + 4:
            cur_ref[b - w] = strip
        return b, [strip[t] for t in range(w + 1)], 0

    strips = [lambda b=b: strip_of(b) for b in range(4 + 2 * w)]
    step_body(strips, w, own, oth, hi_ref, lo_ref, p_ref)


def step_kernel(w, pieces, *refs):
    far = outermost(w) is not None
    n = 1 + len(pieces) + far
    ins, own, oth = refs[:n], refs[n : n + 2], refs[n + 2 : n + 4]
    hi_ref, lo_ref, p_ref = refs[n + 4 :]

    def strip_of(b):
        off = b - w
        if 0 <= off < 4:
            return b, [ins[0][off, t] for t in range(w + 1)], 0
        d = (-off + 3) // 4 if off < 0 else -(off // 4)
        at = [piece[0] for piece in pieces].index(d)
        _, (lo, hi, first, last) = pieces[at]
        row = off + 4 * d - lo
        return b, [ins[1 + at][row, t] for t in range(last - first)], first

    def far_strip(b, core, slab):
        mine = jnp.where(lax.axis_index("layer") == core, 1.0, 0.0)
        first = 0 if core else w + 1 - far_tiles(w)
        return b, [ins[-1][slab, t] * mine for t in range(far_tiles(w))], first

    last = 4 + 2 * w - 1
    strips = [lambda b=b: strip_of(b) for b in range(far, last + 1 - far)]
    if far:
        for slab in (0, 1):
            strips.append(lambda slab=slab: far_strip(0, 0, slab))
            strips.append(lambda slab=slab: far_strip(last, 1, slab))
    step_body(strips, w, own, oth, hi_ref, lo_ref, p_ref)


def far_tiles(w):
    return w + 1 - 2 * (outermost(w) - 1)


def outermost(w):
    return (w + 3) // 4 if w % 4 == 1 else None


def halo_pieces(w):
    out = []
    for d in range(1, (w + 3) // 4 + 1):
        n = min(4, w - 4 * (d - 1))
        if outermost(w) == d:
            break
        out.append((d, (4 - n, 4, 2 * (d - 1), w + 1)))
        out.append((-d, (0, n, 0, w + 1 - 2 * (d - 1))))
    return out


def last_step_kernel(tab, *refs):
    ins, own, oth = refs[:4], refs[4:6], refs[6:8]
    cur_ref, hi_ref, lo_ref, p_ref, g_ref = refs[8:]
    collect(ins, g_ref)
    w = BAND + STEPS - 1
    row0 = tab[PLACE] * 4
    left, count = w + 2, w + 2
    for e in range(4):
        i = tab[PERM + row0 + e]

        def strips(b):
            k = (i + b - w) & 63
            pos = k >> 2
            a, odd = pos >> 1, pos & 1
            r = jnp.where(a < 4, a * 4 + odd, (7 - a) * 4 + 3 - odd)
            u, v, ee = seat(tab, r, k & 3)
            strip = g_ref[u, v, ee]
            if b == w:
                cur_ref[e] = strip
            return [strip[t] for t in range(w + 1)]

        for a in range(0, 2 * w + 2, 2):
            one = shifted(strips(a), left - 2 * w + a, count)
            two = [None] * count
            if a + 1 <= 2 * w:
                two = shifted(strips(a + 1), left - 2 * w + a + 1, count)
            store_split(hi_ref, lo_ref, a * 8, one, two)
        p_ref[...] = product(hi_ref, lo_ref, left * 64, 64).reshape(8, 8, count * 128)
        write_slabs(p_ref, own, oth, e, 0, 0, count)


def pair_kernel(own_ref, got_ref, *outs):
    for k, out_ref in enumerate(outs):
        out_ref[...] = own_ref[k] + got_ref[k]


def total(parts, e, m):
    return (parts[0][e, m] + parts[1][e, m]) + (parts[2][e, m] + parts[3][e, m])


def polynomial(coef_ref, step, cur, square):
    return coef_ref[step, 0] * cur + coef_ref[step, 1] * square


def keep_kernel(tab, *refs):
    low = low_half()
    refs, coef_ref = refs[:-1], refs[-1]
    for s in range(STEPS):
        twice = tab[BRANCH + s] == 1
        coef_ref[s, 0] = jnp.full((8, 128), jnp.where(twice, 2.0, 0.0), F32)
        coef_ref[s, 1] = jnp.full((8, 128), jnp.where(twice, -1.0, 1.0), F32)
    for s, ref in enumerate(refs):
        w = BAND + s
        margin = w + 1 if s == STEPS else w
        for e in range(4):
            i = tab[PLACE + 5] * 4 + e if 0 < s < STEPS else tab[PERM + tab[PLACE] * 4 + e]
            for m in range(ref.shape[1]):
                sides = []
                for v in (2 * m - margin, 2 * m + 1 - margin):
                    sides.append(bit(tab, s, i, (i + v + 64) & 63) if -w <= v <= w else 0)
                ref[e, m] = jnp.where(low, sides[0], sides[1]).astype(F32)


def close_kernel(step, cuts, far, p0, p1, p2, p3, cur_ref, keep_ref, coef_ref, *refs):
    w = BAND + step
    low = low_half()
    for e in range(4):
        turned = [swap_halves(cur_ref[e, t]) for t in range(w + 1)]
        zero = jnp.zeros((8, 128), F32)
        for m in range(w + 2):
            before = turned[m - 1] if m >= 1 else zero
            after = turned[m] if m <= w else zero
            cur = jnp.where(low, before, after)
            square = total((p0, p1, p2, p3), e, m)
            value = polynomial(coef_ref, step, cur, square) * keep_ref[e, m]
            for ref, (lo, hi, first, last) in zip(refs, cuts):
                if lo <= e < hi and first <= m < last:
                    ref[e - lo, m - first] = value
            if far and e == 3 and m >= w + 2 - far:
                refs[-1][0, m - (w + 2 - far)] = value
            if far and e == 0 and m < far:
                refs[-1][1, m] = value
    if far:
        own_ref, oth_ref, far_ref = refs[-3:]
        own_ref[...] = far_ref[lax.axis_index("layer")]
        oth_ref[...] = far_ref[1 - lax.axis_index("layer")]


def finish_kernel(tab, p0, p1, p2, p3, cur_ref, keep_ref, coef_ref, *refs):
    w = BAND + STEPS - 1
    low = low_half()
    row0 = tab[PLACE] * 4
    z, h = tab[PLACE + 6], tab[PLACE + 4]
    own, oth, y_ref = refs[:2], refs[2:4], refs[4]
    y_ref[...] = jnp.zeros_like(y_ref)
    for e in range(4):
        i = tab[PERM + row0 + e]
        for m in range(w + 2):
            cur = cur_ref[e, m - 1] if 1 <= m <= w + 1 else jnp.zeros((8, 128), F32)
            square = total((p0, p1, p2, p3), e, m)
            value = polynomial(coef_ref, STEPS - 1, cur, square) * keep_ref[e, m]
            turned = swap_halves(value)
            for half in (0, 1):
                v = 2 * m + half
                if v == 0:
                    continue
                j = (i + v + 64 - (w + 2)) & 63
                sj = tab[INV + j]
                odd = sj & 1
                piece = jnp.where(odd == half, value, turned)
                side = jnp.where(low, 0, 1) == odd
                core = (sj >> 3) & 1
                at = core ^ h, slot_with((sj >> 4) ^ z, core), e, (sj & 7) >> 1
                y_ref[at] = jnp.where(side, piece, y_ref[at])
    for slot in range(4):
        slot_view(own, slot)[...] = y_ref[0, slot]
        slot_view(oth, slot)[...] = y_ref[1, slot]


def join_kernel(y0, y1, y2, y3, out_ref):
    z, h = lax.axis_index("col"), lax.axis_index("layer")
    for k, y_ref in enumerate((y0, y1, y2, y3)):
        for core in (0, 1):
            for e in range(4):
                start = pl.multiple_of(e * 64 + (2 * slot_of(z, h, k) + (core ^ h)) * 8, 8)
                for t in range(4):
                    out_ref[pl.ds(start, 8), t * 128 : (t + 1) * 128] = y_ref[core, e, t]


def tables(masks, branch, perm):
    r = lax.axis_index("row")
    z = lax.axis_index("col")
    h = lax.axis_index("layer")
    ids = jnp.arange(64, dtype=jnp.int32)
    inverse = jnp.sum(jnp.where(perm[:, None] == ids[None, :], ids[:, None], 0), axis=0)
    shifts = jnp.arange(32, dtype=jnp.int32)
    bits = jnp.sum(masks.reshape(6, 64, 2, 32) << shifts, axis=-1, dtype=jnp.int32)
    pos = jnp.sum(jnp.where(jnp.asarray(RING) == r, jnp.arange(16), 0))
    place = jnp.stack([r, z * 2 + h, r // 4, r % 4, h, pos, z, z]).astype(jnp.int32)
    return jnp.concatenate(
        [perm, inverse.astype(jnp.int32), branch, jnp.zeros((3,), jnp.int32), bits.reshape(-1), place]
    )


def z_exchange(kernel, shape, parts):
    first, rest, other_first, other_rest = parts
    other_first, other_rest = core_swap(other_first), core_swap(other_rest)
    (far,) = call(kernel, [shape], [first, other_first])
    far = z_swap(far, 1)
    stay, near, last = call(kernel, [shape] * 3, [rest, other_rest])
    return [stay, far, z_swap(near, 2), z_swap(last, 3)]


def reduce_group(parts):
    return z_exchange(pair_kernel, parts[0].shape[1:], parts)


def spread_group(parts):
    return z_exchange(pack_kernel, (2,) + parts[0].shape[1:], parts)


def in_parts(shape):
    return [(1,) + shape, (3,) + shape] * 2


def shards(density, masks, branch, perm):
    slabs = (4, 4, 8, 128)
    split = spread_group(call(split_kernel, in_parts(slabs), [density]))
    tab = tables(masks, branch, perm)
    tiles = [BAND + s + 1 for s in range(STEPS)] + [BAND + STEPS + 1]
    shapes = [(4, n, 8, 128) for n in tiles] + [(STEPS, 2, 8, 128)]
    *keep, coef = call(keep_kernel, shapes, [], tab=tab)
    (rows,) = call(
        compact_kernel,
        [(4, BAND + 1, 8, 128)],
        split + [keep[0]],
        [pltpu.VMEM((4, 2, 4, 4, 8, 128), F32)],
        tab=tab,
    )
    gathered = gather_rows(rows)
    for step in range(STEPS - 1):
        w = BAND + step
        left, count = geometry(w)
        depth = (4 + 2 * w + (2 if step and outermost(w) else 0)) * 8
        part = in_parts((4, w + 2, 8, 128))
        scratch = [
            pltpu.VMEM((depth, count * 128), BF16),
            pltpu.VMEM((depth, count * 128), BF16),
            pltpu.VMEM((32, 8, count * 128), F32),
        ]
        if step == 0:
            scratch.append(pltpu.VMEM((4, 4, 4, w + 1, 8, 128), F32))
            *sums, cur = call(
                first_step_kernel, part + [(4, w + 1, 8, 128)], gathered, scratch, tab=tab
            )
        else:
            kernel = lambda *refs, w=w, pieces=pieces: step_kernel(w, pieces, *refs)
            sums = call(kernel, part, [cur] + around, scratch)
        parts = reduce_group(sums)
        pieces = halo_pieces(w + 1) if step < STEPS - 2 else []
        cuts = [(0, 4, 0, w + 2)]
        for _, cut in pieces:
            if cut not in cuts:
                cuts.append(cut)
        far = far_tiles(w + 1) if pieces and outermost(w + 1) else 0
        kernel = lambda *refs, step=step, cuts=cuts, far=far: close_kernel(step, cuts, far, *refs)
        shapes = [(hi - lo, last - first, 8, 128) for lo, hi, first, last in cuts]
        scratch = [pltpu.VMEM((2, far, 8, 128), F32)] if far else []
        shapes += [(far, 8, 128)] * 2 if far else []
        sent = call(kernel, shapes, parts + [cur, keep[step + 1], coef], scratch)
        cur = sent[0]
        around = [ring_shift(sent[cuts.index(cut)], d) for d, cut in pieces]
        if far:
            both = jnp.stack([sent[-2], core_swap(sent[-1])])
            around.append(outward(both, outermost(w + 1)))
        cur, *around = lax.optimization_barrier((cur, *around))
    gathered = gather_rows(cur)
    w = BAND + STEPS - 1
    part = in_parts((4, w + 2, 8, 128))
    scratch = [
        pltpu.VMEM(((2 * w + 2) * 8, (w + 2) * 128), BF16),
        pltpu.VMEM(((2 * w + 2) * 8, (w + 2) * 128), BF16),
        pltpu.VMEM((8, 8, (w + 2) * 128), F32),
        pltpu.VMEM((4, 4, 4, w + 1, 8, 128), F32),
    ]
    *sums, cur = call(
        last_step_kernel, part + [(4, w + 1, 8, 128)], gathered, scratch, tab=tab
    )
    parts = reduce_group(sums)
    tiles = call(
        finish_kernel,
        in_parts(slabs),
        parts + [cur, keep[STEPS], coef],
        [pltpu.VMEM((2, 4) + slabs, F32)],
        tab=tab,
    )
    (out,) = call(join_kernel, [(256, 512)], spread_group(tiles))
    return out


def solution(mesh):
    return jax.shard_map(
        shards,
        mesh=mesh,
        in_specs=(P("row", GROUP), P(), P(), P()),
        out_specs=P("row", GROUP),
        check_vma=False,
    )
```
